32 devices in a mesh: mem: 4 (over y, x), tile: 8 (over z, core).
Axes of the slice: x: 2, y: 2, z: 4, core: 2. Of those that a mesh axis runs over, the one named last changes fastest.
Arguments:
- ensemble: bfloat16 [32, 32, 128, 128], P('mem', None, 'tile'), may hold values from -0.75 to 0.75
- control: float32 [32, 16, 128, 128], P('mem', None, 'tile'), may hold values from -6 to 6
- level_loc: float32 [16, 16], replicated, may hold values from -0.35 to 1.25
- wind_speed: float32 [128, 128], P('tile'), may hold values from 0.1 to 0.35
- cell_codes: int32 [128, 128], P('tile'), may hold values from 0 to 2
- obs_cell: int32 [4096], P('tile'), may hold values from 0 to 2047
- innovation: float32 [32, 4096], P(None, 'tile'), may hold values from -12 to 12
- obs_sigma: float32 [32, 4096], P(None, 'tile'), may hold values from 0.5 to 2
Outputs:
- obs_gradient: float32 [32, 16, 128, 128], P('mem', None, 'tile')
The draws below stay inside these ranges and needn't reach their ends.
Inputs may be any that keep to these rules, and one draw needn't show every extreme that they name: obs_cell[j] counts cells within tile j // 512, as (x - tile's first x) * 128 + y; several observations may share a cell. `cell_codes`: 0 is an open cell, 1 a wall cell that no flux enters or leaves, 2 an open cell that keeps 0.7 of its value each step.
All inputs are finite; a program needn't handle non-finite values.
Results may differ from the reference program's by a relative error of at most 0.0003.
Values may be sent and summed in bfloat16 or wider, within the bound.
A program may use at most 64 MiB of HBM per device.

```python
import math
import jax
import jax.numpy as jnp
from jax import lax

K_DEV = 8
L = 16
V = 2
CX = 16
NY = 128
STEPS = 2
VL = 32
MEMBERS = 32
NX = 128
NOBS = 512
TOTAL_OBS = 4096
N_MEM = 4
N_TILE = 8


def draw_ensemble(key, part):
    shape = (MEMBERS, V * L, NX, NY)
    values = 0.125 * jax.random.truncated_normal(key, -6.0, 6.0, shape, jnp.float32)
    return values.astype(jnp.bfloat16)


def draw_control(key, part):
    shape = (MEMBERS, L, NX, NY)
    values = jax.random.truncated_normal(key, -6.0, 6.0, shape, jnp.float32)
    return values


def draw_level_loc(key, part):
    first_key, second_key = jax.random.split(key)
    rows = jnp.arange(L, dtype=jnp.int32)[:, None]
    cols = jnp.arange(L, dtype=jnp.int32)[None, :]
    dist = jnp.abs(rows - cols).astype(jnp.float32)
    off = jax.random.uniform(first_key, (L, L), jnp.float32, -1.0, 1.0)
    diag = jax.random.uniform(second_key, (L, L), jnp.float32, 0.8, 1.2)
    off_part = 0.35 * off * jnp.exp(-dist / 3.0)
    return jnp.where(dist == 0.0, diag, off_part).astype(jnp.float32)


def plant(values, own_key, least, largest):
    longest = values.shape.index(max(values.shape))
    spots = []
    for shift in (0, 1):
        where = [jax.random.randint(jax.random.fold_in(own_key, axis), (), 0, length) for axis, length in enumerate(values.shape)]
        where[longest] = (where[longest] + shift) % values.shape[longest]
        spots.append(tuple(where))
    return values.at[spots[0]].set(least).at[spots[1]].set(largest)


def levels(rng, dims, cuts, smallest, high):
    def one(position, blocks):
        draws = jax.random.uniform(jax.random.fold_in(jax.random.fold_in(rng, 6), position), (blocks,), jnp.float32, smallest / len(cuts), high / len(cuts))
        return jnp.repeat(jnp.exp(draws), dims[position] // blocks).reshape((-1,) + (1,) * (len(dims) - position - 1))

    level = one(*cuts[0])
    for cut in cuts[1:]:
        level = level * one(*cut)
    return level


def noise(key, dims, spread, reach, cuts=(), kind=jnp.bfloat16):
    result = jax.random.normal(key, dims, jnp.float32) * spread
    if len(cuts) > 0:
        result = levels(key, dims, cuts, -0.22, 0.18) * result
    return jnp.clip(result, min=-reach, max=reach).astype(kind)


def setup_inputs(seed: int = 0) -> dict:
    key_of = jax.random.split(jax.random.key(seed), 9)
    ensemble = draw_ensemble(jax.random.fold_in(key_of[8], 71), 0)
    control = draw_control(jax.random.fold_in(key_of[8], 71), 0)
    level_loc = draw_level_loc(jax.random.fold_in(key_of[8], 71), 0)
    wind_speed = jnp.clip(0.1 + 0.25 * jax.random.uniform(key_of[3], (NX, NY), jnp.float32) ** levels(key_of[3], (NX, NY), ((0, 8),), -0.2, 0.2), 0.1, 0.35)
    cell_codes = plant(jax.random.randint(key_of[4], (NX, NY), 0, 3), jax.random.fold_in(key_of[4], 1), 0, 2).astype(jnp.int32)
    obs_cell = plant(jax.random.randint(key_of[5], (TOTAL_OBS,), 0, CX * NY), jax.random.fold_in(key_of[5], 1), 0, (CX * NY) - 1).astype(jnp.int32)
    innovation = noise(key_of[6], (VL, TOTAL_OBS), 2.0, 12.0, ((1, 8),), jnp.float32)
    obs_sigma = jnp.clip(jnp.exp(math.log(2.0) - 1.3862944 * jax.random.uniform(key_of[7], (VL, TOTAL_OBS), jnp.float32) ** levels(key_of[7], (VL, TOTAL_OBS), ((1, 8),), -0.2, 0.2)), 0.5, 2.0)
    return {"ensemble": ensemble, "control": control, "level_loc": level_loc, "wind_speed": wind_speed, "cell_codes": cell_codes, "obs_cell": obs_cell, "innovation": innovation, "obs_sigma": obs_sigma}


diffusion_rate = 0.12
absorbing = 0.7
step_length = 0.5
huber_delta = 1.0


def smooth_field(values):
    padded = jnp.pad(values, [(0, 0)] * (values.ndim - 2) + [(1, 1), (1, 1)])
    along_x = 0.5 * padded[..., 1:-1, :] + 0.25 * (padded[..., :-2, :] + padded[..., 2:, :])
    return 0.5 * along_x[..., 1:-1] + 0.25 * (along_x[..., :-2] + along_x[..., 2:])


def make_coeffs(open_cells, wind_speed):
    rate = diffusion_rate
    open_east = open_cells * jnp.pad(open_cells[1:], ((0, 1), (0, 0)))
    open_west = jnp.pad(open_east[:-1], ((1, 0), (0, 0)))
    open_north = open_cells * jnp.pad(open_cells[:, 1:], ((0, 0), (0, 1)))
    open_south = jnp.pad(open_north[:, :-1], ((0, 0), (1, 0)))
    wind_west = jnp.pad(wind_speed[:-1], ((1, 0), (0, 0)))
    center = 1.0 - rate * (open_east + open_west + open_north + open_south) - wind_speed * open_east
    forward = (center, (rate + wind_west) * open_west, rate * open_east, rate * open_south, rate * open_north)
    adjoint = (center, rate * open_west, (rate + wind_speed) * open_east, rate * open_south, rate * open_north)
    return forward, adjoint


def apply_stencil(state_field, coeffs):
    center, west_coef, east_coef, south_coef, north_coef = coeffs
    padded = jnp.pad(state_field, ((0, 0), (1, 1), (1, 1)))
    return (center * state_field + west_coef * padded[:, :-2, 1:-1] + east_coef * padded[:, 2:, 1:-1]
            + south_coef * padded[:, 1:-1, :-2] + north_coef * padded[:, 1:-1, 2:])


def reference(ensemble, control, level_loc, wind_speed, cell_codes, obs_cell, innovation, obs_sigma):
    highest = lax.Precision.HIGHEST
    open_cells = (cell_codes != 1).astype(jnp.float32)
    absorb = jnp.where(cell_codes == 2, absorbing, 1.0).astype(jnp.float32)
    forward, adjoint = make_coeffs(open_cells, wind_speed)
    tile_of = jnp.arange(NOBS * N_TILE, dtype=jnp.int32) // NOBS
    flat_index = (tile_of * (CX * NY) + obs_cell).astype(jnp.int32)
    ens_blocks = ensemble.reshape(N_MEM, K_DEV, V, L, NX, NY)

    def localize(block_weights):
        level_mixed = jnp.einsum("ml,klxy->kmxy", level_loc, block_weights, precision=highest)
        return smooth_field(level_mixed)

    def evaluate(weight_blocks):
        def accumulate(total, pair):
            ens_block, block_weights = pair
            mixed = localize(block_weights)
            return total + jnp.sum(ens_block.astype(jnp.float32) * mixed[:, None], 0), None

        increment, _ = lax.scan(accumulate, jnp.zeros((V, L, NX, NY), jnp.float32), (ens_blocks, weight_blocks))
        state_field = increment.reshape(VL, NX, NY)
        for sweep_index in range(STEPS):
            state_field = absorb * apply_stencil(state_field, forward)
        sampled = state_field.reshape(VL, NX * NY)[:, flat_index]
        scaled = (sampled - innovation) / obs_sigma
        obs_weight = jnp.clip(scaled, -huber_delta, huber_delta) / obs_sigma
        gridded = jnp.zeros((VL, NX * NY), jnp.float32).at[:, flat_index].add(obs_weight)
        adjoint_field = gridded.reshape(VL, NX, NY)
        for sweep_index in range(STEPS):
            adjoint_field = apply_stencil(absorb * adjoint_field, adjoint)
        adjoint_field = adjoint_field.reshape(V, L, NX, NY)

        def project(ens_block):
            member_term = jnp.sum(ens_block.astype(jnp.float32) * adjoint_field[None], 1)
            level_mix = jnp.einsum("ml,kmxy->klxy", level_loc, member_term, precision=highest)
            return smooth_field(level_mix)

        return lax.map(project, ens_blocks)

    control_blocks = control.reshape(N_MEM, K_DEV, L, NX, NY)
    first = evaluate(control_blocks)
    next_control = control_blocks - step_length * (control_blocks + first)
    second = evaluate(next_control)
    return second.reshape(MEMBERS, L, NX, NY)
```

```python
import contextlib
import functools

import jax
import jax.numpy as jnp
from jax import lax
from jax.experimental import pallas as pl
from jax.experimental.pallas import tpu as pltpu
from jax.sharding import PartitionSpec as P

V = 2
STEPS = 2
HALO = 8
PACK = 16
SPAN = 32760.0

diffusion_rate = 0.12
absorbing = 0.7
step_length = 0.5
huber_delta = 1.0

MESH = pl.DeviceIdType.MESH
F32 = jnp.float32
BF16 = jnp.bfloat16
I16 = jnp.int16
I32 = jnp.int32
HIGHEST = lax.Precision.HIGHEST
NT = (((1,), (1,)), ((), ()))
mark = contextlib.nullcontext


def log2(n):
    assert n & (n - 1) == 0
    return n.bit_length() - 1


def iota(shape, dim):
    return lax.broadcasted_iota(I32, shape, dim)


def split(x):
    hi = x.astype(BF16)
    return hi, (x - hi.astype(F32)).astype(BF16)


def mm(a, b):
    return jnp.dot(a, b, preferred_element_type=F32)


def nt(a, b):
    return lax.dot_general(a, b, NT, precision=HIGHEST, preferred_element_type=F32)


def dot3(a, b):
    ah, al = a
    bh, bl = split(b)
    return mm(ah, bh) + (mm(ah, bl) + mm(al, bh))


def smoother(ny):
    yi = iota((1, ny), 1)
    from_south = jnp.where(yi > 0, 0.25, 0.0).astype(F32)
    from_north = jnp.where(yi < ny - 1, 0.25, 0.0).astype(F32)

    def smooth_y(v):
        return 0.5 * v + (from_south * pltpu.roll(v, 1, 1) + from_north * pltpu.roll(v, ny - 1, 1))

    return smooth_y


def exponent(parts, ny):
    most = None
    for p in parts:
        v = jnp.max(jnp.abs(p.reshape(-1, ny)), axis=0, keepdims=True)
        most = v if most is None else jnp.maximum(most, v)
    return jnp.floor(jnp.log2(jnp.maximum(most, 1e-30))) + 1.0


def encode(x, e):
    return jnp.round(x * (jnp.exp2(-e) * SPAN)).astype(I32).astype(I16)


def whole_number(q):
    return q.astype(I32).astype(F32)


def unit(code):
    return jnp.exp2(whole_number(code)[0:1]) * (1.0 / SPAN)


def kernel(
    n_mem, n_tile, members, levels, width, ny, nobs,
    ens_hbm, ctl_hbm, loc_hbm, wind_hbm, codes_hbm, cell_hbm, innov_hbm, sigma_hbm,
    term_out, edges_out, mats_out, small_out,
    ens, ctl, loc, wind, codes, cell, innov, sigma, in_sem, hot,
    ensf, work, mats, small, blur2,
    ctl_stage, ctl_halo, codes_halo, wind_halo, cell_halo, innov_halo, sigma_halo,
    ens_stage, ens_halo,
    part, rs_src, rs_main, rs_halo, inc0, ext, fringe, fringes, marks_all, ag,
    r0_send, r0_recv, rs_send, rs_recv, ag_send, ag_recv,
):
    m = lax.axis_index("mem")
    t = lax.axis_index("tile")
    has = (t > 0, t < n_tile - 1)
    rows = V * levels
    share = rows // n_mem
    block = levels * width
    kl = members * levels
    xs = log2(width)
    half = share * HALO
    n = HALO + width + HALO

    def tell(dev):
        pl.semaphore_signal(pltpu.get_barrier_semaphore(), inc=1, device_id=dev, device_id_type=MESH)

    for d in range(1, n_mem):
        tell((lax.rem(m + d, n_mem), t))

    @pl.when(has[0])
    def _():
        for d in range(n_mem):
            tell((lax.rem(m + d, n_mem), t - 1))

    @pl.when(has[1])
    def _():
        for d in range(n_mem):
            tell((lax.rem(m + d, n_mem), t + 1))

    loads = [
        pltpu.make_async_copy(src, dst, in_sem.at[i])
        for i, (src, dst) in enumerate((
            (loc_hbm, loc), (ctl_hbm, ctl), (ens_hbm, ens), (wind_hbm, wind), (codes_hbm, codes),
            (cell_hbm, cell), (innov_hbm.at[m], innov), (sigma_hbm.at[m], sigma),
        ))
    ]
    for load in loads:
        load.start()

    def to_side(side, d, src, dst, ssem, rsem):
        dev = (lax.rem(m + d, n_mem), t + 1 if side == 0 else t - 1)
        return pltpu.make_async_remote_copy(
            src_ref=src, dst_ref=dst, send_sem=ssem, recv_sem=rsem, device_id=dev, device_id_type=MESH
        )

    def to_mem(d, src, dst, ssem, rsem):
        return pltpu.make_async_remote_copy(
            src_ref=src, dst_ref=dst, send_sem=ssem, recv_sem=rsem,
            device_id=(lax.rem(m + d, n_mem), t), device_id_type=MESH,
        )

    near = (pl.ds(width - HALO, HALO), pl.ds(0, HALO))
    first_msgs = []
    for side in (0, 1):
        pairs = [
            (ctl_stage.at[side], ctl_halo.at[side]),
            (codes_hbm.at[near[side]], codes_halo.at[side]),
            (wind_hbm.at[near[side]], wind_halo.at[side]),
            (cell_hbm, cell_halo.at[side]),
            (innov_hbm.at[m], innov_halo.at[side]),
            (sigma_hbm.at[m], sigma_halo.at[side]),
            (ens_stage.at[side], ens_halo.at[side]),
        ]
        first_msgs.append(
            [to_side(side, 0, s, d, r0_send.at[side, i], r0_recv.at[side, i]) for i, (s, d) in enumerate(pairs)]
        )

    def start_side(side, which):
        @pl.when(has[1 - side])
        def _():
            for i in which:
                first_msgs[side][i].start()

    def recv_side(side, which):
        @pl.when(has[side])
        def _():
            for i in which:
                first_msgs[side][i].wait_recv()

    for side in (0, 1):
        @pl.when(jnp.logical_not(has[side]))
        def _():
            ctl_halo[side] = jnp.zeros_like(ctl_halo[side])
            codes_halo[side] = jnp.ones_like(codes_halo[side])
            wind_halo[side] = jnp.zeros_like(wind_halo[side])
            cell_halo[side] = jnp.full_like(cell_halo[side], -1)
            innov_halo[side] = jnp.zeros_like(innov_halo[side])
            sigma_halo[side] = jnp.ones_like(sigma_halo[side])
            ens_halo[side] = jnp.zeros_like(ens_halo[side])
            for e in (0, 1):
                rs_halo[e, side] = jnp.zeros_like(rs_halo[e, side])

    smooth_y = smoother(ny)
    gap = lambda shape, mask: jnp.abs((iota(shape, 0) & mask) - (iota(shape, 1) & mask))
    lev = lambda shape, dim, shift: iota(shape, dim) >> shift

    with mark("w_loc"):
        loads[0].wait()
    with mark("mats0"):
        lo = loc[...]
        spread = (lev((levels, block), 1, xs) == iota((levels, block), 0)).astype(BF16)
        repeat = ((iota((levels, kl), 1) & (levels - 1)) == iota((levels, kl), 0)).astype(BF16)
        near_x = gap((block, block), width - 1)
        near_x = jnp.where(near_x == 0, 0.5, jnp.where(near_x == 1, 0.25, 0.0)).astype(F32)
        same_k = (lev((kl, kl), 0, log2(levels)) == lev((kl, kl), 1, log2(levels))).astype(F32)
        for j, piece in enumerate(split(lo)):
            p = piece.astype(F32)
            tall = jnp.broadcast_to(p[:, None, :], (levels, width, levels)).reshape(block, levels)
            mats[0, j] = (mm(tall.astype(BF16), spread) * near_x).astype(BF16)
            tall = jnp.concatenate([p] * members, axis=0)
            small[0, j] = (mm(tall.astype(BF16), repeat) * same_k).astype(BF16)

    with mark("w_ctl"):
        loads[1].wait()
    ctl_stage[0] = ctl[pl.ds(width - 1, kl, stride=width), :]
    ctl_stage[1] = ctl[pl.ds(0, kl, stride=width), :]

    with mark("w_barrier"):
        peers = n_mem - 1 + n_mem * (jnp.where(t > 0, 1, 0) + jnp.where(t < n_tile - 1, 1, 0))
        pl.semaphore_wait(pltpu.get_barrier_semaphore(), peers)

    for side in (0, 1):
        start_side(side, (0,))
    for side in (0, 1):
        start_side(side, (1, 2, 3, 4, 5))

    with mark("mix_a0"):
        big = (mats[0, 0], mats[0, 1])
        for k in range(0, members, 2):
            both = jnp.concatenate(
                [ctl[k * block:(k + 1) * block, :], ctl[(k + 1) * block:(k + 2) * block, :]], axis=1
            )
            done = dot3(big, both)
            work[k * block:(k + 1) * block, :] = smooth_y(done[:, :ny])
            work[(k + 1) * block:(k + 2) * block, :] = smooth_y(done[:, ny:])

    with mark("ens_stage"):
        loads[2].wait()
        for k in range(members):
            ensf[pl.ds(k * rows * width, rows * width), :] = ens[k].astype(F32).reshape(rows * width, ny)
        for i in (0, 1):
            ens_stage[0, i] = ensf[pl.ds(width - 1 - i, members * rows, stride=width), :].astype(BF16)
            ens_stage[1, i] = ensf[pl.ds(i, members * rows, stride=width), :].astype(BF16)
        for side in (0, 1):
            start_side(side, (6,))

    with mark("w_ctlhalo"):
        for side in (0, 1):
            recv_side(side, (0,))
    with mark("side0"):
        side = dot3((small[0, 0], small[0, 1]), jnp.concatenate([ctl_halo[0], ctl_halo[1]], axis=1))
        for j, x in ((0, 0), (1, width - 1)):
            at = pl.ds(x, kl, stride=width)
            work[at, :] = work[at, :] + smooth_y(0.25 * side[:, j * ny:(j + 1) * ny])

    def coefficients():
        code = jnp.concatenate([codes_halo[0], codes[...], codes_halo[1]], axis=0)
        speed = jnp.concatenate([wind_halo[0], wind[...], wind_halo[1]], axis=0)
        opened = (code != 1).astype(F32)
        absorb = jnp.where(code == 2, absorbing, 1.0).astype(F32)
        yy = iota(code.shape, 1)
        oe = opened * pltpu.roll(opened, n - 1, 0)
        ow = opened * pltpu.roll(opened, 1, 0)
        on = jnp.where(yy < ny - 1, opened * pltpu.roll(opened, ny - 1, 1), 0.0)
        os = jnp.where(yy > 0, opened * pltpu.roll(opened, 1, 1), 0.0)
        k = diffusion_rate
        center = 1.0 - k * (oe + ow + on + os) - speed * oe
        fwd = (center, (k + pltpu.roll(speed, 1, 0)) * ow, k * oe, k * os, k * on)
        adj = (center, k * ow, (k + speed) * oe, k * os, k * on)
        return absorb, fwd, adj

    def stencil(q, coef):
        center, west, east, south, north = coef
        return (
            center * q
            + west * pltpu.roll(q, 1, 0)
            + east * pltpu.roll(q, n - 1, 0)
            + south * pltpu.roll(q, 1, 1)
            + north * pltpu.roll(q, ny - 1, 1)
        )

    def observe(field):
        state = jnp.stack(field, axis=0)
        tiles = (
            (cell_halo[0], innov_halo[0], sigma_halo[0], 0, HALO, width - HALO),
            (cell[...], innov[...], sigma[...], HALO, width, 0),
            (cell_halo[1], innov_halo[1], sigma_halo[1], HALO + width, HALO, 0),
        )
        pieces = []
        for i, (where, seen, dev, at, count, offset) in enumerate(tiles):
            hot_y = hot[i]
            hot_x = (iota((count, nobs), 0) == ((where >> log2(ny)) - offset)).astype(F32)
            part_state = state[:, at:at + count, :].reshape(share * count, ny)
            hi, low = split(part_state)
            got = (mm(hi, hot_y) + mm(low, hot_y)).reshape(share, count, nobs)
            sampled = jnp.sum(got * hot_x[None], axis=1)
            scaled = (sampled - seen) / dev
            weight = jnp.clip(scaled, -huber_delta, huber_delta) / dev
            hi, low = split(weight)
            total = None
            for w in (hi, low):
                spread = (w.astype(F32)[:, None, :] * hot_x[None]).reshape(share * count, nobs).astype(BF16)
                put = lax.dot_general(spread, hot_y, NT, preferred_element_type=F32)
                total = put if total is None else total + put
            pieces.append(total.reshape(share, count, ny))
        return jnp.concatenate(pieces, axis=1)

    def members_sum(e):
        copies = []
        for d in list(range(1, n_mem)) + [0]:
            who = lax.rem(m + d, n_mem)
            r0 = who * share
            l0 = lax.rem(r0, levels)
            total = jnp.zeros((share, width, ny), F32)
            for k in range(members):
                a = work[pl.ds(pl.multiple_of(k * block + l0 * width, width), share * width), :]
                total += ens[k, pl.ds(r0, share)].astype(F32) * a.reshape(share, width, ny)
            if d == 0:
                part[...] = total
            ex = exponent([total], ny)
            q = [encode(total[:, s * HALO:(s + 1) * HALO, :].reshape(half, ny), ex) for s in (0, 1)]
            rs_src[e, d, pl.ds(0, half)] = q[0]
            rs_src[e, d, pl.ds(half, PACK)] = jnp.broadcast_to(ex, (PACK, ny)).astype(I32).astype(I16)
            rs_src[e, d, pl.ds(half + PACK, half)] = q[1]
            if d:
                copy = to_mem(d, rs_src.at[e, d], rs_main.at[e, d], rs_send.at[e, 2, d], rs_recv.at[e, 2, d])
                copy.start()
                copies.append(copy)
        side_copies = [
            [
                to_side(
                    side, d, rs_src.at[e, d, pl.ds((half, 0)[side], half + PACK)], rs_halo.at[e, side, d],
                    rs_send.at[e, side, d], rs_recv.at[e, side, d],
                )
                for d in range(n_mem)
            ]
            for side in (0, 1)
        ]
        for side in (0, 1):
            @pl.when(has[1 - side])
            def _():
                for copy in side_copies[side]:
                    copy.start()
        return copies, side_copies

    def gather_sum(e, copies, side_copies):
        for copy in copies:
            copy.wait_recv()
        for side in (0, 1):
            @pl.when(has[side])
            def _():
                for copy in side_copies[side]:
                    copy.wait_recv()
        own = part[...]
        pieces = [own[:, :HALO], own[:, HALO:]]
        for d in range(1, n_mem):
            u = unit(rs_main[e, d, pl.ds(half, PACK)])
            for s in (0, 1):
                q = rs_main[e, d, pl.ds(s * (half + PACK), half)]
                pieces[s] = pieces[s] + (whole_number(q) * u).reshape(share, HALO, ny)
        outer = []
        for side in (0, 1):
            total = None
            for d in range(n_mem):
                u = unit(rs_halo[e, side, d, pl.ds((0, half)[side], PACK)])
                v = whole_number(rs_halo[e, side, d, pl.ds((PACK, 0)[side], half)]) * u
                total = v if total is None else total + v
            outer.append(total.reshape(share, HALO, ny))
        return jnp.concatenate([outer[0]] + pieces + [outer[1]], axis=1)

    main = rows * width // n_mem
    margin = fringe.shape[0]

    def observation_term(e, whole, stencils):
        absorb, fwd, adj = stencils
        fields = [whole[r] for r in range(share)]
        for _ in range(STEPS):
            fields = [absorb * stencil(q, fwd) for q in fields]
        with mark("observe"):
            gridded = observe(fields)
        fields = [gridded[r] for r in range(share)]
        for _ in range(STEPS):
            fields = [stencil(absorb * p, adj) for p in fields]
        for r in range(share):
            ext[pl.ds(r * n, n), :] = fields[r]
        lines = (HALO - 1, HALO + width) + ((HALO - 2, HALO + width + 1) if e == 0 else ())
        if margin > len(lines) * share:
            fringe[...] = jnp.zeros_like(fringe)
        for i, row in enumerate(lines):
            fringe[pl.ds(i * share, share), :] = ext[pl.ds(row, share, stride=n), :]
        inner = jnp.stack([f[HALO:HALO + width] for f in fields], axis=0).reshape(main, ny)
        outside = fringe[...]
        ex = exponent([inner, outside], ny)
        ag[e, m, pl.ds(0, main)] = encode(inner, ex)
        ag[e, m, pl.ds(main, margin)] = encode(outside, ex)
        ag[e, m, pl.ds(main + margin, PACK)] = jnp.broadcast_to(ex, (PACK, ny)).astype(I32).astype(I16)
        gathers = [
            to_mem(d, ag.at[e, m], ag.at[e, m], ag_send.at[e, d], ag_recv.at[e, d]) for d in range(1, n_mem)
        ]
        for copy in gathers:
            copy.start()
        return gathers, len(lines)

    def adjoint_rows(e, count):
        units = [unit(ag[e, i, pl.ds(main + margin, PACK)]) for i in range(n_mem)]
        inner = jnp.concatenate([whole_number(ag[e, i, pl.ds(0, main)]) * units[i] for i in range(n_mem)], axis=0)
        for i in range(n_mem):
            fringes[i] = whole_number(ag[e, i, pl.ds(main, margin)]) * units[i]
            for j in range(count):
                marks_all[j, pl.ds(i * share, share), :] = fringes[i, pl.ds(j * share, share), :]
        terms = []
        for j in range(count):
            p = ens_halo[j % 2, j // 2].astype(F32).reshape(members, rows, ny) * marks_all[j][None]
            terms.append((p[:, :levels] + p[:, levels:]).reshape(kl, ny))
        return inner, terms

    def member_term(k, inner):
        at = k * rows * width
        return ensf[pl.ds(at, block), :] * inner[:block] + ensf[pl.ds(at + block, block), :] * inner[block:]

    with mark("part0"):
        rs0 = members_sum(0)
    with mark("hidden"):
        for side in (0, 1):
            recv_side(side, (1, 2, 3, 4, 5))
        for load in loads[3:]:
            load.wait()
        for i, where in enumerate((cell_halo[0], cell[...], cell_halo[1])):
            hot[i] = (iota((ny, nobs), 0) == (where & (ny - 1))).astype(BF16)
        pick = (lev((block, levels), 0, xs) == iota((block, levels), 1)).astype(F32)
        pick2 = ((iota((kl, levels), 0) & (levels - 1)) == iota((kl, levels), 1)).astype(F32)
        both = nt(lo, lo)
        far_x = gap((block, block), width - 1)
        far_x = jnp.where(far_x == 0, 0.375, jnp.where(far_x == 1, 0.25, jnp.where(far_x == 2, 0.0625, 0.0)))
        xr, xc = iota((block, block), 0) & (width - 1), iota((block, block), 1) & (width - 1)
        for side, x in ((0, 0), (1, width - 1)):
            lost = jnp.where(has[side], 0.0, 0.0625).astype(F32)
            far_x = far_x - jnp.where((xr == x) & (xc == x), lost, 0.0)
        full = nt(jnp.dot(pick, both, precision=HIGHEST, preferred_element_type=F32), pick) * far_x
        for j, piece in enumerate(split(full)):
            mats[1, j] = piece
        full = nt(jnp.dot(pick2, both, precision=HIGHEST, preferred_element_type=F32), pick2) * same_k
        for j, piece in enumerate(split(full)):
            small[1, j] = piece
        for j, piece in enumerate(split(nt(nt(pick, lo), pick) * near_x)):
            mats_out[j] = piece
        for j, piece in enumerate(split(nt(nt(pick2, lo), pick2) * same_k)):
            small_out[j] = piece
        yr, yc = iota((2 * ny, 2 * ny), 0), iota((2 * ny, 2 * ny), 1)
        far_y = jnp.abs(yr - yc)
        corner = (yr & (ny - 1) == 0) | (yr & (ny - 1) == ny - 1)
        far_y = jnp.where(
            far_y == 0, jnp.where(corner, 0.3125, 0.375),
            jnp.where(far_y == 1, 0.25, jnp.where(far_y == 2, 0.0625, 0.0)),
        )
        blur2[...] = jnp.where((yr >> log2(ny)) == (yc >> log2(ny)), far_y, 0.0).astype(BF16)
        stencils = coefficients()
    with mark("w_rs0"):
        whole = gather_sum(0, *rs0)
    inc0[...] = whole
    with mark("obs0"):
        gathers0, count = observation_term(0, whole, stencils)
    with mark("w_ag0"):
        for copy in gathers0:
            copy.wait_recv()
        for side in (0, 1):
            recv_side(side, (6,))
    with mark("mix1"):
        inner, terms = adjoint_rows(0, count)
        big = (mats[1, 0], mats[1, 1])

        def blur(v):
            hi, low = split(v)
            return mm(hi, blur2[...]) + mm(low, blur2[...])

        for k in range(0, members, 2):
            done = blur(dot3(big, jnp.concatenate([member_term(k, inner), member_term(k + 1, inner)], axis=1)))
            work[k * block:(k + 1) * block, :] = done[:, :ny]
            work[(k + 1) * block:(k + 2) * block, :] = done[:, ny:]
        tiny = (small[1, 0], small[1, 1])
        close = dot3(tiny, jnp.concatenate(terms[:2], axis=1))
        distant = blur(0.25 * close + 0.0625 * dot3(tiny, jnp.concatenate(terms[2:], axis=1)))
        close = blur(0.0625 * close)
        for side, first, second in ((0, 0, 1), (1, width - 1, width - 2)):
            for x, v in ((first, distant), (second, close)):
                at = pl.ds(x, kl, stride=width)
                work[at, :] = work[at, :] + v[:, side * ny:(side + 1) * ny]
    with mark("part1"):
        rs1 = members_sum(1)
    with mark("w_rs1"):
        whole = gather_sum(1, *rs1)
    with mark("obs1"):
        gathers1, count = observation_term(1, step_length * (inc0[...] - whole), stencils)
    with mark("w_ag1"):
        for copy in gathers1:
            copy.wait_recv()
    with mark("term1"):
        inner, terms = adjoint_rows(1, count)
        for k in range(members):
            term_out[pl.ds(k * block, block), :] = member_term(k, inner)
        for side in (0, 1):
            edges_out[:, side * ny:(side + 1) * ny] = terms[side]
    with mark("drain"):
        for copies, side_copies in (rs0, rs1):
            for copy in copies:
                copy.wait_send()
            for side in (0, 1):
                @pl.when(has[1 - side])
                def _():
                    for copy in side_copies[side]:
                        copy.wait_send()
        for copy in gathers0 + gathers1:
            copy.wait_send()
        for s in (0, 1):
            @pl.when(has[1 - s])
            def _():
                for copy in first_msgs[s]:
                    copy.wait_send()


def finish(members, levels, width, ny, term, edges, mats, small, out, work, sem):
    block = levels * width
    smooth_y = smoother(ny)
    side = 0.25 * dot3((small[0], small[1]), edges[...])
    sides = [smooth_y(side[:, j * ny:(j + 1) * ny]) for j in (0, 1)]
    big = (mats[0], mats[1])
    copies = []
    for k in range(0, members, 2):
        both = jnp.concatenate([term[k * block:(k + 1) * block, :], term[(k + 1) * block:(k + 2) * block, :]], axis=1)
        done = dot3(big, both)
        for i in (0, 1):
            base = (k + i) * block
            work[pl.ds(base, block), :] = smooth_y(done[:, i * ny:(i + 1) * ny])
            for j, x in ((0, 0), (1, width - 1)):
                at = pl.ds(base + x, levels, stride=width)
                work[at, :] = work[at, :] + sides[j][(k + i) * levels:(k + i + 1) * levels]
        at = pl.ds(k * block, 2 * block)
        copies.append(pltpu.make_async_copy(work.at[at], out.at[at], sem.at[k // 2]))
        copies[-1].start()
    for copy in copies:
        copy.wait()


def body(n_mem, n_tile, ensemble, control, level_loc, wind_speed, cell_codes, obs_cell, innovation, obs_sigma):
    members, rows, width, ny = ensemble.shape
    assert width == 2 * HALO and members % 2 == 0
    levels = control.shape[1]
    nobs = obs_cell.shape[0]
    share = rows // n_mem
    kl = members * levels
    block = levels * width
    half = share * HALO
    n = width + 2 * HALO
    main = share * width
    margin = -(-4 * share // PACK) * PACK
    message = main + margin + PACK
    vmem = pltpu.VMEM
    dma = pltpu.SemaphoreType.DMA
    scratch = [
        vmem((members, rows, width, ny), BF16),
        vmem((members * block, ny), F32),
        vmem((levels, levels), F32),
        vmem((width, ny), F32),
        vmem((width, ny), I32),
        vmem((1, nobs), I32),
        vmem((share, nobs), F32),
        vmem((share, nobs), F32),
        dma((8,)),
        vmem((3, ny, nobs), BF16),
        vmem((members * rows * width, ny), F32),
        vmem((members * block, ny), F32),
        vmem((2, 2, block, block), BF16),
        vmem((2, 2, kl, kl), BF16),
        vmem((2 * ny, 2 * ny), BF16),
        vmem((2, kl, ny), F32),
        vmem((2, kl, ny), F32),
        vmem((2, HALO, ny), I32),
        vmem((2, HALO, ny), F32),
        vmem((2, 1, nobs), I32),
        vmem((2, share, nobs), F32),
        vmem((2, share, nobs), F32),
        vmem((2, 2, members * rows, ny), BF16),
        vmem((2, 2, members * rows, ny), BF16),
        vmem((share, width, ny), F32),
        vmem((2, n_mem, 2 * half + PACK, ny), I16),
        vmem((2, n_mem, 2 * half + PACK, ny), I16),
        vmem((2, 2, n_mem, half + PACK, ny), I16),
        vmem((share, n, ny), F32),
        vmem((share * n, ny), F32),
        vmem((margin, ny), F32),
        vmem((n_mem, margin, ny), F32),
        vmem((4, rows, ny), F32),
        vmem((2, n_mem, message, ny), I16),
        dma((2, 7)), dma((2, 7)),
        dma((2, 3, n_mem)), dma((2, 3, n_mem)),
        dma((2, n_mem)), dma((2, n_mem)),
    ]
    whole = pl.BlockSpec(memory_space=pltpu.VMEM)
    hbm = pl.BlockSpec(memory_space=pltpu.HBM)
    handed = pl.pallas_call(
        functools.partial(kernel, n_mem, n_tile, members, levels, width, ny, nobs),
        out_shape=(
            pltpu.VMEM((members * block, ny), F32), pltpu.VMEM((kl, 2 * ny), F32),
            pltpu.VMEM((2, block, block), BF16), pltpu.VMEM((2, kl, kl), BF16),
        ),
        in_specs=[hbm] * 8,
        out_specs=(whole,) * 4,
        scratch_shapes=scratch,
        compiler_params=pltpu.CompilerParams(
            collective_id=0, has_side_effects=True, vmem_limit_bytes=40 << 20
        ),
    )(*(pltpu.with_memory_space_constraint(x, pltpu.HBM) for x in (
        ensemble,
        control.reshape(members * block, ny),
        level_loc,
        wind_speed,
        cell_codes,
        obs_cell.reshape(1, nobs),
        innovation.reshape(n_mem, share, nobs),
        obs_sigma.reshape(n_mem, share, nobs),
    )))
    result = pl.pallas_call(
        functools.partial(finish, members, levels, width, ny),
        out_shape=jax.ShapeDtypeStruct((members * block, ny), F32),
        in_specs=[whole] * 4,
        out_specs=hbm,
        scratch_shapes=[vmem((members * block, ny), F32), dma((members // 2,))],
        compiler_params=pltpu.CompilerParams(vmem_limit_bytes=40 << 20),
    )(*(pltpu.with_memory_space_constraint(x, pltpu.VMEM) for x in handed))
    return result.reshape(members, levels, width, ny)


def solution(mesh):
    placed = (
        P("mem", None, "tile", None),
        P("mem", None, "tile", None),
        P(),
        P("tile", None),
        P("tile", None),
        P("tile"),
        P(None, "tile"),
        P(None, "tile"),
    )
    return jax.shard_map(
        functools.partial(body, mesh.shape["mem"], mesh.shape["tile"]),
        mesh=mesh, in_specs=placed, out_specs=P("mem", None, "tile", None), check_vma=False,
    )
```

```python
import contextlib
import functools

import jax
import jax.numpy as jnp
from jax import lax
from jax.experimental import pallas as pl
from jax.experimental.pallas import tpu as pltpu
from jax.sharding import PartitionSpec as P

V = 2
STEPS = 2
HALO = 8
PACK = 16
SPAN = 32760.0

diffusion_rate = 0.12
absorbing = 0.7
step_length = 0.5
huber_delta = 1.0

MESH = pl.DeviceIdType.MESH
F32 = jnp.float32
BF16 = jnp.bfloat16
I16 = jnp.int16
I32 = jnp.int32
HIGHEST = lax.Precision.HIGHEST
NT = (((1,), (1,)), ((), ()))
mark = contextlib.nullcontext


def log2(n):
    assert n & (n - 1) == 0
    return n.bit_length() - 1


def iota(shape, dim):
    return lax.broadcasted_iota(I32, shape, dim)


def split(x):
    hi = x.astype(BF16)
    return hi, (x - hi.astype(F32)).astype(BF16)


def mm(a, b):
    return jnp.dot(a, b, preferred_element_type=F32)


def nt(a, b):
    return lax.dot_general(a, b, NT, precision=HIGHEST, preferred_element_type=F32)


def dot3(a, b):
    ah, al = a
    bh, bl = split(b)
    return mm(ah, bh) + (mm(ah, bl) + mm(al, bh))


def up(n, to):
    return -(-n // to) * to


def reach_of(e):
    return 2 * STEPS + 2 - e


def blocks_of(e, share, width):
    reach = reach_of(e)
    return reach * share, up(reach * share + 1, PACK), up((width - 2 * reach) * share, PACK)


def wait_all(ref, sem):
    pltpu.make_async_copy(ref, ref, sem).wait()


def smoother(ny):
    yi = iota((1, ny), 1)
    from_south = jnp.where(yi > 0, 0.25, 0.0).astype(F32)
    from_north = jnp.where(yi < ny - 1, 0.25, 0.0).astype(F32)

    def smooth_y(v):
        return 0.5 * v + (from_south * pltpu.roll(v, 1, 1) + from_north * pltpu.roll(v, ny - 1, 1))

    return smooth_y


def exponent(parts, ny):
    most = None
    for p in parts:
        v = jnp.max(jnp.abs(p.reshape(-1, ny)), axis=0, keepdims=True)
        most = v if most is None else jnp.maximum(most, v)
    return jnp.floor(jnp.log2(jnp.maximum(most, 1e-30))) + 1.0


def encode(x, e):
    return jnp.round(x * (jnp.exp2(-e) * SPAN)).astype(I32).astype(I16)


def whole_number(q):
    return q.astype(I32).astype(F32)


def unit(code):
    return jnp.exp2(whole_number(code)[0:1]) * (1.0 / SPAN)


def kernel(
    n_mem, n_tile, members, levels, width, ny, nobs,
    ens_hbm, ctl_hbm, loc_hbm, wind_hbm, codes_hbm, cell_hbm, innov_hbm, sigma_hbm,
    ensf, adj_out, edges_out, mats_out, small_out,
    ens, ctl, loc, wind, codes, cell, obs, in_sem, hot,
    work, mats, small, blur2, coef,
    ctl_stage, ctl_halo, surf_stage, surf_halo, obs_halo, ens_stage, ens_halo,
    tot, own, stage0, stage1, src0, src1, main0, main1, halo0, halo1, inc0, inc1,
    flat, fringe, fringes, marks_all, ag0, ag1,
    r0_send, r0_recv, rs_send, rs_recv, ag_send, ag_recv,
):
    m = lax.axis_index("mem")
    t = lax.axis_index("tile")
    has = (t > 0, t < n_tile - 1)
    rows = V * levels
    share = rows // n_mem
    block = levels * width
    kl = members * levels
    xs, ys = log2(width), log2(ny)
    n = HALO + width + HALO
    cuts = nobs // ny
    inner_rows = share * width

    def tell(dev):
        pl.semaphore_signal(pltpu.get_barrier_semaphore(), inc=1, device_id=dev, device_id_type=MESH)

    for d in range(1, n_mem):
        tell((lax.rem(m + d, n_mem), t))

    @pl.when(has[0])
    def _():
        for d in range(n_mem):
            tell((lax.rem(m + d, n_mem), t - 1))

    @pl.when(has[1])
    def _():
        for d in range(n_mem):
            tell((lax.rem(m + d, n_mem), t + 1))

    loads = [
        pltpu.make_async_copy(src, dst, in_sem.at[i])
        for i, (src, dst) in enumerate((
            (loc_hbm, loc), (ctl_hbm, ctl), (ens_hbm, ens), (wind_hbm, wind), (codes_hbm, codes),
            (cell_hbm, cell), (innov_hbm.at[m], obs.at[0]), (sigma_hbm.at[m], obs.at[1]),
        ))
    ]
    for load in loads:
        load.start()

    def to_side(side, d, src, dst, ssem, rsem):
        dev = (lax.rem(m + d, n_mem), t + 1 if side == 0 else t - 1)
        return pltpu.make_async_remote_copy(
            src_ref=src, dst_ref=dst, send_sem=ssem, recv_sem=rsem, device_id=dev, device_id_type=MESH
        )

    def to_mem(d, src, dst, ssem, rsem):
        return pltpu.make_async_remote_copy(
            src_ref=src, dst_ref=dst, send_sem=ssem, recv_sem=rsem,
            device_id=(lax.rem(m + d, n_mem), t), device_id_type=MESH,
        )

    CTL, SURF, OBS, ENS = range(4)
    first_msgs = [
        [
            to_side(side, 0, s, d, r0_send.at[side, i], r0_recv.at[side, i])
            for i, (s, d) in enumerate((
                (ctl_stage.at[side], ctl_halo.at[side]),
                (surf_stage.at[side], surf_halo.at[side]),
                (obs, obs_halo.at[side]),
                (ens_stage.at[side], ens_halo.at[side]),
            ))
        ]
        for side in (0, 1)
    ]

    def start_sides(which):
        for side in (0, 1):
            @pl.when(has[1 - side])
            def _():
                for i in which:
                    first_msgs[side][i].start()

    def recv_sides(which):
        for side in (0, 1):
            @pl.when(has[side])
            def _():
                for i in which:
                    first_msgs[side][i].wait_recv()

    for side in (0, 1):
        @pl.when(jnp.logical_not(has[side]))
        def _():
            ctl_halo[side] = jnp.zeros_like(ctl_halo[side])
            surf_halo[side, pl.ds(0, HALO)] = jnp.zeros((HALO, ny), F32)
            surf_halo[side, pl.ds(HALO, HALO)] = jnp.ones((HALO, ny), F32)
            surf_halo[side, pl.ds(2 * HALO, cuts)] = jnp.full((cuts, ny), -1.0, F32)
            obs_halo[side, 0] = jnp.zeros((share, nobs), F32)
            obs_halo[side, 1] = jnp.ones((share, nobs), F32)
            ens_halo[side] = jnp.zeros_like(ens_halo[side])
            for halo in (halo0, halo1):
                halo[side] = jnp.zeros_like(halo[side])

    smooth_y = smoother(ny)
    gap = lambda shape, mask: jnp.abs((iota(shape, 0) & mask) - (iota(shape, 1) & mask))
    lev = lambda shape, dim, shift: iota(shape, dim) >> shift

    with mark("w_loc"):
        loads[0].wait()
    with mark("mats0"):
        lo = loc[...]
        spread = (lev((levels, block), 1, xs) == iota((levels, block), 0)).astype(BF16)
        repeat = ((iota((levels, kl), 1) & (levels - 1)) == iota((levels, kl), 0)).astype(BF16)
        near_x = gap((block, block), width - 1)
        near_x = jnp.where(near_x == 0, 0.5, jnp.where(near_x == 1, 0.25, 0.0)).astype(F32)
        same_k = (lev((kl, kl), 0, log2(levels)) == lev((kl, kl), 1, log2(levels))).astype(F32)
        for j, piece in enumerate(split(lo)):
            p = piece.astype(F32)
            tall = jnp.broadcast_to(p[:, None, :], (levels, width, levels)).reshape(block, levels)
            mats[0, j] = (mm(tall.astype(BF16), spread) * near_x).astype(BF16)
            tall = jnp.concatenate([p] * members, axis=0)
            small[0, j] = (mm(tall.astype(BF16), repeat) * same_k).astype(BF16)

    with mark("w_ctl"):
        loads[1].wait()
    ctl_stage[0] = ctl[pl.ds(width - 1, kl, stride=width), :]
    ctl_stage[1] = ctl[pl.ds(0, kl, stride=width), :]

    with mark("w_barrier"):
        peers = n_mem - 1 + n_mem * (jnp.where(t > 0, 1, 0) + jnp.where(t < n_tile - 1, 1, 0))
        pl.semaphore_wait(pltpu.get_barrier_semaphore(), peers)

    start_sides((CTL,))

    with mark("mix_a0"):
        big = (mats[0, 0], mats[0, 1])
        for k in range(0, members, 2):
            both = jnp.concatenate(
                [ctl[k * block:(k + 1) * block, :], ctl[(k + 1) * block:(k + 2) * block, :]], axis=1
            )
            done = dot3(big, both)
            work[k * block:(k + 1) * block, :] = smooth_y(done[:, :ny])
            work[(k + 1) * block:(k + 2) * block, :] = smooth_y(done[:, ny:])

    with mark("stage"):
        for load in loads[2:]:
            load.wait()
        for side, at in ((0, pl.ds(width - HALO, HALO)), (1, pl.ds(0, HALO))):
            surf_stage[side, pl.ds(0, HALO)] = wind[at, :]
            surf_stage[side, pl.ds(HALO, HALO)] = codes[at, :].astype(F32)
            for c in range(cuts):
                surf_stage[side, pl.ds(2 * HALO + c, 1)] = cell[:, c * ny:(c + 1) * ny].astype(F32)
        for k in range(members):
            ensf[pl.ds(k * rows * width, rows * width), :] = ens[k].astype(F32).reshape(rows * width, ny)
        for i in (0, 1):
            ens_stage[0, i] = ensf[pl.ds(width - 1 - i, members * rows, stride=width), :].astype(BF16)
            ens_stage[1, i] = ensf[pl.ds(i, members * rows, stride=width), :].astype(BF16)

    with mark("w_ctlhalo"):
        recv_sides((CTL,))
    with mark("side0"):
        side = dot3((small[0, 0], small[0, 1]), jnp.concatenate([ctl_halo[0], ctl_halo[1]], axis=1))
        for j, x in ((0, 0), (1, width - 1)):
            at = pl.ds(x, kl, stride=width)
            work[at, :] = work[at, :] + smooth_y(0.25 * side[:, j * ny:(j + 1) * ny])

    def halo_cells(side):
        return jnp.concatenate([surf_halo[side, pl.ds(2 * HALO + c, 1)] for c in range(cuts)], axis=1).astype(I32)

    def coefficients():
        code = jnp.concatenate(
            [surf_halo[0, pl.ds(HALO, HALO)], codes[...].astype(F32), surf_halo[1, pl.ds(HALO, HALO)]], axis=0
        )
        speed = jnp.concatenate([surf_halo[0, pl.ds(0, HALO)], wind[...], surf_halo[1, pl.ds(0, HALO)]], axis=0)
        opened = (code != 1.0).astype(F32)
        absorb = jnp.where(code == 2.0, absorbing, 1.0).astype(F32)
        yy = iota(code.shape, 1)
        west = lambda v: pltpu.roll(v, 1, 0)
        east = lambda v: pltpu.roll(v, n - 1, 0)
        south = lambda v: pltpu.roll(v, 1, 1)
        north = lambda v: pltpu.roll(v, ny - 1, 1)
        oe = opened * east(opened)
        ow = opened * west(opened)
        on = jnp.where(yy < ny - 1, opened * north(opened), 0.0)
        os = jnp.where(yy > 0, opened * south(opened), 0.0)
        k = diffusion_rate
        center = 1.0 - k * (oe + ow + on + os) - speed * oe
        every = (
            absorb * center, absorb * (k + west(speed)) * ow, absorb * k * oe, absorb * k * os, absorb * k * on,
            center * absorb, k * ow * west(absorb), (k + speed) * oe * east(absorb),
            k * os * south(absorb), k * on * north(absorb),
        )
        for i, v in enumerate(every):
            coef[i] = jnp.broadcast_to(v[:, None, :], (n, share, ny))

    def stencil(q, first, which):
        count = q.shape[0] - 2
        c = lambda i: coef[which + i, pl.ds(HALO + first + 1, count)]
        mid = q[1:-1]
        turn = lambda by: pltpu.roll(mid.reshape(count * share, ny), by, 1).reshape(count, share, ny)
        return c(0) * mid + c(1) * q[:-2] + c(2) * q[2:] + c(3) * turn(1) + c(4) * turn(ny - 1)

    def observe(state, reach):
        tiles = (
            (halo_cells(0), obs_halo[0, 0], obs_halo[0, 1], 0, reach, width - reach),
            (cell[...], obs[0], obs[1], reach, width, 0),
            (halo_cells(1), obs_halo[1, 0], obs_halo[1, 1], reach + width, reach, 0),
        )
        pieces = []
        for i, (where, seen, dev, at, count, offset) in enumerate(tiles):
            hot_y = hot[i]
            place = jnp.broadcast_to(where >> ys, (share, nobs))
            hit = place[None] == iota((count, share, nobs), 0) + offset
            hi, low = split(state[at:at + count].reshape(count * share, ny))
            got = mm(jnp.concatenate([hi, low], axis=1), jnp.concatenate([hot_y, hot_y], axis=0))
            sampled = jnp.sum(jnp.where(hit, got.reshape(count, share, nobs), 0.0), axis=0)
            scaled = (sampled - seen) / dev
            weight = jnp.clip(scaled, -huber_delta, huber_delta) / dev
            put = [
                jnp.where(hit, w.astype(F32)[None], 0.0).reshape(count * share, nobs).astype(BF16)
                for w in split(weight)
            ]
            total = lax.dot_general(
                jnp.concatenate(put, axis=1), jnp.concatenate([hot_y, hot_y], axis=1), NT, preferred_element_type=F32
            )
            pieces.append(total.reshape(count, share, ny))
        return jnp.concatenate(pieces, axis=0)

    exchange = ((stage0, src0, main0, halo0, inc0), (stage1, src1, main1, halo1, inc1))

    def members_sum(e):
        stage, src, main, halo, _ = exchange[e]
        reach = reach_of(e)
        data, hb, mb = blocks_of(e, share, width)
        copies = []
        for d in list(range(1, n_mem)) + [0]:
            who = lax.rem(m + d, n_mem)
            r0 = who * share
            l0 = lax.rem(r0, levels)
            total = jnp.zeros((share, width, ny), F32)
            for k in range(members):
                a = work[pl.ds(pl.multiple_of(k * block + l0 * width, width), share * width), :]
                total += ens[k, pl.ds(r0, share)].astype(F32) * a.reshape(share, width, ny)
            tot[d] = total.reshape(inner_rows, ny)
            ex = exponent([total], ny)
            scale = jnp.exp2(-ex) * SPAN
            for x in range(width):
                v = tot[d, pl.ds(x, share, stride=width), :]
                if d == 0:
                    own[pl.ds(x * share, share), :] = v
                at = x * share
                if x >= reach:
                    at += hb - data
                if x >= width - reach:
                    at += mb - (width - 2 * reach) * share
                stage[d, pl.ds(at, share), :] = jnp.round(v * scale)
            for at in (data, hb + mb + data):
                stage[d, pl.ds(at, hb - data), :] = jnp.broadcast_to(ex, (hb - data, ny))
            used = (width - 2 * reach) * share
            if used < mb:
                stage[d, pl.ds(hb + used, mb - used), :] = jnp.zeros((mb - used, ny), F32)
            src[d] = stage[d].astype(I32).astype(I16)
            if d:
                copy = to_mem(d, src.at[d], main.at[d - 1], rs_send.at[e, 2], rs_recv.at[e, 2])
                copy.start()
        for side in (0, 1):
            @pl.when(has[1 - side])
            def _():
                for d in range(n_mem):
                    to_side(
                        side, d, src.at[d, pl.ds((hb + mb, 0)[side], hb)], halo.at[side, d],
                        rs_send.at[e, side], rs_recv.at[e, side],
                    ).start()

    def gather_sum(e):
        _, _, main, halo, inc = exchange[e]
        data, hb, mb = blocks_of(e, share, width)
        used = width * share - 2 * data
        wait_all(main, rs_recv.at[e, 2])
        for side in (0, 1):
            @pl.when(has[side])
            def _():
                wait_all(halo.at[side], rs_recv.at[e, side])
        pieces = [own[pl.ds(0, data), :], own[pl.ds(data, used), :], own[pl.ds(data + used, data), :]]
        for d in range(n_mem - 1):
            first = whole_number(main[d, pl.ds(0, hb)])
            u = jnp.exp2(first[data:data + 1]) * (1.0 / SPAN)
            pieces[0] = pieces[0] + (first * u)[:data]
            pieces[1] = pieces[1] + (whole_number(main[d, pl.ds(hb, mb)]) * u)[:used]
            pieces[2] = pieces[2] + (whole_number(main[d, pl.ds(hb + mb, hb)]) * u)[:data]
        outer = []
        for side in (0, 1):
            total = None
            for d in range(n_mem):
                v = whole_number(halo[side, d])
                v = v * (jnp.exp2(v[data:data + 1]) * (1.0 / SPAN))
                total = v if total is None else total + v
            outer.append(total[:data])
        at = 0
        for v in (outer[0], *pieces, outer[1]):
            inc[pl.ds(at, v.shape[0]), :] = v
            at += v.shape[0]

    def observation_term(e, field):
        ag = (ag0, ag1)[e]
        reach = reach_of(e)
        margin = ag.shape[1] - inner_rows - PACK
        q = field.reshape(width + 2 * reach, share, ny)
        for i in range(STEPS):
            q = stencil(q, i - reach, 0)
        with mark("observe"):
            q = observe(q, reach - STEPS)
        for i in range(STEPS):
            q = stencil(q, i + STEPS - reach, 5)
        spare = reach - 2 * STEPS
        lines = [spare - 1, spare + width] + ([spare - 2, spare + width + 1] if spare > 1 else [])
        if margin > len(lines) * share:
            fringe[...] = jnp.zeros_like(fringe)
        for i, x in enumerate(lines):
            fringe[pl.ds(i * share, share), :] = q[x]
        for x in range(width):
            flat[pl.ds(x, share, stride=width), :] = q[spare + x]
        ex = exponent([q], ny)
        ag[m, pl.ds(0, inner_rows)] = encode(flat[...], ex)
        ag[m, pl.ds(inner_rows, margin)] = encode(fringe[pl.ds(0, margin), :], ex)
        ag[m, pl.ds(inner_rows + margin, PACK)] = jnp.broadcast_to(ex, (PACK, ny)).astype(I32).astype(I16)
        for d in range(1, n_mem):
            to_mem(d, ag.at[m], ag.at[m], ag_send.at[e], ag_recv.at[e]).start()

    def adjoint_rows(e):
        ag = (ag0, ag1)[e]
        margin = ag.shape[1] - inner_rows - PACK
        for i in range(n_mem):
            u = unit(ag[i, pl.ds(inner_rows + margin, PACK)])
            adj_out[pl.ds(i * inner_rows, inner_rows), :] = whole_number(ag[i, pl.ds(0, inner_rows)]) * u
            fringes[i, pl.ds(0, margin)] = whole_number(ag[i, pl.ds(inner_rows, margin)]) * u
            for j in range(4 - 2 * e):
                marks_all[j, pl.ds(i * share, share), :] = fringes[i, pl.ds(j * share, share), :]
        terms = []
        for j in range(4 - 2 * e):
            p = ens_halo[j % 2, j // 2].astype(F32).reshape(members, rows, ny) * marks_all[j][None]
            terms.append((p[:, :levels] + p[:, levels:]).reshape(kl, ny))
        return terms

    with mark("part0"):
        members_sum(0)
    with mark("hidden"):
        start_sides((SURF, OBS, ENS))
        pick = (lev((block, levels), 0, xs) == iota((block, levels), 1)).astype(F32)
        pick2 = ((iota((kl, levels), 0) & (levels - 1)) == iota((kl, levels), 1)).astype(F32)
        both = nt(lo, lo)
        far_x = gap((block, block), width - 1)
        far_x = jnp.where(far_x == 0, 0.375, jnp.where(far_x == 1, 0.25, jnp.where(far_x == 2, 0.0625, 0.0)))
        xr, xc = iota((block, block), 0) & (width - 1), iota((block, block), 1) & (width - 1)
        for side, x in ((0, 0), (1, width - 1)):
            lost = jnp.where(has[side], 0.0, 0.0625).astype(F32)
            far_x = far_x - jnp.where((xr == x) & (xc == x), lost, 0.0)
        full = nt(jnp.dot(pick, both, precision=HIGHEST, preferred_element_type=F32), pick) * far_x
        for j, piece in enumerate(split(full)):
            mats[1, j] = piece
        full = nt(jnp.dot(pick2, both, precision=HIGHEST, preferred_element_type=F32), pick2) * same_k
        for j, piece in enumerate(split(full)):
            small[1, j] = piece
        for j, piece in enumerate(split(nt(nt(pick, lo), pick) * near_x)):
            mats_out[j] = piece
        for j, piece in enumerate(split(nt(nt(pick2, lo), pick2) * same_k)):
            small_out[j] = piece
        yr, yc = iota((2 * ny, 2 * ny), 0), iota((2 * ny, 2 * ny), 1)
        far_y = jnp.abs(yr - yc)
        corner = (yr & (ny - 1) == 0) | (yr & (ny - 1) == ny - 1)
        far_y = jnp.where(
            far_y == 0, jnp.where(corner, 0.3125, 0.375),
            jnp.where(far_y == 1, 0.25, jnp.where(far_y == 2, 0.0625, 0.0)),
        )
        blur2[...] = jnp.where((yr >> ys) == (yc >> ys), far_y, 0.0).astype(BF16)
        recv_sides((SURF, OBS))
        for i, where in enumerate((halo_cells(0), cell[...], halo_cells(1))):
            hot[i] = (iota((ny, nobs), 0) == (where & (ny - 1))).astype(BF16)
        coefficients()
    with mark("w_rs0"):
        gather_sum(0)
    with mark("obs0"):
        observation_term(0, inc0[...])
    with mark("w_ag0"):
        wait_all(ag0.at[pl.ds(0, n_mem - 1)], ag_recv.at[0])
        recv_sides((ENS,))
    with mark("mix1"):
        terms = adjoint_rows(0)
        big = (mats[1, 0], mats[1, 1])

        def blur(v):
            hi, low = split(v)
            return mm(hi, blur2[...]) + mm(low, blur2[...])

        for k in range(0, members, 2):
            done = blur(dot3(big, jnp.concatenate([member_term(ensf, adj_out, block, k + i) for i in (0, 1)], axis=1)))
            work[k * block:(k + 1) * block, :] = done[:, :ny]
            work[(k + 1) * block:(k + 2) * block, :] = done[:, ny:]
        tiny = (small[1, 0], small[1, 1])
        close = dot3(tiny, jnp.concatenate(terms[:2], axis=1))
        distant = blur(0.25 * close + 0.0625 * dot3(tiny, jnp.concatenate(terms[2:], axis=1)))
        close = blur(0.0625 * close)
        for side, first, second in ((0, 0, 1), (1, width - 1, width - 2)):
            for x, v in ((first, distant), (second, close)):
                at = pl.ds(x, kl, stride=width)
                work[at, :] = work[at, :] + v[:, side * ny:(side + 1) * ny]
    with mark("part1"):
        members_sum(1)
    with mark("w_rs1"):
        gather_sum(1)
    with mark("obs1"):
        observation_term(1, step_length * (inc0[pl.ds(share, inc1.shape[0]), :] - inc1[...]))
    with mark("w_ag1"):
        wait_all(ag1.at[pl.ds(0, n_mem - 1)], ag_recv.at[1])
    with mark("term1"):
        terms = adjoint_rows(1)
        for side in (0, 1):
            edges_out[:, side * ny:(side + 1) * ny] = terms[side]
    with mark("drain"):
        for e in (0, 1):
            _, _, main, halo, _ = exchange[e]
            wait_all(main, rs_send.at[e, 2])
            wait_all((ag0, ag1)[e].at[pl.ds(0, n_mem - 1)], ag_send.at[e])
            for side in (0, 1):
                @pl.when(has[1 - side])
                def _():
                    wait_all(halo.at[side], rs_send.at[e, side])
        for side in (0, 1):
            @pl.when(has[1 - side])
            def _():
                for copy in first_msgs[side]:
                    copy.wait_send()


def member_term(ensf, adj, block, k):
    at = 2 * k * block
    return ensf[pl.ds(at, block), :] * adj[:block] + ensf[pl.ds(at + block, block), :] * adj[block:]


def finish(members, levels, width, ny, ensf, adj, edges, mats, small, out, work, sem):
    block = levels * width
    smooth_y = smoother(ny)
    side = 0.25 * dot3((small[0], small[1]), edges[...])
    sides = [smooth_y(side[:, j * ny:(j + 1) * ny]) for j in (0, 1)]
    big = (mats[0], mats[1])
    for k in range(0, members, 2):
        done = dot3(big, jnp.concatenate([member_term(ensf, adj, block, k + i) for i in (0, 1)], axis=1))
        for i in (0, 1):
            base = (k + i) * block
            work[pl.ds(base, block), :] = smooth_y(done[:, i * ny:(i + 1) * ny])
            for j, x in ((0, 0), (1, width - 1)):
                at = pl.ds(base + x, levels, stride=width)
                work[at, :] = work[at, :] + sides[j][(k + i) * levels:(k + i + 1) * levels]
            at = pl.ds(base, block)
            pltpu.make_async_copy(work.at[at], out.at[at], sem.at[0]).start()
    pltpu.make_async_copy(work, out, sem.at[0]).wait()


def body(n_mem, n_tile, ensemble, control, level_loc, wind_speed, cell_codes, obs_cell, innovation, obs_sigma):
    members, rows, width, ny = ensemble.shape
    levels = control.shape[1]
    assert width >= 2 * HALO and members % 2 == 0 and rows == 2 * levels
    nobs = obs_cell.shape[0]
    share = rows // n_mem
    kl = members * levels
    block = levels * width
    n = width + 2 * HALO
    vmem = pltpu.VMEM
    dma = pltpu.SemaphoreType.DMA
    sizes = [blocks_of(e, share, width) for e in (0, 1)]
    full = [2 * hb + mb for _, hb, mb in sizes]
    margins = [up((4 - 2 * e) * share, PACK) for e in (0, 1)]
    surf = up(2 * HALO + nobs // ny, 8)
    scratch = [
        vmem((members, rows, width, ny), BF16),
        vmem((members * block, ny), F32),
        vmem((levels, levels), F32),
        vmem((width, ny), F32),
        vmem((width, ny), I32),
        vmem((1, nobs), I32),
        vmem((2, share, nobs), F32),
        dma((8,)),
        vmem((3, ny, nobs), BF16),
        vmem((members * block, ny), F32),
        vmem((2, 2, block, block), BF16),
        vmem((2, 2, kl, kl), BF16),
        vmem((2 * ny, 2 * ny), BF16),
        vmem((10, n, share, ny), F32),
        vmem((2, kl, ny), F32),
        vmem((2, kl, ny), F32),
        vmem((2, surf, ny), F32),
        vmem((2, surf, ny), F32),
        vmem((2, 2, share, nobs), F32),
        vmem((2, 2, members * rows, ny), BF16),
        vmem((2, 2, members * rows, ny), BF16),
        vmem((n_mem, share * width, ny), F32),
        vmem((share * width, ny), F32),
        *(vmem((n_mem, full[e], ny), F32) for e in (0, 1)),
        *(vmem((n_mem, full[e], ny), I16) for e in (0, 1)),
        *(vmem((n_mem - 1, full[e], ny), I16) for e in (0, 1)),
        *(vmem((2, n_mem, sizes[e][1], ny), I16) for e in (0, 1)),
        *(vmem((share * width + 2 * sizes[e][0], ny), F32) for e in (0, 1)),
        vmem((share * width, ny), F32),
        vmem((margins[0], ny), F32),
        vmem((n_mem, margins[0], ny), F32),
        vmem((4, rows, ny), F32),
        *(vmem((n_mem, share * width + margins[e] + PACK, ny), I16) for e in (0, 1)),
        dma((2, 4)), dma((2, 4)),
        dma((2, 3)), dma((2, 3)),
        dma((2,)), dma((2,)),
    ]
    whole = pl.BlockSpec(memory_space=pltpu.VMEM)
    hbm = pl.BlockSpec(memory_space=pltpu.HBM)
    handed = pl.pallas_call(
        functools.partial(kernel, n_mem, n_tile, members, levels, width, ny, nobs),
        out_shape=(
            vmem((members * rows * width, ny), F32), vmem((rows * width, ny), F32), vmem((kl, 2 * ny), F32),
            vmem((2, block, block), BF16), vmem((2, kl, kl), BF16),
        ),
        in_specs=[hbm] * 8,
        out_specs=(whole,) * 5,
        scratch_shapes=scratch,
        compiler_params=pltpu.CompilerParams(
            collective_id=0, has_side_effects=True, vmem_limit_bytes=40 << 20
        ),
    )(*(pltpu.with_memory_space_constraint(x, pltpu.HBM) for x in (
        ensemble,
        control.reshape(members * block, ny),
        level_loc,
        wind_speed,
        cell_codes,
        obs_cell.reshape(1, nobs),
        innovation.reshape(n_mem, share, nobs),
        obs_sigma.reshape(n_mem, share, nobs),
    )))
    result = pl.pallas_call(
        functools.partial(finish, members, levels, width, ny),
        out_shape=jax.ShapeDtypeStruct((members * block, ny), F32),
        in_specs=[whole] * 5,
        out_specs=hbm,
        scratch_shapes=[vmem((members * block, ny), F32), dma((1,))],
        compiler_params=pltpu.CompilerParams(vmem_limit_bytes=40 << 20),
    )(*(pltpu.with_memory_space_constraint(x, pltpu.VMEM) for x in handed))
    return result.reshape(members, levels, width, ny)


def solution(mesh):
    placed = (
        P("mem", None, "tile", None),
        P("mem", None, "tile", None),
        P(),
        P("tile", None),
        P("tile", None),
        P("tile"),
        P(None, "tile"),
        P(None, "tile"),
    )
    return jax.shard_map(
        functools.partial(body, mesh.shape["mem"], mesh.shape["tile"]),
        mesh=mesh, in_specs=placed, out_specs=P("mem", None, "tile", None), check_vma=False,
    )
```

```python
import contextlib
import functools

import jax
import jax.numpy as jnp
from jax import lax
from jax.experimental import pallas as pl
from jax.experimental.pallas import tpu as pltpu
from jax.sharding import PartitionSpec as P

V = 2
STEPS = 2
HALO = 8
PACK = 16
SPAN = 32760.0

diffusion_rate = 0.12
absorbing = 0.7
step_length = 0.5
huber_delta = 1.0

MESH = pl.DeviceIdType.MESH
F32 = jnp.float32
BF16 = jnp.bfloat16
I16 = jnp.int16
I32 = jnp.int32
HIGHEST = lax.Precision.HIGHEST
NT = (((1,), (1,)), ((), ()))
mark = contextlib.nullcontext


def log2(n):
    assert n & (n - 1) == 0
    return n.bit_length() - 1


def iota(shape, dim):
    return lax.broadcasted_iota(I32, shape, dim)


def split(x):
    hi = x.astype(BF16)
    return hi, (x - hi.astype(F32)).astype(BF16)


def mm(a, b):
    return jnp.dot(a, b, preferred_element_type=F32)


def nt(a, b):
    return lax.dot_general(a, b, NT, precision=HIGHEST, preferred_element_type=F32)


def dot3(a, b):
    ah, al = a
    bh, bl = split(b)
    return mm(jnp.concatenate([ah, ah, al], axis=1), jnp.concatenate([bh, bl, bh], axis=0))


def dot3_apart(a, b):
    ah, al = a
    bh, bl = split(b)
    return mm(ah, bh) + (mm(ah, bl) + mm(al, bh))


def up(n, to):
    return -(-n // to) * to


def reach_of(e):
    return 2 * STEPS + 2 - e


def blocks_of(e, share, width):
    reach = reach_of(e)
    return reach * share, up(reach * share + 1, PACK), up((width - 2 * reach) * share, PACK)


def wait_all(ref, sem):
    pltpu.make_async_copy(ref, ref, sem).wait()


def smoother(ny):
    yi = iota((1, ny), 1)
    from_south = jnp.where(yi > 0, 0.25, 0.0).astype(F32)
    from_north = jnp.where(yi < ny - 1, 0.25, 0.0).astype(F32)

    def smooth_y(v):
        return 0.5 * v + (from_south * pltpu.roll(v, 1, 1) + from_north * pltpu.roll(v, ny - 1, 1))

    return smooth_y


def exponent(parts, ny):
    most = None
    for p in parts:
        v = jnp.max(jnp.abs(p.reshape(-1, ny)), axis=0, keepdims=True)
        most = v if most is None else jnp.maximum(most, v)
    return jnp.floor(jnp.log2(jnp.maximum(most, 1e-30))) + 1.0


def encode(x, e):
    return jnp.round(x * (jnp.exp2(-e) * SPAN)).astype(I32).astype(I16)


def whole_number(q):
    return q.astype(I32).astype(F32)


def unit(code):
    return jnp.exp2(whole_number(code)[0:1]) * (1.0 / SPAN)


def kernel(
    n_mem, n_tile, members, levels, width, ny, nobs,
    ens_hbm, ctl_hbm, loc_hbm, wind_hbm, codes_hbm, cell_hbm, innov_hbm, sigma_hbm,
    ensf, adj_out, edges_out, mats_out, small_out,
    ens, ctl, loc, wind, codes, cell, obs, in_sem, hot,
    work, mats, small, blur2, coef,
    ctl_stage, ctl_halo, surf_stage, surf_halo, obs_halo, ens_stage, ens_halo,
    tot, own, stage0, stage1, src0, src1, main0, main1, halo0, halo1, inc0, inc1,
    flat, fringe, fringes, marks_all, ag0, ag1, edge_src, edge_main, edge_halo, wide,
    r0_send, r0_recv, rs_send, rs_recv, ag_send, ag_recv, edge_send, edge_recv,
):
    m = lax.axis_index("mem")
    t = lax.axis_index("tile")
    has = (t > 0, t < n_tile - 1)
    rows = V * levels
    share = rows // n_mem
    block = levels * width
    kl = members * levels
    xs, ys = log2(width), log2(ny)
    n = HALO + width + HALO
    cuts = nobs // ny
    assert 1 << log2(n_mem) == n_mem
    peers = range(n_mem - 1, 0, -1)
    outward = 1 - (t & 1)
    inner_rows = share * width

    def tell(dev):
        pl.semaphore_signal(pltpu.get_barrier_semaphore(), inc=1, device_id=dev, device_id_type=MESH)

    for d in peers:
        tell((m ^ d, t))

    @pl.when(has[0])
    def _():
        for d in range(n_mem):
            tell((m ^ d, t - 1))

    @pl.when(has[1])
    def _():
        for d in range(n_mem):
            tell((m ^ d, t + 1))

    loads = [
        pltpu.make_async_copy(src, dst, in_sem.at[i])
        for i, (src, dst) in enumerate((
            (loc_hbm, loc),
            *((ctl_hbm.at[pl.ds(at, 2 * block)], ctl.at[pl.ds(at, 2 * block)]) for at in range(0, members * block, 2 * block)),
            (ens_hbm, ens), (wind_hbm, wind), (codes_hbm, codes),
            (cell_hbm, cell), (innov_hbm.at[m], obs.at[0]), (sigma_hbm.at[m], obs.at[1]),
        ))
    ]
    for load in loads:
        load.start()

    def to_side(side, d, src, dst, ssem, rsem):
        dev = (m ^ d, t + 1 - 2 * side)
        return pltpu.make_async_remote_copy(
            src_ref=src, dst_ref=dst, send_sem=ssem, recv_sem=rsem, device_id=dev, device_id_type=MESH
        )

    def to_mem(d, src, dst, ssem, rsem):
        return pltpu.make_async_remote_copy(
            src_ref=src, dst_ref=dst, send_sem=ssem, recv_sem=rsem,
            device_id=(m ^ d, t), device_id_type=MESH,
        )

    ctl_loads, late_loads = loads[1:1 + members // 2], loads[1 + members // 2:]
    def both_sides(start):
        for s in (outward, 1 - outward):
            dev = t + 1 - 2 * s

            @pl.when((dev >= 0) & (dev < n_tile))
            def _():
                start(s)

    CTL, SURF, OBS, ENS = range(4)
    def first_msg(side, i):
        s, d = (
            (ctl_stage.at[side], ctl_halo.at[side]),
            (surf_stage.at[side], surf_halo.at[side]),
            (obs, obs_halo.at[side]),
            (ens_stage.at[side], ens_halo.at[side]),
        )[i]
        return to_side(side, 0, s, d, r0_send.at[side, i], r0_recv.at[side, i])

    def start_sides(which):
        def start(side):
            for i in which:
                first_msg(side, i).start()

        both_sides(start)

    def recv_sides(which):
        for side in (0, 1):
            @pl.when(has[side])
            def _():
                for i in which:
                    first_msg(side, i).wait_recv()

    for side in (0, 1):
        @pl.when(jnp.logical_not(has[side]))
        def _():
            ctl_halo[side] = jnp.zeros_like(ctl_halo[side])
            surf_halo[side, pl.ds(0, HALO)] = jnp.zeros((HALO, ny), F32)
            surf_halo[side, pl.ds(HALO, HALO)] = jnp.ones((HALO, ny), F32)
            surf_halo[side, pl.ds(2 * HALO, cuts)] = jnp.full((cuts, ny), -1.0, F32)
            obs_halo[side, 0] = jnp.zeros((share, nobs), F32)
            obs_halo[side, 1] = jnp.ones((share, nobs), F32)
            ens_halo[side] = jnp.zeros_like(ens_halo[side])
            for halo in (halo0, halo1, edge_halo):
                halo[side] = jnp.zeros_like(halo[side])

    smooth_y = smoother(ny)
    gap = lambda shape, mask: jnp.abs((iota(shape, 0) & mask) - (iota(shape, 1) & mask))
    lev = lambda shape, dim, shift: iota(shape, dim) >> shift

    with mark("w_loc"):
        loads[0].wait()
    with mark("mats0"):
        lo = loc[...]
        spread = (lev((levels, block), 1, xs) == iota((levels, block), 0)).astype(BF16)
        repeat = ((iota((levels, kl), 1) & (levels - 1)) == iota((levels, kl), 0)).astype(BF16)
        near_x = gap((block, block), width - 1)
        near_x = jnp.where(near_x == 0, 0.5, jnp.where(near_x == 1, 0.25, 0.0)).astype(F32)
        same_k = (lev((kl, kl), 0, log2(levels)) == lev((kl, kl), 1, log2(levels))).astype(F32)
        for j, piece in enumerate(split(lo)):
            p = piece.astype(F32)
            tall = jnp.broadcast_to(p[:, None, :], (levels, width, levels)).reshape(block, levels)
            mats[0, j] = (mm(tall.astype(BF16), spread) * near_x).astype(BF16)
            tall = jnp.concatenate([p] * members, axis=0)
            small[0, j] = (mm(tall.astype(BF16), repeat) * same_k).astype(BF16)

    def mix_pair(k):
        both = jnp.concatenate(
            [ctl[k * block:(k + 1) * block, :], ctl[(k + 1) * block:(k + 2) * block, :]], axis=1
        )
        wide[k // 2] = dot3((mats[0, 0], mats[0, 1]), both)

    with mark("mix_first"):
        ctl_loads[0].wait()
        mix_pair(0)
    with mark("w_ctl"):
        for load in ctl_loads[1:]:
            load.wait()
    ctl_stage[0] = ctl[pl.ds(width - 1, kl, stride=width), :]
    ctl_stage[1] = ctl[pl.ds(0, kl, stride=width), :]

    with mark("w_barrier"):
        count = n_mem - 1 + n_mem * (jnp.where(t > 0, 1, 0) + jnp.where(t < n_tile - 1, 1, 0))
        pl.semaphore_wait(pltpu.get_barrier_semaphore(), count)

    start_sides((CTL,))

    with mark("mix_a0"):
        for k in range(2, members, 2):
            mix_pair(k)
        for k in range(members):
            work[pl.ds(k * block, block), :] = smooth_y(wide[k // 2, :, (k % 2) * ny:(k % 2 + 1) * ny])

    with mark("stage"):
        for load in late_loads:
            load.wait()
        for side, at in ((0, pl.ds(width - HALO, HALO)), (1, pl.ds(0, HALO))):
            surf_stage[side, pl.ds(0, HALO)] = wind[at, :]
            surf_stage[side, pl.ds(HALO, HALO)] = codes[at, :].astype(F32)
            for c in range(cuts):
                surf_stage[side, pl.ds(2 * HALO + c, 1)] = cell[:, c * ny:(c + 1) * ny].astype(F32)
        start_sides((SURF,))

    def member_edges():
        for k in range(members):
            ensf[pl.ds(k * rows * width, rows * width), :] = ens[k].astype(F32).reshape(rows * width, ny)
        for i in (0, 1):
            ens_stage[0, i] = ensf[pl.ds(width - 1 - i, members * rows, stride=width), :].astype(BF16)
            ens_stage[1, i] = ensf[pl.ds(i, members * rows, stride=width), :].astype(BF16)

    def send_edges():
        sides = 0.25 * dot3((small[0, 0], small[0, 1]), jnp.concatenate([ctl_halo[0], ctl_halo[1]], axis=1))
        for j in (0, 1):
            a = smooth_y(sides[:, j * ny:(j + 1) * ny]).reshape(members, 1, levels, ny)
            p = ens_stage[1 - j, 0].astype(F32).reshape(members, V, levels, ny) * a
            total = jnp.sum(p, axis=0).reshape(rows, ny)
            for i in range(n_mem):
                edge_src[i, j] = total[i * share:(i + 1) * share]
        for d in peers:
            who = m ^ d
            to_mem(d, edge_src.at[who], edge_main.at[d - 1], edge_send.at[2], edge_recv.at[2]).start()

        def start(side):
            for d in (*peers, 0):
                to_side(
                    side, d, edge_src.at[m ^ d, 1 - side], edge_halo.at[side, d], edge_send.at[side], edge_recv.at[side]
                ).start()

        both_sides(start)

    def add_edges():
        recv_sides((OBS,))
        wait_all(edge_main, edge_recv.at[2])
        for side in (0, 1):
            @pl.when(has[side])
            def _():
                wait_all(edge_halo.at[side], edge_recv.at[side])
        reach = reach_of(0)
        for j, x, out in ((0, 0, -1), (1, width - 1, width)):
            v = edge_src[m, j]
            for d in range(n_mem - 1):
                v = v + edge_main[d, j]
            at = pl.ds((reach + x) * share, share)
            inc0[at, :] = inc0[at, :] + v
            v = edge_halo[j, 0]
            for d in range(1, n_mem):
                v = v + edge_halo[j, d]
            at = pl.ds((reach + out) * share, share)
            inc0[at, :] = inc0[at, :] + v

    def halo_cells(side):
        return jnp.concatenate([surf_halo[side, pl.ds(2 * HALO + c, 1)] for c in range(cuts)], axis=1).astype(I32)

    def coefficients():
        code = jnp.concatenate(
            [surf_halo[0, pl.ds(HALO, HALO)], codes[...].astype(F32), surf_halo[1, pl.ds(HALO, HALO)]], axis=0
        )
        speed = jnp.concatenate([surf_halo[0, pl.ds(0, HALO)], wind[...], surf_halo[1, pl.ds(0, HALO)]], axis=0)
        opened = (code != 1.0).astype(F32)
        absorb = jnp.where(code == 2.0, absorbing, 1.0).astype(F32)
        yy = iota(code.shape, 1)
        west = lambda v: pltpu.roll(v, 1, 0)
        east = lambda v: pltpu.roll(v, n - 1, 0)
        south = lambda v: pltpu.roll(v, 1, 1)
        north = lambda v: pltpu.roll(v, ny - 1, 1)
        oe = opened * east(opened)
        ow = opened * west(opened)
        on = jnp.where(yy < ny - 1, opened * north(opened), 0.0)
        os = jnp.where(yy > 0, opened * south(opened), 0.0)
        k = diffusion_rate
        center = 1.0 - k * (oe + ow + on + os) - speed * oe
        every = (
            absorb * center, absorb * (k + west(speed)) * ow, absorb * k * oe, absorb * k * os, absorb * k * on,
            center * absorb, k * ow * west(absorb), (k + speed) * oe * east(absorb),
            k * os * south(absorb), k * on * north(absorb),
        )
        for i, v in enumerate(every):
            coef[i] = jnp.broadcast_to(v[:, None, :], (n, share, ny))

    def stencil(q, first, which):
        count = q.shape[0] - 2
        c = lambda i: coef[which + i, pl.ds(HALO + first + 1, count)]
        mid = q[1:-1]
        turn = lambda by: pltpu.roll(mid.reshape(count * share, ny), by, 1).reshape(count, share, ny)
        return c(0) * mid + c(1) * q[:-2] + c(2) * q[2:] + c(3) * turn(1) + c(4) * turn(ny - 1)

    def observe(state, reach):
        tiles = (
            (halo_cells(0), obs_halo[0, 0], obs_halo[0, 1], 0, reach, width - reach),
            (cell[...], obs[0], obs[1], reach, width, 0),
            (halo_cells(1), obs_halo[1, 0], obs_halo[1, 1], reach + width, reach, 0),
        )
        pieces = []
        for i, (where, seen, dev, at, count, offset) in enumerate(tiles):
            hot_y = hot[i]
            place = jnp.broadcast_to(where >> ys, (share, nobs))
            hit = place[None] == iota((count, share, nobs), 0) + offset
            hi, low = split(state[at:at + count].reshape(count * share, ny))
            got = mm(jnp.concatenate([hi, low], axis=1), jnp.concatenate([hot_y, hot_y], axis=0))
            sampled = jnp.sum(jnp.where(hit, got.reshape(count, share, nobs), 0.0), axis=0)
            scaled = (sampled - seen) / dev
            weight = jnp.clip(scaled, -huber_delta, huber_delta) / dev
            put = [
                jnp.where(hit, w.astype(F32)[None], 0.0).reshape(count * share, nobs).astype(BF16)
                for w in split(weight)
            ]
            total = lax.dot_general(
                jnp.concatenate(put, axis=1), jnp.concatenate([hot_y, hot_y], axis=1), NT, preferred_element_type=F32
            )
            pieces.append(total.reshape(count, share, ny))
        return jnp.concatenate(pieces, axis=0)

    exchange = ((stage0, src0, main0, halo0, inc0), (stage1, src1, main1, halo1, inc1))

    def members_sum(e):
        stage, src, main, halo, _ = exchange[e]
        reach = reach_of(e)
        data, hb, mb = blocks_of(e, share, width)
        copies = []
        for d in (*peers, 0):
            who = m ^ d
            r0 = who * share
            l0 = lax.rem(r0, levels)
            total = jnp.zeros((share, width, ny), F32)
            for k in range(members):
                a = work[pl.ds(pl.multiple_of(k * block + l0 * width, width), share * width), :]
                total += ens[k, pl.ds(r0, share)].astype(F32) * a.reshape(share, width, ny)
            tot[d] = total.reshape(inner_rows, ny)
            ex = exponent([total], ny)
            scale = jnp.exp2(-ex) * SPAN
            for x in range(width):
                v = tot[d, pl.ds(x, share, stride=width), :]
                if d == 0:
                    own[pl.ds(x * share, share), :] = v
                at = x * share
                if x >= reach:
                    at += hb - data
                if x >= width - reach:
                    at += mb - (width - 2 * reach) * share
                stage[d, pl.ds(at, share), :] = jnp.round(v * scale)
            for at in (data, hb + mb + data):
                stage[d, pl.ds(at, hb - data), :] = jnp.broadcast_to(ex, (hb - data, ny))
            used = (width - 2 * reach) * share
            if used < mb:
                stage[d, pl.ds(hb + used, mb - used), :] = jnp.zeros((mb - used, ny), F32)
            src[d] = stage[d].astype(I32).astype(I16)
            if d:
                copy = to_mem(d, src.at[d], main.at[d - 1], rs_send.at[e, 2], rs_recv.at[e, 2])
                copy.start()

        def start(side):
            at = pl.multiple_of((1 - side) * (hb + mb), PACK)
            for d in (*peers, 0):
                to_side(
                    side, d, src.at[d, pl.ds(at, hb)], halo.at[side, d], rs_send.at[e, side], rs_recv.at[e, side]
                ).start()

        both_sides(start)

    def gather_sum(e):
        _, _, main, halo, inc = exchange[e]
        data, hb, mb = blocks_of(e, share, width)
        used = width * share - 2 * data
        wait_all(main, rs_recv.at[e, 2])
        for side in (0, 1):
            @pl.when(has[side])
            def _():
                wait_all(halo.at[side], rs_recv.at[e, side])
        pieces = [own[pl.ds(0, data), :], own[pl.ds(data, used), :], own[pl.ds(data + used, data), :]]
        for d in range(n_mem - 1):
            first = whole_number(main[d, pl.ds(0, hb)])
            u = jnp.exp2(first[data:data + 1]) * (1.0 / SPAN)
            pieces[0] = pieces[0] + (first * u)[:data]
            pieces[1] = pieces[1] + (whole_number(main[d, pl.ds(hb, mb)]) * u)[:used]
            pieces[2] = pieces[2] + (whole_number(main[d, pl.ds(hb + mb, hb)]) * u)[:data]
        outer = []
        for side in (0, 1):
            total = None
            for d in range(n_mem):
                v = whole_number(halo[side, d])
                v = v * (jnp.exp2(v[data:data + 1]) * (1.0 / SPAN))
                total = v if total is None else total + v
            outer.append(total[:data])
        at = 0
        for v in (outer[0], *pieces, outer[1]):
            inc[pl.ds(at, v.shape[0]), :] = v
            at += v.shape[0]

    def observation_term(e, field):
        ag = (ag0, ag1)[e]
        reach = reach_of(e)
        margin = ag.shape[1] - inner_rows - PACK
        q = field.reshape(width + 2 * reach, share, ny)
        for i in range(STEPS):
            q = stencil(q, i - reach, 0)
        with mark("observe"):
            q = observe(q, reach - STEPS)
        for i in range(STEPS):
            q = stencil(q, i + STEPS - reach, 5)
        spare = reach - 2 * STEPS
        lines = [spare - 1, spare + width] + ([spare - 2, spare + width + 1] if spare > 1 else [])
        if margin > len(lines) * share:
            fringe[...] = jnp.zeros_like(fringe)
        for i, x in enumerate(lines):
            fringe[pl.ds(i * share, share), :] = q[x]
        for x in range(width):
            flat[pl.ds(x, share, stride=width), :] = q[spare + x]
        ex = exponent([q], ny)
        ag[m, pl.ds(0, inner_rows)] = encode(flat[...], ex)
        ag[m, pl.ds(inner_rows, margin)] = encode(fringe[pl.ds(0, margin), :], ex)
        ag[m, pl.ds(inner_rows + margin, PACK)] = jnp.broadcast_to(ex, (PACK, ny)).astype(I32).astype(I16)
        for d in peers:
            to_mem(d, ag.at[m], ag.at[m], ag_send.at[e], ag_recv.at[e]).start()

    def adjoint_rows(e):
        ag = (ag0, ag1)[e]
        margin = ag.shape[1] - inner_rows - PACK
        for i in range(n_mem):
            u = unit(ag[i, pl.ds(inner_rows + margin, PACK)])
            adj_out[pl.ds(i * inner_rows, inner_rows), :] = whole_number(ag[i, pl.ds(0, inner_rows)]) * u
            fringes[i, pl.ds(0, margin)] = whole_number(ag[i, pl.ds(inner_rows, margin)]) * u
            for j in range(4 - 2 * e):
                marks_all[j, pl.ds(i * share, share), :] = fringes[i, pl.ds(j * share, share), :]
        terms = []
        for j in range(4 - 2 * e):
            p = ens_halo[j % 2, j // 2].astype(F32).reshape(members, rows, ny) * marks_all[j][None]
            terms.append((p[:, :levels] + p[:, levels:]).reshape(kl, ny))
        return terms

    with mark("part0"):
        members_sum(0)
    with mark("member_edges"):
        member_edges()
    with mark("w_ctlhalo"):
        recv_sides((CTL,))
    with mark("edges"):
        send_edges()
    with mark("hidden"):
        start_sides((OBS, ENS))
        pick = (lev((block, levels), 0, xs) == iota((block, levels), 1)).astype(F32)
        pick2 = ((iota((kl, levels), 0) & (levels - 1)) == iota((kl, levels), 1)).astype(F32)
        both = nt(lo, lo)
        far_x = gap((block, block), width - 1)
        far_x = jnp.where(far_x == 0, 0.375, jnp.where(far_x == 1, 0.25, jnp.where(far_x == 2, 0.0625, 0.0)))
        xr, xc = iota((block, block), 0) & (width - 1), iota((block, block), 1) & (width - 1)
        for side, x in ((0, 0), (1, width - 1)):
            lost = jnp.where(has[side], 0.0, 0.0625).astype(F32)
            far_x = far_x - jnp.where((xr == x) & (xc == x), lost, 0.0)
        full = nt(jnp.dot(pick, both, precision=HIGHEST, preferred_element_type=F32), pick) * far_x
        for j, piece in enumerate(split(full)):
            mats[1, j] = piece
        full = nt(jnp.dot(pick2, both, precision=HIGHEST, preferred_element_type=F32), pick2) * same_k
        for j, piece in enumerate(split(full)):
            small[1, j] = piece
        for j, piece in enumerate(split(nt(nt(pick, lo), pick) * near_x)):
            mats_out[j] = piece
        for j, piece in enumerate(split(nt(nt(pick2, lo), pick2) * same_k)):
            small_out[j] = piece
        yr, yc = iota((2 * ny, 2 * ny), 0), iota((2 * ny, 2 * ny), 1)
        far_y = jnp.abs(yr - yc)
        corner = (yr & (ny - 1) == 0) | (yr & (ny - 1) == ny - 1)
        far_y = jnp.where(
            far_y == 0, jnp.where(corner, 0.3125, 0.375),
            jnp.where(far_y == 1, 0.25, jnp.where(far_y == 2, 0.0625, 0.0)),
        )
        blur2[...] = jnp.where((yr >> ys) == (yc >> ys), far_y, 0.0).astype(BF16)
        recv_sides((SURF,))
        for i, where in enumerate((halo_cells(0), cell[...], halo_cells(1))):
            hot[i] = (iota((ny, nobs), 0) == (where & (ny - 1))).astype(BF16)
        coefficients()
    with mark("w_rs0"):
        gather_sum(0)
    with mark("w_edge"):
        add_edges()
    with mark("obs0"):
        observation_term(0, inc0[...])
    with mark("w_ag0"):
        wait_all(ag0.at[pl.ds(0, n_mem - 1)], ag_recv.at[0])
        recv_sides((ENS,))
    with mark("mix1"):
        terms = adjoint_rows(0)
        big = (mats[1, 0], mats[1, 1])

        def blur(v):
            hi, low = split(v)
            return mm(jnp.concatenate([hi, low], axis=1), jnp.concatenate([blur2[...], blur2[...]], axis=0))

        for k in range(0, members, 2):
            wide[k // 2] = dot3(
                big, jnp.concatenate([member_term(ensf, adj_out, block, k + i) for i in (0, 1)], axis=1)
            )
        for k in range(0, members, 2):
            done = blur(wide[k // 2])
            work[k * block:(k + 1) * block, :] = done[:, :ny]
            work[(k + 1) * block:(k + 2) * block, :] = done[:, ny:]
        tiny = (small[1, 0], small[1, 1])
        close = dot3(tiny, jnp.concatenate(terms[:2], axis=1))
        distant = blur(0.25 * close + 0.0625 * dot3(tiny, jnp.concatenate(terms[2:], axis=1)))
        close = blur(0.0625 * close)
        for side, first, second in ((0, 0, 1), (1, width - 1, width - 2)):
            for x, v in ((first, distant), (second, close)):
                at = pl.ds(x, kl, stride=width)
                work[at, :] = work[at, :] + v[:, side * ny:(side + 1) * ny]
    with mark("part1"):
        members_sum(1)
    with mark("w_rs1"):
        gather_sum(1)
    with mark("obs1"):
        observation_term(1, step_length * (inc0[pl.ds(share, inc1.shape[0]), :] - inc1[...]))
    with mark("w_ag1"):
        wait_all(ag1.at[pl.ds(0, n_mem - 1)], ag_recv.at[1])
    with mark("term1"):
        terms = adjoint_rows(1)
        for side in (0, 1):
            edges_out[:, side * ny:(side + 1) * ny] = terms[side]
    with mark("drain"):
        for e in (0, 1):
            _, _, main, halo, _ = exchange[e]
            wait_all(main, rs_send.at[e, 2])
            if e == 0:
                wait_all(edge_main, edge_send.at[2])
            wait_all((ag0, ag1)[e].at[pl.ds(0, n_mem - 1)], ag_send.at[e])
            for side in (0, 1):
                @pl.when(has[1 - side])
                def _():
                    wait_all(halo.at[side], rs_send.at[e, side])
                    if e == 0:
                        wait_all(edge_halo.at[side], edge_send.at[side])
        for side in (0, 1):
            @pl.when(has[1 - side])
            def _():
                for i in (CTL, SURF, OBS, ENS):
                    first_msg(side, i).wait_send()


def member_term(ensf, adj, block, k):
    at = 2 * k * block
    return ensf[pl.ds(at, block), :] * adj[:block] + ensf[pl.ds(at + block, block), :] * adj[block:]


def finish(members, levels, width, ny, ensf, adj, edges, mats, small, out, work, sem):
    block = levels * width
    smooth_y = smoother(ny)
    side = 0.25 * dot3((small[0], small[1]), edges[...])
    sides = [smooth_y(side[:, j * ny:(j + 1) * ny]) for j in (0, 1)]
    big = (mats[0], mats[1])
    for k in range(0, members, 2):
        done = dot3_apart(big, jnp.concatenate([member_term(ensf, adj, block, k + i) for i in (0, 1)], axis=1))
        for i in (0, 1):
            base = (k + i) * block
            work[pl.ds(base, block), :] = smooth_y(done[:, i * ny:(i + 1) * ny])
            for j, x in ((0, 0), (1, width - 1)):
                at = pl.ds(base + x, levels, stride=width)
                work[at, :] = work[at, :] + sides[j][(k + i) * levels:(k + i + 1) * levels]
            at = pl.ds(base, block)
            pltpu.make_async_copy(work.at[at], out.at[at], sem.at[0]).start()
    pltpu.make_async_copy(work, out, sem.at[0]).wait()


def body(n_mem, n_tile, ensemble, control, level_loc, wind_speed, cell_codes, obs_cell, innovation, obs_sigma):
    members, rows, width, ny = ensemble.shape
    levels = control.shape[1]
    assert width >= 2 * HALO and members % 2 == 0 and rows == 2 * levels
    nobs = obs_cell.shape[0]
    share = rows // n_mem
    kl = members * levels
    block = levels * width
    n = width + 2 * HALO
    vmem = pltpu.VMEM
    dma = pltpu.SemaphoreType.DMA
    sizes = [blocks_of(e, share, width) for e in (0, 1)]
    full = [2 * hb + mb for _, hb, mb in sizes]
    margins = [up((4 - 2 * e) * share, PACK) for e in (0, 1)]
    surf = up(2 * HALO + nobs // ny, 8)
    scratch = [
        vmem((members, rows, width, ny), BF16),
        vmem((members * block, ny), F32),
        vmem((levels, levels), F32),
        vmem((width, ny), F32),
        vmem((width, ny), I32),
        vmem((1, nobs), I32),
        vmem((2, share, nobs), F32),
        dma((7 + members // 2,)),
        vmem((3, ny, nobs), BF16),
        vmem((members * block, ny), F32),
        vmem((2, 2, block, block), BF16),
        vmem((2, 2, kl, kl), BF16),
        vmem((2 * ny, 2 * ny), BF16),
        vmem((10, n, share, ny), F32),
        vmem((2, kl, ny), F32),
        vmem((2, kl, ny), F32),
        vmem((2, surf, ny), F32),
        vmem((2, surf, ny), F32),
        vmem((2, 2, share, nobs), F32),
        vmem((2, 2, members * rows, ny), BF16),
        vmem((2, 2, members * rows, ny), BF16),
        vmem((n_mem, share * width, ny), F32),
        vmem((share * width, ny), F32),
        *(vmem((n_mem, full[e], ny), F32) for e in (0, 1)),
        *(vmem((n_mem, full[e], ny), I16) for e in (0, 1)),
        *(vmem((n_mem - 1, full[e], ny), I16) for e in (0, 1)),
        *(vmem((2, n_mem, sizes[e][1], ny), I16) for e in (0, 1)),
        *(vmem((share * width + 2 * sizes[e][0], ny), F32) for e in (0, 1)),
        vmem((share * width, ny), F32),
        vmem((margins[0], ny), F32),
        vmem((n_mem, margins[0], ny), F32),
        vmem((4, rows, ny), F32),
        *(vmem((n_mem, share * width + margins[e] + PACK, ny), I16) for e in (0, 1)),
        vmem((n_mem, 2, share, ny), F32),
        vmem((n_mem - 1, 2, share, ny), F32),
        vmem((2, n_mem, share, ny), F32),
        vmem((members // 2, block, 2 * ny), F32),
        dma((2, 4)), dma((2, 4)),
        dma((2, 3)), dma((2, 3)),
        dma((2,)), dma((2,)),
        dma((3,)), dma((3,)),
    ]
    whole = pl.BlockSpec(memory_space=pltpu.VMEM)
    hbm = pl.BlockSpec(memory_space=pltpu.HBM)
    handed = pl.pallas_call(
        functools.partial(kernel, n_mem, n_tile, members, levels, width, ny, nobs),
        out_shape=(
            vmem((members * rows * width, ny), F32), vmem((rows * width, ny), F32), vmem((kl, 2 * ny), F32),
            vmem((2, block, block), BF16), vmem((2, kl, kl), BF16),
        ),
        in_specs=[hbm] * 8,
        out_specs=(whole,) * 5,
        scratch_shapes=scratch,
        compiler_params=pltpu.CompilerParams(
            collective_id=0, has_side_effects=True, vmem_limit_bytes=40 << 20
        ),
    )(*(pltpu.with_memory_space_constraint(x, pltpu.HBM) for x in (
        ensemble,
        control.reshape(members * block, ny),
        level_loc,
        wind_speed,
        cell_codes,
        obs_cell.reshape(1, nobs),
        innovation.reshape(n_mem, share, nobs),
        obs_sigma.reshape(n_mem, share, nobs),
    )))
    result = pl.pallas_call(
        functools.partial(finish, members, levels, width, ny),
        out_shape=jax.ShapeDtypeStruct((members * block, ny), F32),
        in_specs=[whole] * 5,
        out_specs=hbm,
        scratch_shapes=[vmem((members * block, ny), F32), dma((1,))],
        compiler_params=pltpu.CompilerParams(vmem_limit_bytes=40 << 20),
    )(*(pltpu.with_memory_space_constraint(x, pltpu.VMEM) for x in handed))
    return result.reshape(members, levels, width, ny)


def solution(mesh):
    placed = (
        P("mem", None, "tile", None),
        P("mem", None, "tile", None),
        P(),
        P("tile", None),
        P("tile", None),
        P("tile"),
        P(None, "tile"),
        P(None, "tile"),
    )
    return jax.shard_map(
        functools.partial(body, mesh.shape["mem"], mesh.shape["tile"]),
        mesh=mesh, in_specs=placed, out_specs=P("mem", None, "tile", None), check_vma=False,
    )
```

```python
import contextlib
import functools
import math

import jax
import jax.numpy as jnp
from jax import lax
from jax.experimental import pallas as pl
from jax.experimental.pallas import tpu as pltpu
from jax.sharding import PartitionSpec as P

V = 2
STEPS = 2
HALO = 8
PACK = 16
SPAN = 32760.0

diffusion_rate = 0.12
absorbing = 0.7
step_length = 0.5
huber_delta = 1.0

MESH = pl.DeviceIdType.MESH
F32 = jnp.float32
BF16 = jnp.bfloat16
I16 = jnp.int16
I32 = jnp.int32
HIGHEST = lax.Precision.HIGHEST
NT = (((1,), (1,)), ((), ()))
mark = contextlib.nullcontext


def log2(n):
    assert n & (n - 1) == 0
    return n.bit_length() - 1


def iota(shape, dim):
    return lax.broadcasted_iota(I32, shape, dim)


def split(x):
    hi = x.astype(BF16)
    return hi, (x - hi.astype(F32)).astype(BF16)


def mm(a, b):
    return jnp.dot(a, b, preferred_element_type=F32)


def nt(a, b):
    return lax.dot_general(a, b, NT, precision=HIGHEST, preferred_element_type=F32)


def dot3(a, b):
    ah, al = a
    bh, bl = split(b)
    return mm(jnp.concatenate([ah, ah, al], axis=1), jnp.concatenate([bh, bl, bh], axis=0))


def dot3_apart(a, b):
    ah, al = a
    bh, bl = split(b)
    return mm(ah, bh) + (mm(ah, bl) + mm(al, bh))


def tripled(a, outer):
    pieces = []
    for v in (a, outer):
        hi, low = split(v)
        pieces += [hi, hi, low]
    spare = up(3 * outer.shape[1], 128) - 3 * outer.shape[1]
    if spare:
        pieces.append(jnp.zeros((a.shape[0], spare), BF16))
    return jnp.concatenate(pieces, axis=1)


def mixed(table, b, outer):
    pieces = []
    for v in (b, outer):
        hi, low = split(v)
        pieces += [hi, low, hi]
    spare = up(3 * outer.shape[0], 128) - 3 * outer.shape[0]
    if spare:
        pieces.append(jnp.zeros((spare, b.shape[1]), BF16))
    return mm(table, jnp.concatenate(pieces, axis=0))


def side_by_side(terms, k, levels):
    return jnp.concatenate(
        [jnp.concatenate([v[(k + i) * levels:(k + i + 1) * levels] for v in terms], axis=0) for i in (0, 1)], axis=1
    )


def up(n, to):
    return -(-n // to) * to


def parts_of(share):
    parts = 2 if share % 8 == 0 else 1
    return parts, share // parts


def blocks_of(part, width):
    least = 2 * STEPS + 2
    reach = least if least * part % 8 == 0 else HALO
    data = reach * part
    return reach, data, up(data + 1, PACK), up(width * part - 2 * data, PACK)


def margin_of(e, part):
    return up((4 - 2 * e) * part + 1, PACK)


def wait_all(ref, sem):
    pltpu.make_async_copy(ref, ref, sem).wait()


def smoother(ny):
    yi = iota((1, ny), 1)
    from_south = jnp.where(yi > 0, 0.25, 0.0).astype(F32)
    from_north = jnp.where(yi < ny - 1, 0.25, 0.0).astype(F32)

    def smooth_y(v):
        return 0.5 * v + (from_south * pltpu.roll(v, 1, 1) + from_north * pltpu.roll(v, ny - 1, 1))

    return smooth_y


def exponent(parts, ny):
    most = None
    for p in parts:
        v = jnp.max(jnp.abs(p.reshape(-1, ny)), axis=0, keepdims=True)
        most = v if most is None else jnp.maximum(most, v)
    return jnp.floor(jnp.log2(jnp.maximum(most, 1e-30))) + 1.0


def encode(x, e):
    return jnp.round(x * (jnp.exp2(-e) * SPAN)).astype(I32).astype(I16)


def whole_number(q):
    return q.astype(I32).astype(F32)


def unit(code):
    return jnp.exp2(whole_number(code)[0:1]) * (1.0 / SPAN)


def kernel(
    n_mem, n_tile, members, levels, width, ny, nobs,
    ens_hbm, ctl_hbm, loc_hbm, wind_hbm, codes_hbm, cell_hbm, innov_hbm, sigma_hbm,
    ensf, adj_out, edges_out, mats_out, small_out,
    ens, ctl, loc, wind, codes, cell, obs, in_sem, hot,
    work, mats, small, table1, blur2, coef, thin,
    ctl_stage, ctl_halo, surf_stage, surf_halo, obs_halo, seen, ens_stage, ens_halo,
    tot, stage, rs_src, rs_main, rs_halo, inc,
    turned, fringe, fringes, marks_all, ag0, ag1, edge_src, edge_main, edge_halo, wide,
    sent, r0_recv, rs_recv, ag_recv, edge_recv,
):
    m = lax.axis_index("mem")
    t = lax.axis_index("tile")
    has = (t > 0, t < n_tile - 1)
    rows = V * levels
    share = rows // n_mem
    block = levels * width
    kl = members * levels
    xs, ys = log2(width), log2(ny)
    n = HALO + width + HALO
    parts, sp = parts_of(share)
    reach, data, hb, mb = blocks_of(sp, width)
    across = width + 2 * reach
    copies = max(8 // sp, 1)
    deep = sp * copies
    cuts = nobs // ny
    assert 1 << log2(n_mem) == n_mem
    peers = range(n_mem - 1, 0, -1)
    outward = 1 - (t & 1)
    inner_rows = sp * width

    def tell(dev):
        pl.semaphore_signal(pltpu.get_barrier_semaphore(), inc=1, device_id=dev, device_id_type=MESH)

    for d in peers:
        tell((m ^ d, t))

    @pl.when(has[0])
    def _():
        for d in range(n_mem):
            tell((m ^ d, t - 1))

    @pl.when(has[1])
    def _():
        for d in range(n_mem):
            tell((m ^ d, t + 1))

    loads = [
        pltpu.make_async_copy(src, dst, in_sem.at[i])
        for i, (src, dst) in enumerate((
            (loc_hbm, loc),
            *((ctl_hbm.at[pl.ds(at, 2 * block)], ctl.at[pl.ds(at, 2 * block)]) for at in range(0, members * block, 2 * block)),
            (ens_hbm, ens), (wind_hbm, wind), (codes_hbm, codes),
            (cell_hbm, cell), (innov_hbm.at[m], obs.at[0]), (sigma_hbm.at[m], obs.at[1]),
        ))
    ]
    for load in loads:
        load.start()

    def to_side(side, d, src, dst, ssem, rsem):
        dev = (m ^ d, t + 1 - 2 * side)
        return pltpu.make_async_remote_copy(
            src_ref=src, dst_ref=dst, send_sem=ssem, recv_sem=rsem, device_id=dev, device_id_type=MESH
        )

    def to_mem(d, src, dst, ssem, rsem):
        return pltpu.make_async_remote_copy(
            src_ref=src, dst_ref=dst, send_sem=ssem, recv_sem=rsem,
            device_id=(m ^ d, t), device_id_type=MESH,
        )

    ctl_loads, late_loads = loads[1:1 + members // 2], loads[1 + members // 2:]
    def both_sides(start):
        for s in (outward, 1 - outward):
            dev = t + 1 - 2 * s

            @pl.when((dev >= 0) & (dev < n_tile))
            def _():
                start(s)

    CTL, SURF, OBS, ENS = range(4)
    def first_msg(side, i):
        s, d = (
            (ctl_stage.at[side], ctl_halo.at[side]),
            (surf_stage.at[side], surf_halo.at[side]),
            (obs, obs_halo.at[side]),
            (ens_stage.at[side], ens_halo.at[side]),
        )[i]
        return to_side(side, 0, s, d, sent.at[side], r0_recv.at[side, i])

    def start_sides(which):
        def start(side):
            for i in which:
                first_msg(side, i).start()

        both_sides(start)

    def recv_sides(which):
        for side in (0, 1):
            @pl.when(has[side])
            def _():
                for i in which:
                    first_msg(side, i).wait_recv()

    for side in (0, 1):
        @pl.when(jnp.logical_not(has[side]))
        def _():
            ctl_halo[side] = jnp.zeros_like(ctl_halo[side])
            surf_halo[side, pl.ds(0, HALO)] = jnp.zeros((HALO, ny), F32)
            surf_halo[side, pl.ds(HALO, HALO)] = jnp.ones((HALO, ny), F32)
            surf_halo[side, pl.ds(2 * HALO, cuts)] = jnp.full((cuts, ny), -1.0, F32)
            obs_halo[side, 0] = jnp.zeros((share, nobs), F32)
            obs_halo[side, 1] = jnp.ones((share, nobs), F32)
            ens_halo[side] = jnp.zeros_like(ens_halo[side])
            edge_halo[side] = jnp.zeros_like(edge_halo[side])
            for e in (0, 1):
                for p in range(parts):
                    rs_halo[e, p, side] = jnp.zeros_like(rs_halo[e, p, side])

    smooth_y = smoother(ny)
    gap = lambda shape, mask: jnp.abs((iota(shape, 0) & mask) - (iota(shape, 1) & mask))
    lev = lambda shape, dim, shift: iota(shape, dim) >> shift

    with mark("w_loc"):
        loads[0].wait()
    with mark("mats0"):
        lo = loc[...]
        spread = (lev((levels, block), 1, xs) == iota((levels, block), 0)).astype(BF16)
        repeat = ((iota((levels, kl), 1) & (levels - 1)) == iota((levels, kl), 0)).astype(BF16)
        near_x = gap((block, block), width - 1)
        near_x = jnp.where(near_x == 0, 0.5, jnp.where(near_x == 1, 0.25, 0.0)).astype(F32)
        same_k = (lev((kl, kl), 0, log2(levels)) == lev((kl, kl), 1, log2(levels))).astype(F32)
        for j, piece in enumerate(split(lo)):
            p = piece.astype(F32)
            tall = jnp.broadcast_to(p[:, None, :], (levels, width, levels)).reshape(block, levels)
            mats[0, j] = (mm(tall.astype(BF16), spread) * near_x).astype(BF16)
            tall = jnp.concatenate([p] * members, axis=0)
            small[0, j] = (mm(tall.astype(BF16), repeat) * same_k).astype(BF16)

    def mix_pair(k):
        both = jnp.concatenate(
            [ctl[k * block:(k + 1) * block, :], ctl[(k + 1) * block:(k + 2) * block, :]], axis=1
        )
        wide[k // 2] = dot3((mats[0, 0], mats[0, 1]), both)

    with mark("mix_first"):
        ctl_loads[0].wait()
        mix_pair(0)
    with mark("w_ctl"):
        for load in ctl_loads[1:]:
            load.wait()
    ctl_stage[0] = ctl[pl.ds(width - 1, kl, stride=width), :]
    ctl_stage[1] = ctl[pl.ds(0, kl, stride=width), :]

    with mark("w_barrier"):
        count = n_mem - 1 + n_mem * (jnp.where(t > 0, 1, 0) + jnp.where(t < n_tile - 1, 1, 0))
        pl.semaphore_wait(pltpu.get_barrier_semaphore(), count)

    start_sides((CTL,))

    with mark("mix_a0"):
        for k in range(2, members, 2):
            mix_pair(k)
        for k in range(members):
            work[pl.ds(k * block, block), :] = smooth_y(wide[k // 2, :, (k % 2) * ny:(k % 2 + 1) * ny])

    with mark("stage"):
        for load in late_loads:
            load.wait()
        for side, at in ((0, pl.ds(width - HALO, HALO)), (1, pl.ds(0, HALO))):
            surf_stage[side, pl.ds(0, HALO)] = wind[at, :]
            surf_stage[side, pl.ds(HALO, HALO)] = codes[at, :].astype(F32)
            for c in range(cuts):
                surf_stage[side, pl.ds(2 * HALO + c, 1)] = cell[:, c * ny:(c + 1) * ny].astype(F32)
        start_sides((SURF, OBS))

    def member_edges():
        for k in range(members):
            ensf[pl.ds(k * rows * width, rows * width), :] = ens[k].astype(F32).reshape(rows * width, ny)
        for i in (0, 1):
            ens_stage[0, i] = ensf[pl.ds(width - 1 - i, members * rows, stride=width), :].astype(BF16)
            ens_stage[1, i] = ensf[pl.ds(i, members * rows, stride=width), :].astype(BF16)

    def send_edges():
        sides = 0.25 * dot3((small[0, 0], small[0, 1]), jnp.concatenate([ctl_halo[0], ctl_halo[1]], axis=1))
        for j in (0, 1):
            a = smooth_y(sides[:, j * ny:(j + 1) * ny]).reshape(members, 1, levels, ny)
            p = ens_stage[1 - j, 0].astype(F32).reshape(members, V, levels, ny) * a
            total = jnp.sum(p, axis=0).reshape(rows, ny)
            for i in range(n_mem):
                edge_src[i, j] = total[i * share:(i + 1) * share]
        for d in peers:
            who = m ^ d
            to_mem(d, edge_src.at[who], edge_main.at[d - 1], sent.at[2], edge_recv.at[2]).start()

        def start(side):
            for d in (*peers, 0):
                to_side(
                    side, d, edge_src.at[m ^ d, 1 - side], edge_halo.at[side, d], sent.at[side], edge_recv.at[side]
                ).start()

        both_sides(start)

    def wait_edges():
        wait_all(edge_main, edge_recv.at[2])
        for side in (0, 1):
            @pl.when(has[side])
            def _():
                wait_all(edge_halo.at[side], edge_recv.at[side])

    def add_edges(p):
        rows_of = pl.ds(p * sp, sp)
        for j, x, out in ((0, 0, -1), (1, width - 1, width)):
            v = edge_src[m, j, rows_of]
            for d in range(n_mem - 1):
                v = v + edge_main[d, j, rows_of]
            at = pl.ds((reach + x) * sp, sp)
            inc[0, p, at] = inc[0, p, at] + v
            v = edge_halo[j, 0, rows_of]
            for d in range(1, n_mem):
                v = v + edge_halo[j, d, rows_of]
            at = pl.ds((reach + out) * sp, sp)
            inc[0, p, at] = inc[0, p, at] + v

    def halo_cells(side):
        return jnp.concatenate([surf_halo[side, pl.ds(2 * HALO + c, 1)] for c in range(cuts)], axis=1).astype(I32)

    def coefficients():
        code = jnp.concatenate(
            [surf_halo[0, pl.ds(HALO, HALO)], codes[...].astype(F32), surf_halo[1, pl.ds(HALO, HALO)]], axis=0
        )
        speed = jnp.concatenate([surf_halo[0, pl.ds(0, HALO)], wind[...], surf_halo[1, pl.ds(0, HALO)]], axis=0)
        opened = (code != 1.0).astype(F32)
        absorb = jnp.where(code == 2.0, absorbing, 1.0).astype(F32)
        yy = iota(code.shape, 1)
        west = lambda v: pltpu.roll(v, 1, 0)
        east = lambda v: pltpu.roll(v, n - 1, 0)
        south = lambda v: pltpu.roll(v, 1, 1)
        north = lambda v: pltpu.roll(v, ny - 1, 1)
        oe = opened * east(opened)
        ow = opened * west(opened)
        on = jnp.where(yy < ny - 1, opened * north(opened), 0.0)
        os = jnp.where(yy > 0, opened * south(opened), 0.0)
        k = diffusion_rate
        center = 1.0 - k * (oe + ow + on + os) - speed * oe
        every = (
            absorb * center, absorb * (k + west(speed)) * ow, absorb * k * oe, absorb * k * os, absorb * k * on,
            center * absorb, k * ow * west(absorb), (k + speed) * oe * east(absorb),
            k * os * south(absorb), k * on * north(absorb),
        )
        for i, v in enumerate(every):
            thin[i] = v
            for r in range(sp):
                coef[i, pl.ds(r, across, stride=sp), :] = thin[i, pl.ds(HALO - reach, across), :]

    def stencil(q, which):
        size = across * sp
        return (
            coef[which] * q
            + coef[which + 1] * pltpu.roll(q, sp, 0)
            + coef[which + 2] * pltpu.roll(q, size - sp, 0)
            + coef[which + 3] * pltpu.roll(q, 1, 1)
            + coef[which + 4] * pltpu.roll(q, ny - 1, 1)
        )

    def copy_seen(i, values):
        for p in range(parts):
            for c in range(copies):
                at = pl.ds(c * sp, sp)
                seen[i, p, 0, at] = values[0, pl.ds(p * sp, sp), :]
                seen[i, p, 1, at] = 1.0 / values[1, pl.ds(p * sp, sp), :]

    def observe(state, p):
        tiles = (
            (halo_cells(0), 0, reach, width - reach),
            (cell[...], reach, width, 0),
            (halo_cells(1), reach + width, reach, 0),
        )
        pieces = []
        for i, (where, at, count, offset) in enumerate(tiles):
            hot_y = hot[i]
            lines = count * sp
            shape = (lines // deep, deep, nobs)
            place = jnp.broadcast_to(where >> ys, (deep, nobs)) - offset
            hit = place[None] == ((iota(shape, 0) * deep + iota(shape, 1)) >> log2(sp))
            hi, low = split(state[at * sp:at * sp + lines])
            got = mm(jnp.concatenate([hi, low], axis=0), hot_y)
            some = jnp.sum(jnp.where(hit, (got[:lines] + got[lines:]).reshape(shape), 0.0), axis=0)
            sampled = some
            for c in range(1, copies):
                sampled = sampled + pltpu.roll(some, c * sp, 0)
            weight = jnp.clip((sampled - seen[i, p, 0]) * seen[i, p, 1], -huber_delta, huber_delta) * seen[i, p, 1]
            put = [
                jnp.where(hit, w.astype(F32)[None], 0.0).reshape(lines, nobs).astype(BF16) for w in split(weight)
            ]
            both = lax.dot_general(jnp.concatenate(put, axis=0), hot_y, NT, preferred_element_type=F32)
            pieces.append(both[:lines] + both[lines:])
        return jnp.concatenate(pieces, axis=0)

    def short(x):
        return x.astype(I32).astype(I16)

    def members_sum(e):
        for p in range(parts):
            for d in (*peers, 0):
                who = m ^ d
                r0 = who * share + p * sp
                l0 = lax.rem(r0, levels)
                total = jnp.zeros((sp, width, ny), F32)
                for k in range(members):
                    a = work[pl.ds(pl.multiple_of(k * block + l0 * width, width), sp * width), :]
                    total += ens[k, pl.ds(r0, sp)].astype(F32) * a.reshape(sp, width, ny)
                tot[p, d] = total.reshape(inner_rows, ny)
                ex = exponent([total], ny)
                scale = jnp.exp2(-ex) * SPAN
                for x in range(width):
                    stage[p, d, pl.ds(x * sp, sp), :] = tot[p, d, pl.ds(x, sp, stride=width), :]
                filler = jnp.broadcast_to(ex, (hb - data, ny))
                for first, at in ((0, 0), (inner_rows - data, hb + mb)):
                    v = jnp.round(stage[p, d, pl.ds(first, data), :] * scale)
                    rs_src[e, p, d, pl.ds(at, hb)] = short(jnp.concatenate([v, filler], axis=0))
                if mb:
                    rs_src[e, p, d, pl.ds(hb, mb)] = short(jnp.round(stage[p, d, pl.ds(data, mb), :] * scale))
            for d in peers:
                to_mem(d, rs_src.at[e, p, d], rs_main.at[e, p, d - 1], sent.at[2], rs_recv.at[e, p, 2]).start()

            def start(side):
                at = pl.multiple_of((1 - side) * (hb + mb), PACK)
                for d in (*peers, 0):
                    to_side(
                        side, d, rs_src.at[e, p, d, pl.ds(at, hb)], rs_halo.at[e, p, side, d],
                        sent.at[side], rs_recv.at[e, p, side],
                    ).start()

            both_sides(start)

    def gather_sum(e, p):
        wait_all(rs_main.at[e, p], rs_recv.at[e, p, 2])
        for side in (0, 1):
            @pl.when(has[side])
            def _():
                wait_all(rs_halo.at[e, p, side], rs_recv.at[e, p, side])
        bounds = ((0, data, 0, hb), (data, mb, hb, mb), (inner_rows - data, data, hb + mb, hb))
        pieces = [stage[p, 0, pl.ds(at, count), :] if count else None for at, count, _, _ in bounds]
        for d in range(n_mem - 1):
            u = None
            for i, (_, count, at, size) in enumerate(bounds):
                if count:
                    v = whole_number(rs_main[e, p, d, pl.ds(at, size)])
                    u = jnp.exp2(v[data:data + 1]) * (1.0 / SPAN) if u is None else u
                    pieces[i] = pieces[i] + (v * u)[:count]
        outer = []
        for side in (0, 1):
            total = None
            for d in range(n_mem):
                v = whole_number(rs_halo[e, p, side, d])
                v = v * (jnp.exp2(v[data:data + 1]) * (1.0 / SPAN))
                total = v if total is None else total + v
            outer.append(total[:data])
        at = 0
        for v in (outer[0], *pieces, outer[1]):
            if v is not None:
                inc[e, p, pl.ds(at, v.shape[0])] = v
                at += v.shape[0]

    def observation_term(e, some, fields):
        ag = (ag0, ag1)[e]
        margin = margin_of(e, sp)
        for i in range(STEPS):
            fields = [stencil(q, 0) for q in fields]
        with mark("observe"):
            fields = [observe(q, p) for p, q in zip(some, fields)]
        for i in range(STEPS):
            fields = [stencil(q, 5) for q in fields]
        lines = (-1, width) + ((-2, width + 1) if e == 0 else ())
        used = len(lines) * sp
        for p, q in zip(some, fields):
            turned[p] = q
            ex = exponent([turned[p, pl.ds((reach - 2) * sp, (width + 4) * sp), :]], ny)
            scale = jnp.exp2(-ex) * SPAN
            for i, x in enumerate(lines):
                fringe[p, pl.ds(i * sp, sp), :] = jnp.round(turned[p, pl.ds((reach + x) * sp, sp), :] * scale)
            fringe[p, pl.ds(used, margin - used), :] = jnp.broadcast_to(ex, (margin - used, ny))
            for r in range(sp):
                v = turned[p, pl.ds(reach * sp + r, width, stride=sp), :]
                ag[p, m, pl.ds(r * width, width)] = short(jnp.round(v * scale))
            ag[p, m, pl.ds(inner_rows, margin)] = short(fringe[p, pl.ds(0, margin), :])
        for p in some:
            for d in peers:
                to_mem(d, ag.at[p, m], ag.at[p, m], sent.at[2], ag_recv.at[e, p]).start()

    def adjoint_rows(e):
        ag = (ag0, ag1)[e]
        margin = margin_of(e, sp)
        for p in range(parts):
            wait_all(ag.at[p, pl.ds(0, n_mem - 1)], ag_recv.at[e, p])
            for i in range(n_mem):
                v = whole_number(ag[p, i, pl.ds(inner_rows, margin)])
                u = jnp.exp2(v[margin - 1:margin]) * (1.0 / SPAN)
                at = i * share + p * sp
                adj_out[pl.ds(at * width, inner_rows), :] = whole_number(ag[p, i, pl.ds(0, inner_rows)]) * u
                fringes[p, i, pl.ds(0, margin)] = v * u
                for j in range(4 - 2 * e):
                    marks_all[j, pl.ds(at, sp), :] = fringes[p, i, pl.ds(j * sp, sp), :]
        terms = []
        for j in range(4 - 2 * e):
            v = ens_halo[j % 2, j // 2].astype(F32).reshape(members, rows, ny) * marks_all[j][None]
            terms.append((v[:, :levels] + v[:, levels:]).reshape(kl, ny))
        return terms

    with mark("part0"):
        members_sum(0)
    with mark("member_edges"):
        member_edges()
    with mark("w_ctlhalo"):
        recv_sides((CTL,))
    with mark("edges"):
        send_edges()
    with mark("hidden"):
        pick = (lev((block, levels), 0, xs) == iota((block, levels), 1)).astype(F32)
        pick2 = ((iota((kl, levels), 0) & (levels - 1)) == iota((kl, levels), 1)).astype(F32)
        both = nt(lo, lo)
        far_x = gap((block, block), width - 1)
        far_x = jnp.where(far_x == 0, 0.375, jnp.where(far_x == 1, 0.25, jnp.where(far_x == 2, 0.0625, 0.0)))
        xr, xc = iota((block, block), 0) & (width - 1), iota((block, block), 1) & (width - 1)
        for side, x in ((0, 0), (1, width - 1)):
            lost = jnp.where(has[side], 0.0, 0.0625).astype(F32)
            far_x = far_x - jnp.where((xr == x) & (xc == x), lost, 0.0)
        xi = iota((block, levels), 0) & (width - 1)
        at_x = lambda v, *marks: v * sum(jnp.where(xi == x, c, 0.0).astype(F32) for x, c in marks)
        last = width - 1
        tall = jnp.dot(pick, both, precision=HIGHEST, preferred_element_type=F32)
        table1[...] = tripled(nt(tall, pick) * far_x, jnp.concatenate([
            at_x(tall, (0, 0.25), (1, 0.0625)), at_x(tall, (last, 0.25), (last - 1, 0.0625)),
            at_x(tall, (0, 0.0625)), at_x(tall, (last, 0.0625)),
        ], axis=1))
        for j, piece in enumerate(split(nt(nt(pick, lo), pick) * near_x)):
            mats_out[j] = piece
        for j, piece in enumerate(split(nt(nt(pick2, lo), pick2) * same_k)):
            small_out[j] = piece
        yr, yc = iota((2 * ny, 2 * ny), 0), iota((2 * ny, 2 * ny), 1)
        far_y = jnp.abs(yr - yc)
        corner = (yr & (ny - 1) == 0) | (yr & (ny - 1) == ny - 1)
        far_y = jnp.where(
            far_y == 0, jnp.where(corner, 0.3125, 0.375),
            jnp.where(far_y == 1, 0.25, jnp.where(far_y == 2, 0.0625, 0.0)),
        )
        blur2[...] = jnp.where((yr >> ys) == (yc >> ys), far_y, 0.0).astype(BF16)
        recv_sides((SURF,))
        copy_seen(1, obs)
        for i, where in enumerate((halo_cells(0), cell[...], halo_cells(1))):
            hot[i] = (iota((ny, nobs), 0) == (where & (ny - 1))).astype(BF16)
        coefficients()
        start_sides((ENS,))
    every = range(parts)
    for p in every:
        with mark(f"w_rs0_{p}"):
            gather_sum(0, p)
    with mark("w_obs"):
        recv_sides((OBS,))
        for side in (0, 1):
            copy_seen(2 * side, obs_halo.at[side])
    with mark("w_edge"):
        wait_edges()
        for p in every:
            add_edges(p)
    with mark("obs0"):
        for p in every:
            observation_term(0, [p], [inc[0, p]])
    with mark("w_ens"):
        recv_sides((ENS,))
    with mark("w_ag0"):
        terms = adjoint_rows(0)
    with mark("mix1"):
        def blur(v):
            hi, low = split(v)
            return mm(jnp.concatenate([hi, low], axis=1), jnp.concatenate([blur2[...], blur2[...]], axis=0))

        for k in range(0, members, 2):
            wide[k // 2] = mixed(
                table1[...], jnp.concatenate([member_term(ensf, adj_out, block, k + i) for i in (0, 1)], axis=1),
                side_by_side(terms, k, levels),
            )
        for k in range(0, members, 2):
            done = blur(wide[k // 2])
            work[k * block:(k + 1) * block, :] = done[:, :ny]
            work[(k + 1) * block:(k + 2) * block, :] = done[:, ny:]
    with mark("part1"):
        members_sum(1)
    for p in range(parts):
        with mark(f"w_rs1_{p}"):
            gather_sum(1, p)
        with mark(f"obs1_{p}"):
            observation_term(1, [p], [step_length * (inc[0, p] - inc[1, p])])
    with mark("term1"):
        terms = adjoint_rows(1)
        for side in (0, 1):
            edges_out[:, side * ny:(side + 1) * ny] = terms[side]
    with mark("drain"):
        size = lambda ref: math.prod(ref.shape) * ref.dtype.itemsize
        line = ny * 4
        total = size(rs_main) + size(edge_main) + (n_mem - 1) * (size(ag0) + size(ag1)) // n_mem
        wait_all(ensf.at[pl.ds(0, total // line)], sent.at[2])
        total = sum(size(ref) for ref in (rs_halo, edge_halo, ctl_halo, surf_halo, obs_halo, ens_halo)) // 2
        for side in (0, 1):
            @pl.when(has[1 - side])
            def _():
                wait_all(ensf.at[pl.ds(0, total // line)], sent.at[side])


def member_term(ensf, adj, block, k):
    at = 2 * k * block
    return ensf[pl.ds(at, block), :] * adj[:block] + ensf[pl.ds(at + block, block), :] * adj[block:]


def finish(members, levels, width, ny, ensf, adj, edges, mats, small, out, work, sem):
    block = levels * width
    smooth_y = smoother(ny)
    side = 0.25 * dot3((small[0], small[1]), edges[...])
    sides = [smooth_y(side[:, j * ny:(j + 1) * ny]) for j in (0, 1)]
    big = (mats[0], mats[1])
    for k in range(0, members, 2):
        done = dot3_apart(big, jnp.concatenate([member_term(ensf, adj, block, k + i) for i in (0, 1)], axis=1))
        for i in (0, 1):
            base = (k + i) * block
            work[pl.ds(base, block), :] = smooth_y(done[:, i * ny:(i + 1) * ny])
            for j, x in ((0, 0), (1, width - 1)):
                at = pl.ds(base + x, levels, stride=width)
                work[at, :] = work[at, :] + sides[j][(k + i) * levels:(k + i + 1) * levels]
            at = pl.ds(base, block)
            pltpu.make_async_copy(work.at[at], out.at[at], sem.at[0]).start()
    pltpu.make_async_copy(work, out, sem.at[0]).wait()


def body(n_mem, n_tile, ensemble, control, level_loc, wind_speed, cell_codes, obs_cell, innovation, obs_sigma):
    members, rows, width, ny = ensemble.shape
    levels = control.shape[1]
    assert width >= 2 * HALO and members % 2 == 0 and rows == 2 * levels
    nobs = obs_cell.shape[0]
    share = rows // n_mem
    kl = members * levels
    block = levels * width
    n = width + 2 * HALO
    vmem = pltpu.VMEM
    dma = pltpu.SemaphoreType.DMA
    parts, sp = parts_of(share)
    reach, data, hb, mb = blocks_of(sp, width)
    size = 2 * hb + mb
    tall = max(8, sp)
    margins = [margin_of(e, sp) for e in (0, 1)]
    surf = up(2 * HALO + nobs // ny, 8)
    scratch = [
        vmem((members, rows, width, ny), BF16),
        vmem((members * block, ny), F32),
        vmem((levels, levels), F32),
        vmem((width, ny), F32),
        vmem((width, ny), I32),
        vmem((1, nobs), I32),
        vmem((2, share, nobs), F32),
        dma((7 + members // 2,)),
        vmem((3, ny, nobs), BF16),
        vmem((members * block, ny), F32),
        vmem((1, 2, block, block), BF16),
        vmem((1, 2, kl, kl), BF16),
        vmem((block, 3 * block + up(12 * levels, 128)), BF16),
        vmem((2 * ny, 2 * ny), BF16),
        vmem((10, (width + 2 * reach) * sp, ny), F32),
        vmem((10, n, ny), F32),
        vmem((2, kl, ny), F32),
        vmem((2, kl, ny), F32),
        vmem((2, surf, ny), F32),
        vmem((2, surf, ny), F32),
        vmem((2, 2, share, nobs), F32),
        vmem((3, parts, 2, tall, nobs), F32),
        vmem((2, 2, members * rows, ny), BF16),
        vmem((2, 2, members * rows, ny), BF16),
        vmem((parts, n_mem, sp * width, ny), F32),
        vmem((parts, n_mem, sp * width, ny), F32),
        vmem((2, parts, n_mem, size, ny), I16),
        vmem((2, parts, n_mem - 1, size, ny), I16),
        vmem((2, parts, 2, n_mem, hb, ny), I16),
        vmem((2, parts, (width + 2 * reach) * sp, ny), F32),
        vmem((parts, (width + 2 * reach) * sp, ny), F32),
        vmem((parts, margins[0], ny), F32),
        vmem((parts, n_mem, margins[0], ny), F32),
        vmem((4, rows, ny), F32),
        *(vmem((parts, n_mem, sp * width + margins[e], ny), I16) for e in (0, 1)),
        vmem((n_mem, 2, share, ny), F32),
        vmem((n_mem - 1, 2, share, ny), F32),
        vmem((2, n_mem, share, ny), F32),
        vmem((members // 2, block, 2 * ny), F32),
        dma((3,)), dma((2, 4)), dma((2, parts, 3)), dma((2, parts)), dma((3,)),
    ]
    whole = pl.BlockSpec(memory_space=pltpu.VMEM)
    hbm = pl.BlockSpec(memory_space=pltpu.HBM)
    handed = pl.pallas_call(
        functools.partial(kernel, n_mem, n_tile, members, levels, width, ny, nobs),
        out_shape=(
            vmem((members * rows * width, ny), F32), vmem((rows * width, ny), F32), vmem((kl, 2 * ny), F32),
            vmem((2, block, block), BF16), vmem((2, kl, kl), BF16),
        ),
        in_specs=[hbm] * 8,
        out_specs=(whole,) * 5,
        scratch_shapes=scratch,
        compiler_params=pltpu.CompilerParams(
            collective_id=0, has_side_effects=True, vmem_limit_bytes=40 << 20
        ),
    )(*(pltpu.with_memory_space_constraint(x, pltpu.HBM) for x in (
        ensemble,
        control.reshape(members * block, ny),
        level_loc,
        wind_speed,
        cell_codes,
        obs_cell.reshape(1, nobs),
        innovation.reshape(n_mem, share, nobs),
        obs_sigma.reshape(n_mem, share, nobs),
    )))
    result = pl.pallas_call(
        functools.partial(finish, members, levels, width, ny),
        out_shape=jax.ShapeDtypeStruct((members * block, ny), F32),
        in_specs=[whole] * 5,
        out_specs=hbm,
        scratch_shapes=[vmem((members * block, ny), F32), dma((1,))],
        compiler_params=pltpu.CompilerParams(vmem_limit_bytes=40 << 20),
    )(*(pltpu.with_memory_space_constraint(x, pltpu.VMEM) for x in handed))
    return result.reshape(members, levels, width, ny)


def solution(mesh):
    placed = (
        P("mem", None, "tile", None),
        P("mem", None, "tile", None),
        P(),
        P("tile", None),
        P("tile", None),
        P("tile"),
        P(None, "tile"),
        P(None, "tile"),
    )
    return jax.shard_map(
        functools.partial(body, mesh.shape["mem"], mesh.shape["tile"]),
        mesh=mesh, in_specs=placed, out_specs=P("mem", None, "tile", None), check_vma=False,
    )
```

```python
import contextlib
import functools
import math

import jax
import jax.numpy as jnp
from jax import lax
from jax.experimental import pallas as pl
from jax.experimental.pallas import tpu as pltpu
from jax.sharding import PartitionSpec as P

V = 2
STEPS = 2
HALO = 8
PACK = 16
SPAN = 32760.0

diffusion_rate = 0.12
absorbing = 0.7
step_length = 0.5
huber_delta = 1.0

MESH = pl.DeviceIdType.MESH
F32 = jnp.float32
BF16 = jnp.bfloat16
I16 = jnp.int16
I32 = jnp.int32
HIGHEST = lax.Precision.HIGHEST
NT = (((1,), (1,)), ((), ()))
mark = contextlib.nullcontext


def log2(n):
    assert n & (n - 1) == 0
    return n.bit_length() - 1


def iota(shape, dim):
    return lax.broadcasted_iota(I32, shape, dim)


def split(x):
    hi = x.astype(BF16)
    return hi, (x - hi.astype(F32)).astype(BF16)


def mm(a, b):
    return jnp.dot(a, b, preferred_element_type=F32)


def nt(a, b):
    return lax.dot_general(a, b, NT, precision=HIGHEST, preferred_element_type=F32)


def dot3(a, b):
    ah, al = a
    bh, bl = split(b)
    return mm(jnp.concatenate([ah, ah, al], axis=1), jnp.concatenate([bh, bl, bh], axis=0))


def tripled(a, outer):
    pieces = []
    for v in (a, outer):
        if v is not None:
            hi, low = split(v)
            pieces += [hi, hi, low]
    used = sum(v.shape[1] for v in pieces)
    spare = up(used, 128) - used
    if spare:
        pieces.append(jnp.zeros((a.shape[0], spare), BF16))
    return jnp.concatenate(pieces, axis=1)


def mixed(table, b, outer):
    pieces = []
    for v in (b, outer):
        if v is not None:
            hi, low = split(v)
            pieces += [hi, low, hi]
    used = sum(v.shape[0] for v in pieces)
    spare = up(used, 128) - used
    if spare:
        pieces.append(jnp.zeros((spare, b.shape[1]), BF16))
    return mm(table, jnp.concatenate(pieces, axis=0))


def side_by_side(terms, k, levels):
    return jnp.concatenate(
        [jnp.concatenate([v[(k + i) * levels:(k + i + 1) * levels] for v in terms], axis=0) for i in (0, 1)], axis=1
    )


def up(n, to):
    return -(-n // to) * to


def parts_of(share):
    parts = 2 if share % 8 == 0 else 1
    return parts, share // parts


def blocks_of(part, width):
    least = 2 * STEPS + 2
    reach = least if least * part % 8 == 0 else HALO
    data = reach * part
    return reach, data, up(data + 1, PACK), up(width * part - 2 * data, PACK)


def margin_of(e, part):
    return up((4 - 2 * e) * part + 1, PACK)


def wait_all(ref, sem):
    pltpu.make_async_copy(ref, ref, sem).wait()


def smoother(ny):
    yi = iota((1, ny), 1)
    from_south = jnp.where(yi > 0, 0.25, 0.0).astype(F32)
    from_north = jnp.where(yi < ny - 1, 0.25, 0.0).astype(F32)

    def smooth_y(v):
        return 0.5 * v + (from_south * pltpu.roll(v, 1, 1) + from_north * pltpu.roll(v, ny - 1, 1))

    return smooth_y


def exponent(parts, ny):
    most = None
    for p in parts:
        v = jnp.max(jnp.abs(p.reshape(-1, ny)), axis=0, keepdims=True)
        most = v if most is None else jnp.maximum(most, v)
    return jnp.floor(jnp.log2(jnp.maximum(most, 1e-30))) + 1.0


def encode(x, e):
    return jnp.round(x * (jnp.exp2(-e) * SPAN)).astype(I32).astype(I16)


def whole_number(q):
    return q.astype(I32).astype(F32)


def unit(code):
    return jnp.exp2(whole_number(code)[0:1]) * (1.0 / SPAN)


def kernel(
    n_mem, n_tile, members, levels, width, ny, nobs,
    ens_hbm, ctl_hbm, loc_hbm, wind_hbm, codes_hbm, cell_hbm, innov_hbm, sigma_hbm,
    ensf, adj_out, edges_out, wide, final_b,
    ens, ctl, loc, wind, codes, cell, obs, in_sem, hot,
    work, mats, small, table_a, table_b, blur2, coef, thin,
    ctl_stage, ctl_halo, surf_stage, surf_halo, obs_halo, seen, ens_stage, ens_halo,
    tot, stage, rs_src, rs_main, rs_halo, inc,
    turned, fringe, fringes, marks_all, ag0, ag1, edge_src, edge_main, edge_halo, final_a,
    sent, r0_recv, rs_recv, ag_recv, edge_recv,
):
    m = lax.axis_index("mem")
    t = lax.axis_index("tile")
    has = (t > 0, t < n_tile - 1)
    rows = V * levels
    share = rows // n_mem
    block = levels * width
    kl = members * levels
    xs, ys = log2(width), log2(ny)
    n = HALO + width + HALO
    parts, sp = parts_of(share)
    reach, data, hb, mb = blocks_of(sp, width)
    across = width + 2 * reach
    copies = max(8 // sp, 1)
    deep = sp * copies
    tables, finals = (table_a, table_b)[2 - parts:], (final_a, final_b)[2 - parts:]
    cuts = nobs // ny
    assert 1 << log2(n_mem) == n_mem
    peers = range(n_mem - 1, 0, -1)
    outward = 1 - (t & 1)
    inner_rows = sp * width

    def tell(dev):
        pl.semaphore_signal(pltpu.get_barrier_semaphore(), inc=1, device_id=dev, device_id_type=MESH)

    for d in peers:
        tell((m ^ d, t))

    @pl.when(has[0])
    def _():
        for d in range(n_mem):
            tell((m ^ d, t - 1))

    @pl.when(has[1])
    def _():
        for d in range(n_mem):
            tell((m ^ d, t + 1))

    loads = [
        pltpu.make_async_copy(src, dst, in_sem.at[i])
        for i, (src, dst) in enumerate((
            (loc_hbm, loc),
            *((ctl_hbm.at[pl.ds(at, 2 * block)], ctl.at[pl.ds(at, 2 * block)]) for at in range(0, members * block, 2 * block)),
            (ens_hbm, ens), (wind_hbm, wind), (codes_hbm, codes),
            (cell_hbm, cell), (innov_hbm.at[m], obs.at[0]), (sigma_hbm.at[m], obs.at[1]),
        ))
    ]
    for load in loads:
        load.start()

    def to_side(side, d, src, dst, ssem, rsem):
        dev = (m ^ d, t + 1 - 2 * side)
        return pltpu.make_async_remote_copy(
            src_ref=src, dst_ref=dst, send_sem=ssem, recv_sem=rsem, device_id=dev, device_id_type=MESH
        )

    def to_mem(d, src, dst, ssem, rsem):
        return pltpu.make_async_remote_copy(
            src_ref=src, dst_ref=dst, send_sem=ssem, recv_sem=rsem,
            device_id=(m ^ d, t), device_id_type=MESH,
        )

    ctl_loads, late_loads = loads[1:1 + members // 2], loads[1 + members // 2:]
    def both_sides(start):
        for s in (outward, 1 - outward):
            dev = t + 1 - 2 * s

            @pl.when((dev >= 0) & (dev < n_tile))
            def _():
                start(s)

    CTL, SURF, OBS, ENS = range(4)
    def first_msg(side, i):
        s, d = (
            (ctl_stage.at[side], ctl_halo.at[side]),
            (surf_stage.at[side], surf_halo.at[side]),
            (obs, obs_halo.at[side]),
            (ens_stage.at[side], ens_halo.at[side]),
        )[i]
        return to_side(side, 0, s, d, sent.at[side], r0_recv.at[side, i])

    def start_sides(which):
        def start(side):
            for i in which:
                first_msg(side, i).start()

        both_sides(start)

    def recv_sides(which):
        for side in (0, 1):
            @pl.when(has[side])
            def _():
                for i in which:
                    first_msg(side, i).wait_recv()

    for side in (0, 1):
        @pl.when(jnp.logical_not(has[side]))
        def _():
            ctl_halo[side] = jnp.zeros_like(ctl_halo[side])
            surf_halo[side, pl.ds(0, HALO)] = jnp.zeros((HALO, ny), F32)
            surf_halo[side, pl.ds(HALO, HALO)] = jnp.ones((HALO, ny), F32)
            surf_halo[side, pl.ds(2 * HALO, cuts)] = jnp.full((cuts, ny), -1.0, F32)
            obs_halo[side, 0] = jnp.zeros((share, nobs), F32)
            obs_halo[side, 1] = jnp.ones((share, nobs), F32)
            ens_halo[side] = jnp.zeros_like(ens_halo[side])
            edge_halo[side] = jnp.zeros_like(edge_halo[side])
            for e in (0, 1):
                for p in range(parts):
                    rs_halo[e, p, side] = jnp.zeros_like(rs_halo[e, p, side])

    smooth_y = smoother(ny)
    gap = lambda shape, mask: jnp.abs((iota(shape, 0) & mask) - (iota(shape, 1) & mask))
    lev = lambda shape, dim, shift: iota(shape, dim) >> shift

    with mark("w_loc"):
        loads[0].wait()
    with mark("mats0"):
        lo = loc[...]
        spread = (lev((levels, block), 1, xs) == iota((levels, block), 0)).astype(BF16)
        repeat = ((iota((levels, kl), 1) & (levels - 1)) == iota((levels, kl), 0)).astype(BF16)
        near_x = gap((block, block), width - 1)
        near_x = jnp.where(near_x == 0, 0.5, jnp.where(near_x == 1, 0.25, 0.0)).astype(F32)
        same_k = (lev((kl, kl), 0, log2(levels)) == lev((kl, kl), 1, log2(levels))).astype(F32)
        for j, piece in enumerate(split(lo)):
            p = piece.astype(F32)
            tall = jnp.broadcast_to(p[:, None, :], (levels, width, levels)).reshape(block, levels)
            mats[0, j] = (mm(tall.astype(BF16), spread) * near_x).astype(BF16)
            tall = jnp.concatenate([p] * members, axis=0)
            small[0, j] = (mm(tall.astype(BF16), repeat) * same_k).astype(BF16)

    def mix_pair(k):
        both = jnp.concatenate(
            [ctl[k * block:(k + 1) * block, :], ctl[(k + 1) * block:(k + 2) * block, :]], axis=1
        )
        wide[k // 2] = dot3((mats[0, 0], mats[0, 1]), both)

    with mark("mix_first"):
        ctl_loads[0].wait()
        mix_pair(0)
    with mark("w_ctl"):
        for load in ctl_loads[1:]:
            load.wait()
    ctl_stage[0] = ctl[pl.ds(width - 1, kl, stride=width), :]
    ctl_stage[1] = ctl[pl.ds(0, kl, stride=width), :]

    with mark("w_barrier"):
        count = n_mem - 1 + n_mem * (jnp.where(t > 0, 1, 0) + jnp.where(t < n_tile - 1, 1, 0))
        pl.semaphore_wait(pltpu.get_barrier_semaphore(), count)

    start_sides((CTL,))

    with mark("mix_a0"):
        for k in range(2, members, 2):
            mix_pair(k)
        for k in range(members):
            work[pl.ds(k * block, block), :] = smooth_y(wide[k // 2, :, (k % 2) * ny:(k % 2 + 1) * ny])

    with mark("stage"):
        for load in late_loads:
            load.wait()
        for side, at in ((0, pl.ds(width - HALO, HALO)), (1, pl.ds(0, HALO))):
            surf_stage[side, pl.ds(0, HALO)] = wind[at, :]
            surf_stage[side, pl.ds(HALO, HALO)] = codes[at, :].astype(F32)
            for c in range(cuts):
                surf_stage[side, pl.ds(2 * HALO + c, 1)] = cell[:, c * ny:(c + 1) * ny].astype(F32)
        start_sides((SURF, OBS))

    def member_edges():
        for k in range(members):
            ensf[pl.ds(k * rows * width, rows * width), :] = ens[k].astype(F32).reshape(rows * width, ny)
        for i in (0, 1):
            ens_stage[0, i] = ensf[pl.ds(width - 1 - i, members * rows, stride=width), :].astype(BF16)
            ens_stage[1, i] = ensf[pl.ds(i, members * rows, stride=width), :].astype(BF16)

    def send_edges():
        sides = 0.25 * dot3((small[0, 0], small[0, 1]), jnp.concatenate([ctl_halo[0], ctl_halo[1]], axis=1))
        for j in (0, 1):
            a = smooth_y(sides[:, j * ny:(j + 1) * ny]).reshape(members, 1, levels, ny)
            p = ens_stage[1 - j, 0].astype(F32).reshape(members, V, levels, ny) * a
            total = jnp.sum(p, axis=0).reshape(rows, ny)
            for i in range(n_mem):
                edge_src[i, j] = total[i * share:(i + 1) * share]
        for d in peers:
            who = m ^ d
            to_mem(d, edge_src.at[who], edge_main.at[d - 1], sent.at[2], edge_recv.at[2]).start()

        def start(side):
            for d in (*peers, 0):
                to_side(
                    side, d, edge_src.at[m ^ d, 1 - side], edge_halo.at[side, d], sent.at[side], edge_recv.at[side]
                ).start()

        both_sides(start)

    def wait_edges():
        wait_all(edge_main, edge_recv.at[2])
        for side in (0, 1):
            @pl.when(has[side])
            def _():
                wait_all(edge_halo.at[side], edge_recv.at[side])

    def add_edges(p):
        rows_of = pl.ds(p * sp, sp)
        for j, x, out in ((0, 0, -1), (1, width - 1, width)):
            v = edge_src[m, j, rows_of]
            for d in range(n_mem - 1):
                v = v + edge_main[d, j, rows_of]
            at = pl.ds((reach + x) * sp, sp)
            inc[0, p, at] = inc[0, p, at] + v
            v = edge_halo[j, 0, rows_of]
            for d in range(1, n_mem):
                v = v + edge_halo[j, d, rows_of]
            at = pl.ds((reach + out) * sp, sp)
            inc[0, p, at] = inc[0, p, at] + v

    def halo_cells(side):
        return jnp.concatenate([surf_halo[side, pl.ds(2 * HALO + c, 1)] for c in range(cuts)], axis=1).astype(I32)

    def coefficients():
        code = jnp.concatenate(
            [surf_halo[0, pl.ds(HALO, HALO)], codes[...].astype(F32), surf_halo[1, pl.ds(HALO, HALO)]], axis=0
        )
        speed = jnp.concatenate([surf_halo[0, pl.ds(0, HALO)], wind[...], surf_halo[1, pl.ds(0, HALO)]], axis=0)
        opened = (code != 1.0).astype(F32)
        absorb = jnp.where(code == 2.0, absorbing, 1.0).astype(F32)
        yy = iota(code.shape, 1)
        west = lambda v: pltpu.roll(v, 1, 0)
        east = lambda v: pltpu.roll(v, n - 1, 0)
        south = lambda v: pltpu.roll(v, 1, 1)
        north = lambda v: pltpu.roll(v, ny - 1, 1)
        oe = opened * east(opened)
        ow = opened * west(opened)
        on = jnp.where(yy < ny - 1, opened * north(opened), 0.0)
        os = jnp.where(yy > 0, opened * south(opened), 0.0)
        k = diffusion_rate
        center = 1.0 - k * (oe + ow + on + os) - speed * oe
        every = (
            absorb * center, absorb * (k + west(speed)) * ow, absorb * k * oe, absorb * k * os, absorb * k * on,
            center * absorb, k * ow * west(absorb), (k + speed) * oe * east(absorb),
            k * os * south(absorb), k * on * north(absorb),
        )
        for i, v in enumerate(every):
            thin[i] = v
            for r in range(sp):
                coef[i, pl.ds(r, across, stride=sp), :] = thin[i, pl.ds(HALO - reach, across), :]

    def stencil(q, which):
        size = across * sp
        return (
            coef[which] * q
            + coef[which + 1] * pltpu.roll(q, sp, 0)
            + coef[which + 2] * pltpu.roll(q, size - sp, 0)
            + coef[which + 3] * pltpu.roll(q, 1, 1)
            + coef[which + 4] * pltpu.roll(q, ny - 1, 1)
        )

    def copy_seen(i, values):
        for p in range(parts):
            for c in range(copies):
                at = pl.ds(c * sp, sp)
                seen[i, p, 0, at] = values[0, pl.ds(p * sp, sp), :]
                seen[i, p, 1, at] = 1.0 / values[1, pl.ds(p * sp, sp), :]

    def observe(state, p):
        tiles = (
            (halo_cells(0), 0, reach, width - reach),
            (cell[...], reach, width, 0),
            (halo_cells(1), reach + width, reach, 0),
        )
        pieces = []
        for i, (where, at, count, offset) in enumerate(tiles):
            hot_y = hot[i]
            lines = count * sp
            shape = (lines // deep, deep, nobs)
            place = jnp.broadcast_to(where >> ys, (deep, nobs)) - offset
            hit = place[None] == ((iota(shape, 0) * deep + iota(shape, 1)) >> log2(sp))
            hi, low = split(state[at * sp:at * sp + lines])
            got = mm(jnp.concatenate([hi, low], axis=0), hot_y)
            some = jnp.sum(jnp.where(hit, (got[:lines] + got[lines:]).reshape(shape), 0.0), axis=0)
            sampled = some
            for c in range(1, copies):
                sampled = sampled + pltpu.roll(some, c * sp, 0)
            weight = jnp.clip((sampled - seen[i, p, 0]) * seen[i, p, 1], -huber_delta, huber_delta) * seen[i, p, 1]
            put = [
                jnp.where(hit, w.astype(F32)[None], 0.0).reshape(lines, nobs).astype(BF16) for w in split(weight)
            ]
            both = lax.dot_general(jnp.concatenate(put, axis=0), hot_y, NT, preferred_element_type=F32)
            pieces.append(both[:lines] + both[lines:])
        return jnp.concatenate(pieces, axis=0)

    def short(x):
        return x.astype(I32).astype(I16)

    def members_sum(e, p):
        for d in (*peers, 0):
            who = m ^ d
            r0 = who * share + p * sp
            l0 = lax.rem(r0, levels)
            total = jnp.zeros((sp, width, ny), F32)
            for k in range(members):
                a = work[pl.ds(pl.multiple_of(k * block + l0 * width, width), sp * width), :]
                total += ens[k, pl.ds(r0, sp)].astype(F32) * a.reshape(sp, width, ny)
            tot[p, d] = total.reshape(inner_rows, ny)
            ex = exponent([total], ny)
            scale = jnp.exp2(-ex) * SPAN
            for x in range(width):
                stage[p, d, pl.ds(x * sp, sp), :] = tot[p, d, pl.ds(x, sp, stride=width), :]
            filler = jnp.broadcast_to(ex, (hb - data, ny))
            for first, at in ((0, 0), (inner_rows - data, hb + mb)):
                v = jnp.round(stage[p, d, pl.ds(first, data), :] * scale)
                rs_src[e, p, d, pl.ds(at, hb)] = short(jnp.concatenate([v, filler], axis=0))
            if mb:
                rs_src[e, p, d, pl.ds(hb, mb)] = short(jnp.round(stage[p, d, pl.ds(data, mb), :] * scale))
    def send_sum(e, p):
        for d in peers:
            to_mem(d, rs_src.at[e, p, d], rs_main.at[e, p, d - 1], sent.at[2], rs_recv.at[e, p, 2]).start()

        def start(side):
            at = pl.multiple_of((1 - side) * (hb + mb), PACK)
            for d in (*peers, 0):
                to_side(
                    side, d, rs_src.at[e, p, d, pl.ds(at, hb)], rs_halo.at[e, p, side, d],
                    sent.at[side], rs_recv.at[e, p, side],
                ).start()

        both_sides(start)

    def gather_sum(e, p):
        wait_all(rs_main.at[e, p], rs_recv.at[e, p, 2])
        for side in (0, 1):
            @pl.when(has[side])
            def _():
                wait_all(rs_halo.at[e, p, side], rs_recv.at[e, p, side])
        bounds = ((0, data, 0, hb), (data, mb, hb, mb), (inner_rows - data, data, hb + mb, hb))
        pieces = [stage[p, 0, pl.ds(at, count), :] if count else None for at, count, _, _ in bounds]
        for d in range(n_mem - 1):
            u = None
            for i, (_, count, at, size) in enumerate(bounds):
                if count:
                    v = whole_number(rs_main[e, p, d, pl.ds(at, size)])
                    u = jnp.exp2(v[data:data + 1]) * (1.0 / SPAN) if u is None else u
                    pieces[i] = pieces[i] + (v * u)[:count]
        outer = []
        for side in (0, 1):
            total = None
            for d in range(n_mem):
                v = whole_number(rs_halo[e, p, side, d])
                v = v * (jnp.exp2(v[data:data + 1]) * (1.0 / SPAN))
                total = v if total is None else total + v
            outer.append(total[:data])
        at = 0
        for v in (outer[0], *pieces, outer[1]):
            if v is not None:
                inc[e, p, pl.ds(at, v.shape[0])] = v
                at += v.shape[0]

    def observation_term(e, some, fields):
        ag = (ag0, ag1)[e]
        margin = margin_of(e, sp)
        for i in range(STEPS):
            fields = [stencil(q, 0) for q in fields]
        with mark("observe"):
            fields = [observe(q, p) for p, q in zip(some, fields)]
        for i in range(STEPS):
            fields = [stencil(q, 5) for q in fields]
        lines = (-1, width) + ((-2, width + 1) if e == 0 else ())
        used = len(lines) * sp
        for p, q in zip(some, fields):
            turned[p] = q
            ex = exponent([turned[p, pl.ds((reach - 2) * sp, (width + 4) * sp), :]], ny)
            scale = jnp.exp2(-ex) * SPAN
            for i, x in enumerate(lines):
                fringe[p, pl.ds(i * sp, sp), :] = jnp.round(turned[p, pl.ds((reach + x) * sp, sp), :] * scale)
            fringe[p, pl.ds(used, margin - used), :] = jnp.broadcast_to(ex, (margin - used, ny))
            for r in range(sp):
                v = turned[p, pl.ds(reach * sp + r, width, stride=sp), :]
                ag[p, m, pl.ds(r * width, width)] = short(jnp.round(v * scale))
            ag[p, m, pl.ds(inner_rows, margin)] = short(fringe[p, pl.ds(0, margin), :])
        for p in some:
            for d in peers:
                to_mem(d, ag.at[p, m], ag.at[p, m], sent.at[2], ag_recv.at[e, p]).start()

    def adjoint_rows(e, p):
        ag = (ag0, ag1)[e]
        margin = margin_of(e, sp)
        wait_all(ag.at[p, pl.ds(0, n_mem - 1)], ag_recv.at[e, p])
        for i in range(n_mem):
            v = whole_number(ag[p, i, pl.ds(inner_rows, margin)])
            u = jnp.exp2(v[margin - 1:margin]) * (1.0 / SPAN)
            at = i * share + p * sp
            adj_out[pl.ds(at * width, inner_rows), :] = whole_number(ag[p, i, pl.ds(0, inner_rows)]) * u
            fringes[p, i, pl.ds(0, margin)] = v * u
            for j in range(4 - 2 * e):
                marks_all[j, pl.ds(at, sp), :] = fringes[p, i, pl.ds(j * sp, sp), :]

    def edge_terms(e):
        terms = []
        for j in range(4 - 2 * e):
            v = ens_halo[j % 2, j // 2].astype(F32).reshape(members, rows, ny) * marks_all[j][None]
            terms.append((v[:, :levels] + v[:, levels:]).reshape(kl, ny))
        return terms

    def pair_term(k, p):
        return member_pair(ensf, adj_out, levels, width, share, k, p)

    with mark("part0"):
        members_sum(0, 0)
        send_sum(0, 0)
        for p in range(1, parts):
            members_sum(0, p)
    with mark("member_edges"):
        member_edges()
    with mark("w_ctlhalo"):
        recv_sides((CTL,))
    with mark("edges"):
        send_edges()
        for p in range(1, parts):
            send_sum(0, p)
    with mark("hidden"):
        pick = (lev((block, levels), 0, xs) == iota((block, levels), 1)).astype(F32)
        both = nt(lo, lo)
        xi = iota((block, levels), 0) & (width - 1)
        at_x = lambda v, *marks: v * sum(jnp.where(xi == x, c, 0.0).astype(F32) for x, c in marks)
        last = width - 1
        high = jnp.dot(pick, both, precision=HIGHEST, preferred_element_type=F32)
        columns = block // parts
        ci = iota((columns, levels), 0)
        level = ((ci >> log2(inner_rows)) << log2(share)) + ((ci & (inner_rows - 1)) >> xs)
        far_x = gap((block, columns), width - 1)
        far_x = jnp.where(far_x == 0, 0.375, jnp.where(far_x == 1, 0.25, jnp.where(far_x == 2, 0.0625, 0.0)))
        xr, xc = iota((block, columns), 0) & (width - 1), iota((block, columns), 1) & (width - 1)
        for side, x in ((0, 0), (1, last)):
            lost = jnp.where(has[side], 0.0, 0.0625).astype(F32)
            far_x = far_x - jnp.where((xr == x) & (xc == x), lost, 0.0)
        outer = jnp.concatenate([
            at_x(high, (0, 0.25), (1, 0.0625)), at_x(high, (last, 0.25), (last - 1, 0.0625)),
            at_x(high, (0, 0.0625)), at_x(high, (last, 0.0625)),
        ], axis=1)
        for p in range(parts):
            own_pick = (level + p * sp == iota((columns, levels), 1)).astype(F32)
            tables[p][...] = tripled(nt(high, own_pick) * far_x, outer if p == parts - 1 else None)
        high = nt(pick, lo)
        near_x = gap((block, columns), width - 1)
        near_x = jnp.where(near_x == 0, 0.5, jnp.where(near_x == 1, 0.25, 0.0)).astype(F32)
        outer = jnp.concatenate([at_x(high, (0, 0.25)), at_x(high, (last, 0.25))], axis=1)
        for p in range(parts):
            own_pick = (level + p * sp == iota((columns, levels), 1)).astype(F32)
            finals[p][...] = tripled(nt(high, own_pick) * near_x, outer if p == parts - 1 else None)
        yr, yc = iota((2 * ny, 2 * ny), 0), iota((2 * ny, 2 * ny), 1)
        far_y = jnp.abs(yr - yc)
        corner = (yr & (ny - 1) == 0) | (yr & (ny - 1) == ny - 1)
        far_y = jnp.where(
            far_y == 0, jnp.where(corner, 0.3125, 0.375),
            jnp.where(far_y == 1, 0.25, jnp.where(far_y == 2, 0.0625, 0.0)),
        )
        blur2[...] = jnp.where((yr >> ys) == (yc >> ys), far_y, 0.0).astype(BF16)
        recv_sides((SURF,))
        copy_seen(1, obs)
        for i, where in enumerate((halo_cells(0), cell[...], halo_cells(1))):
            hot[i] = (iota((ny, nobs), 0) == (where & (ny - 1))).astype(BF16)
        coefficients()
        start_sides((ENS,))
    for p in range(parts):
        with mark(f"w_rs0_{p}"):
            gather_sum(0, p)
        if p == 0:
            with mark("w_obs"):
                recv_sides((OBS,))
                for side in (0, 1):
                    copy_seen(2 * side, obs_halo.at[side])
            with mark("w_edge"):
                wait_edges()
        with mark(f"obs0_{p}"):
            add_edges(p)
            observation_term(0, [p], [inc[0, p]])
    with mark("w_ens"):
        recv_sides((ENS,))
    for p in range(parts - 1):
        with mark(f"w_ag0_{p}"):
            adjoint_rows(0, p)
        with mark(f"mix1_{p}"):
            for k in range(0, members, 2):
                v = mixed(tables[p][...], pair_term(k, p), None)
                wide[k // 2] = v if p == 0 else wide[k // 2] + v
    with mark("w_ag0"):
        adjoint_rows(0, parts - 1)
        terms = edge_terms(0)
    with mark("mix1"):
        def blur(v):
            hi, low = split(v)
            return mm(jnp.concatenate([hi, low], axis=1), jnp.concatenate([blur2[...], blur2[...]], axis=0))

        for k in range(0, members, 2):
            v = mixed(tables[parts - 1][...], pair_term(k, parts - 1), side_by_side(terms, k, levels))
            wide[k // 2] = v if parts == 1 else wide[k // 2] + v
        for k in range(0, members, 2):
            done = blur(wide[k // 2])
            work[k * block:(k + 1) * block, :] = done[:, :ny]
            work[(k + 1) * block:(k + 2) * block, :] = done[:, ny:]
    with mark("part1"):
        for p in range(parts):
            members_sum(1, p)
            send_sum(1, p)
    for p in range(parts):
        with mark(f"w_rs1_{p}"):
            gather_sum(1, p)
        with mark(f"obs1_{p}"):
            observation_term(1, [p], [step_length * (inc[0, p] - inc[1, p])])
    for p in range(parts - 1):
        with mark(f"w_ag1_{p}"):
            adjoint_rows(1, p)
        with mark(f"mix2_{p}"):
            for k in range(0, members, 2):
                v = mixed(finals[p][...], pair_term(k, p), None)
                wide[k // 2] = v if p == 0 else wide[k // 2] + v
    with mark("term1"):
        adjoint_rows(1, parts - 1)
        terms = edge_terms(1)
        for side in (0, 1):
            edges_out[:, side * ny:(side + 1) * ny] = terms[side]
    with mark("drain"):
        size = lambda ref: math.prod(ref.shape) * ref.dtype.itemsize
        line = ny * 4
        total = size(rs_main) + size(edge_main) + (n_mem - 1) * (size(ag0) + size(ag1)) // n_mem
        wait_all(ensf.at[pl.ds(0, total // line)], sent.at[2])
        total = sum(size(ref) for ref in (rs_halo, edge_halo, ctl_halo, surf_halo, obs_halo, ens_halo)) // 2
        for side in (0, 1):
            @pl.when(has[1 - side])
            def _():
                wait_all(ensf.at[pl.ds(0, total // line)], sent.at[side])


def member_pair(ensf, adj, levels, width, share, k, p):
    block = levels * width
    _, sp = parts_of(share)

    def term(k):
        pieces = []
        for i in range(levels // share):
            at = (i * share + p * sp) * width
            low, high = pl.ds(at, sp * width), pl.ds(block + at, sp * width)
            base = 2 * k * block + at
            pieces.append(
                ensf[pl.ds(base, sp * width), :] * adj[low, :] + ensf[pl.ds(base + block, sp * width), :] * adj[high, :]
            )
        return jnp.concatenate(pieces, axis=0)

    return jnp.concatenate([term(k), term(k + 1)], axis=1)


def finish(members, levels, width, share, ny, ensf, adj, edges, wide, table, out, work, sem):
    block = levels * width
    parts, _ = parts_of(share)
    smooth_y = smoother(ny)
    terms = [edges[:, j * ny:(j + 1) * ny] for j in (0, 1)]
    for k in range(0, members, 2):
        done = mixed(
            table[...], member_pair(ensf, adj, levels, width, share, k, parts - 1), side_by_side(terms, k, levels)
        )
        if parts > 1:
            done = done + wide[k // 2]
        for i in (0, 1):
            at = pl.ds((k + i) * block, block)
            work[at, :] = smooth_y(done[:, i * ny:(i + 1) * ny])
            pltpu.make_async_copy(work.at[at], out.at[at], sem.at[0]).start()
    pltpu.make_async_copy(work, out, sem.at[0]).wait()


def body(n_mem, n_tile, ensemble, control, level_loc, wind_speed, cell_codes, obs_cell, innovation, obs_sigma):
    members, rows, width, ny = ensemble.shape
    levels = control.shape[1]
    assert width >= 2 * HALO and members % 2 == 0 and rows == 2 * levels
    nobs = obs_cell.shape[0]
    share = rows // n_mem
    kl = members * levels
    block = levels * width
    n = width + 2 * HALO
    vmem = pltpu.VMEM
    dma = pltpu.SemaphoreType.DMA
    parts, sp = parts_of(share)
    reach, data, hb, mb = blocks_of(sp, width)
    size = 2 * hb + mb
    tall = max(8, sp)
    margins = [margin_of(e, sp) for e in (0, 1)]
    surf = up(2 * HALO + nobs // ny, 8)
    scratch = [
        vmem((members, rows, width, ny), BF16),
        vmem((members * block, ny), F32),
        vmem((levels, levels), F32),
        vmem((width, ny), F32),
        vmem((width, ny), I32),
        vmem((1, nobs), I32),
        vmem((2, share, nobs), F32),
        dma((7 + members // 2,)),
        vmem((3, ny, nobs), BF16),
        vmem((members * block, ny), F32),
        vmem((1, 2, block, block), BF16),
        vmem((1, 2, kl, kl), BF16),
        vmem((block, up(3 * block // parts, 128)), BF16),
        vmem((block, up(3 * block // parts + 12 * levels, 128)), BF16),
        vmem((2 * ny, 2 * ny), BF16),
        vmem((10, (width + 2 * reach) * sp, ny), F32),
        vmem((10, n, ny), F32),
        vmem((2, kl, ny), F32),
        vmem((2, kl, ny), F32),
        vmem((2, surf, ny), F32),
        vmem((2, surf, ny), F32),
        vmem((2, 2, share, nobs), F32),
        vmem((3, parts, 2, tall, nobs), F32),
        vmem((2, 2, members * rows, ny), BF16),
        vmem((2, 2, members * rows, ny), BF16),
        vmem((parts, n_mem, sp * width, ny), F32),
        vmem((parts, n_mem, sp * width, ny), F32),
        vmem((2, parts, n_mem, size, ny), I16),
        vmem((2, parts, n_mem - 1, size, ny), I16),
        vmem((2, parts, 2, n_mem, hb, ny), I16),
        vmem((2, parts, (width + 2 * reach) * sp, ny), F32),
        vmem((parts, (width + 2 * reach) * sp, ny), F32),
        vmem((parts, margins[0], ny), F32),
        vmem((parts, n_mem, margins[0], ny), F32),
        vmem((4, rows, ny), F32),
        *(vmem((parts, n_mem, sp * width + margins[e], ny), I16) for e in (0, 1)),
        vmem((n_mem, 2, share, ny), F32),
        vmem((n_mem - 1, 2, share, ny), F32),
        vmem((2, n_mem, share, ny), F32),
        vmem((block, up(3 * block // parts, 128)), BF16),
        dma((3,)), dma((2, 4)), dma((2, parts, 3)), dma((2, parts)), dma((3,)),
    ]
    whole = pl.BlockSpec(memory_space=pltpu.VMEM)
    hbm = pl.BlockSpec(memory_space=pltpu.HBM)
    handed = pl.pallas_call(
        functools.partial(kernel, n_mem, n_tile, members, levels, width, ny, nobs),
        out_shape=(
            vmem((members * rows * width, ny), F32), vmem((rows * width, ny), F32), vmem((kl, 2 * ny), F32),
            vmem((members // 2, block, 2 * ny), F32), vmem((block, up(3 * block // parts + 6 * levels, 128)), BF16),
        ),
        in_specs=[hbm] * 8,
        out_specs=(whole,) * 5,
        scratch_shapes=scratch,
        compiler_params=pltpu.CompilerParams(
            collective_id=0, has_side_effects=True, vmem_limit_bytes=40 << 20
        ),
    )(*(pltpu.with_memory_space_constraint(x, pltpu.HBM) for x in (
        ensemble,
        control.reshape(members * block, ny),
        level_loc,
        wind_speed,
        cell_codes,
        obs_cell.reshape(1, nobs),
        innovation.reshape(n_mem, share, nobs),
        obs_sigma.reshape(n_mem, share, nobs),
    )))
    result = pl.pallas_call(
        functools.partial(finish, members, levels, width, share, ny),
        out_shape=jax.ShapeDtypeStruct((members * block, ny), F32),
        in_specs=[whole] * 5,
        out_specs=hbm,
        scratch_shapes=[vmem((members * block, ny), F32), dma((1,))],
        compiler_params=pltpu.CompilerParams(vmem_limit_bytes=40 << 20),
    )(*(pltpu.with_memory_space_constraint(x, pltpu.VMEM) for x in handed))
    return result.reshape(members, levels, width, ny)


def solution(mesh):
    placed = (
        P("mem", None, "tile", None),
        P("mem", None, "tile", None),
        P(),
        P("tile", None),
        P("tile", None),
        P("tile"),
        P(None, "tile"),
        P(None, "tile"),
    )
    return jax.shard_map(
        functools.partial(body, mesh.shape["mem"], mesh.shape["tile"]),
        mesh=mesh, in_specs=placed, out_specs=P("mem", None, "tile", None), check_vma=False,
    )
```

```python
import contextlib
import functools
import math

import jax
import jax.numpy as jnp
from jax import lax
from jax.experimental import pallas as pl
from jax.experimental.pallas import tpu as pltpu
from jax.sharding import PartitionSpec as P

V = 2
STEPS = 2
HALO = 8
PACK = 16
SPAN = 32760.0

diffusion_rate = 0.12
absorbing = 0.7
step_length = 0.5
huber_delta = 1.0

MESH = pl.DeviceIdType.MESH
F32 = jnp.float32
BF16 = jnp.bfloat16
I16 = jnp.int16
I32 = jnp.int32
HIGHEST = lax.Precision.HIGHEST
NT = (((1,), (1,)), ((), ()))
mark = contextlib.nullcontext


def log2(n):
    assert n & (n - 1) == 0
    return n.bit_length() - 1


def iota(shape, dim):
    return lax.broadcasted_iota(I32, shape, dim)


def split(x):
    hi = x.astype(BF16)
    return hi, (x - hi.astype(F32)).astype(BF16)


def mm(a, b):
    return jnp.dot(a, b, preferred_element_type=F32)


def nt(a, b):
    return lax.dot_general(a, b, NT, precision=HIGHEST, preferred_element_type=F32)


def dot3(a, b):
    ah, al = a
    bh, bl = split(b)
    return mm(jnp.concatenate([ah, ah, al], axis=1), jnp.concatenate([bh, bl, bh], axis=0))


def tripled(a, outer):
    pieces = []
    for v in (a, outer):
        if v is not None:
            hi, low = split(v)
            pieces += [hi, hi, low]
    used = sum(v.shape[1] for v in pieces)
    spare = up(used, 128) - used
    if spare:
        pieces.append(jnp.zeros((a.shape[0], spare), BF16))
    return jnp.concatenate(pieces, axis=1)


def mixed(table, b, outer):
    pieces = []
    for v in (b, outer):
        if v is not None:
            hi, low = split(v)
            pieces += [hi, low, hi]
    used = sum(v.shape[0] for v in pieces)
    spare = up(used, 128) - used
    if spare:
        pieces.append(jnp.zeros((spare, b.shape[1]), BF16))
    return mm(table, jnp.concatenate(pieces, axis=0))


def side_by_side(terms, k, levels):
    return jnp.concatenate(
        [jnp.concatenate([v[(k + i) * levels:(k + i + 1) * levels] for v in terms], axis=0) for i in (0, 1)], axis=1
    )


def up(n, to):
    return -(-n // to) * to


def parts_of(share):
    parts = 2 if share % 8 == 0 else 1
    return parts, share // parts


def blocks_of(part, width):
    least = 2 * STEPS + 2
    reach = least if least * part % 8 == 0 else HALO
    data = reach * part
    return reach, data, up(data + 1, PACK), up(width * part - 2 * data, PACK)


def margin_of(e, part):
    return up((4 - 2 * e) * part + 1, PACK)


def wait_all(ref, sem):
    pltpu.make_async_copy(ref, ref, sem).wait()


def smoother(ny):
    yi = iota((1, ny), 1)
    from_south = jnp.where(yi > 0, 0.25, 0.0).astype(F32)
    from_north = jnp.where(yi < ny - 1, 0.25, 0.0).astype(F32)

    def smooth_y(v):
        return 0.5 * v + (from_south * pltpu.roll(v, 1, 1) + from_north * pltpu.roll(v, ny - 1, 1))

    return smooth_y


def exponent(parts, ny):
    most = None
    for p in parts:
        v = jnp.max(jnp.abs(p.reshape(-1, ny)), axis=0, keepdims=True)
        most = v if most is None else jnp.maximum(most, v)
    return jnp.floor(jnp.log2(jnp.maximum(most, 1e-30))) + 1.0


def encode(x, e):
    return jnp.round(x * (jnp.exp2(-e) * SPAN)).astype(I32).astype(I16)


def whole_number(q):
    return q.astype(I32).astype(F32)


def unit(code):
    return jnp.exp2(whole_number(code)[0:1]) * (1.0 / SPAN)


def kernel(
    n_mem, n_tile, members, levels, width, ny, nobs,
    ens_hbm, ctl_hbm, loc_hbm, wind_hbm, codes_hbm, cell_hbm, innov_hbm, sigma_hbm,
    ensf, adj_out, edges_out, wide, final_b,
    ens, ctl, loc, wind, codes, cell, obs, in_sem, hot,
    work, mats, small, table_a, table_b, blur2, coef, thin,
    ctl_stage, ctl_halo, surf_stage, surf_halo, obs_halo, seen, ens_stage, ens_halo,
    tot, stage, rs_src, rs_main, rs_halo, inc,
    turned, fringe, fringes, marks_all, ag0, ag1, edge_src, edge_main, edge_halo, final_a,
    sent, r0_recv, rs_recv, ag_recv, edge_recv,
):
    m = lax.axis_index("mem")
    t = lax.axis_index("tile")
    has = (t > 0, t < n_tile - 1)
    rows = V * levels
    share = rows // n_mem
    block = levels * width
    kl = members * levels
    xs, ys = log2(width), log2(ny)
    n = HALO + width + HALO
    parts, sp = parts_of(share)
    reach, data, hb, mb = blocks_of(sp, width)
    across = width + 2 * reach
    copies = max(8 // sp, 1)
    deep = sp * copies
    tables, finals = (table_a, table_b)[2 - parts:], (final_a, final_b)[2 - parts:]
    cuts = nobs // ny
    assert 1 << log2(n_mem) == n_mem
    peers = range(n_mem - 1, 0, -1)
    outward = 1 - (t & 1)
    inner_rows = sp * width

    def tell(dev):
        pl.semaphore_signal(pltpu.get_barrier_semaphore(), inc=1, device_id=dev, device_id_type=MESH)

    for d in peers:
        tell((m ^ d, t))

    @pl.when(has[0])
    def _():
        for d in range(n_mem):
            tell((m ^ d, t - 1))

    @pl.when(has[1])
    def _():
        for d in range(n_mem):
            tell((m ^ d, t + 1))

    loads = [
        pltpu.make_async_copy(src, dst, in_sem.at[i])
        for i, (src, dst) in enumerate((
            (loc_hbm, loc),
            *((ctl_hbm.at[pl.ds(at, 2 * block)], ctl.at[pl.ds(at, 2 * block)]) for at in range(0, members * block, 2 * block)),
            (ens_hbm, ens), (wind_hbm, wind), (codes_hbm, codes),
            (cell_hbm, cell), (innov_hbm.at[m], obs.at[0]), (sigma_hbm.at[m], obs.at[1]),
        ))
    ]
    for load in loads:
        load.start()

    def to_side(side, d, src, dst, ssem, rsem):
        dev = (m ^ d, t + 1 - 2 * side)
        return pltpu.make_async_remote_copy(
            src_ref=src, dst_ref=dst, send_sem=ssem, recv_sem=rsem, device_id=dev, device_id_type=MESH
        )

    def to_mem(d, src, dst, ssem, rsem):
        return pltpu.make_async_remote_copy(
            src_ref=src, dst_ref=dst, send_sem=ssem, recv_sem=rsem,
            device_id=(m ^ d, t), device_id_type=MESH,
        )

    ctl_loads, late_loads = loads[1:1 + members // 2], loads[1 + members // 2:]
    def both_sides(start):
        for s in (outward, 1 - outward):
            dev = t + 1 - 2 * s

            @pl.when((dev >= 0) & (dev < n_tile))
            def _():
                start(s)

    CTL, SURF, OBS, ENS = range(4)
    def first_msg(side, i):
        s, d = (
            (ctl_stage.at[side], ctl_halo.at[side]),
            (surf_stage.at[side], surf_halo.at[side]),
            (obs, obs_halo.at[side]),
            (ens_stage.at[side], ens_halo.at[side]),
        )[i]
        return to_side(side, 0, s, d, sent.at[side], r0_recv.at[side, i])

    def start_sides(which):
        def start(side):
            for i in which:
                first_msg(side, i).start()

        both_sides(start)

    def recv_sides(which):
        for side in (0, 1):
            @pl.when(has[side])
            def _():
                for i in which:
                    first_msg(side, i).wait_recv()

    for side in (0, 1):
        @pl.when(jnp.logical_not(has[side]))
        def _():
            ctl_halo[side] = jnp.zeros_like(ctl_halo[side])
            surf_halo[side, pl.ds(0, HALO)] = jnp.zeros((HALO, ny), F32)
            surf_halo[side, pl.ds(HALO, HALO)] = jnp.ones((HALO, ny), F32)
            surf_halo[side, pl.ds(2 * HALO, cuts)] = jnp.full((cuts, ny), -1.0, F32)
            obs_halo[side, 0] = jnp.zeros((share, nobs), F32)
            obs_halo[side, 1] = jnp.ones((share, nobs), F32)
            ens_halo[side] = jnp.zeros_like(ens_halo[side])
            edge_halo[side] = jnp.zeros_like(edge_halo[side])
            for e in (0, 1):
                for p in range(parts):
                    rs_halo[e, p, side] = jnp.zeros_like(rs_halo[e, p, side])

    smooth_y = smoother(ny)
    gap = lambda shape, mask: jnp.abs((iota(shape, 0) & mask) - (iota(shape, 1) & mask))
    lev = lambda shape, dim, shift: iota(shape, dim) >> shift

    with mark("w_loc"):
        loads[0].wait()
    with mark("mats0"):
        lo = loc[...]
        spread = (lev((levels, block), 1, xs) == iota((levels, block), 0)).astype(BF16)
        repeat = ((iota((levels, kl), 1) & (levels - 1)) == iota((levels, kl), 0)).astype(BF16)
        near_x = gap((block, block), width - 1)
        near_x = jnp.where(near_x == 0, 0.5, jnp.where(near_x == 1, 0.25, 0.0)).astype(F32)
        same_k = (lev((kl, kl), 0, log2(levels)) == lev((kl, kl), 1, log2(levels))).astype(F32)
        for j, piece in enumerate(split(lo)):
            p = piece.astype(F32)
            tall = jnp.broadcast_to(p[:, None, :], (levels, width, levels)).reshape(block, levels)
            mats[0, j] = (mm(tall.astype(BF16), spread) * near_x).astype(BF16)
            tall = jnp.concatenate([p] * members, axis=0)
            small[0, j] = (mm(tall.astype(BF16), repeat) * same_k).astype(BF16)

    def mix_pair(k):
        both = jnp.concatenate(
            [ctl[k * block:(k + 1) * block, :], ctl[(k + 1) * block:(k + 2) * block, :]], axis=1
        )
        wide[k // 2] = dot3((mats[0, 0], mats[0, 1]), both)

    with mark("mix_first"):
        ctl_loads[0].wait()
        mix_pair(0)
    with mark("w_ctl"):
        for load in ctl_loads[1:]:
            load.wait()
    for side, x in ((0, width - 1), (1, 0)):
        v = ctl[pl.ds(x, kl, stride=width), :]
        ex = exponent([v], ny)
        ctl_stage[side, pl.ds(0, kl)] = encode(v, ex)
        ctl_stage[side, pl.ds(kl, PACK)] = jnp.broadcast_to(ex, (PACK, ny)).astype(I32).astype(I16)

    with mark("w_barrier"):
        count = n_mem - 1 + n_mem * (jnp.where(t > 0, 1, 0) + jnp.where(t < n_tile - 1, 1, 0))
        pl.semaphore_wait(pltpu.get_barrier_semaphore(), count)

    start_sides((CTL,))

    with mark("mix_a0"):
        for k in range(2, members, 2):
            mix_pair(k)
        for k in range(members):
            work[pl.ds(k * block, block), :] = smooth_y(wide[k // 2, :, (k % 2) * ny:(k % 2 + 1) * ny])

    with mark("stage"):
        for load in late_loads:
            load.wait()
        for side, at in ((0, pl.ds(width - HALO, HALO)), (1, pl.ds(0, HALO))):
            surf_stage[side, pl.ds(0, HALO)] = wind[at, :]
            surf_stage[side, pl.ds(HALO, HALO)] = codes[at, :].astype(F32)
            for c in range(cuts):
                surf_stage[side, pl.ds(2 * HALO + c, 1)] = cell[:, c * ny:(c + 1) * ny].astype(F32)
        start_sides((SURF, OBS))

    def member_edges():
        for k in range(members):
            ensf[pl.ds(k * rows * width, rows * width), :] = ens[k].astype(F32).reshape(rows * width, ny)
        for i in (0, 1):
            ens_stage[0, i] = ensf[pl.ds(width - 1 - i, members * rows, stride=width), :].astype(BF16)
            ens_stage[1, i] = ensf[pl.ds(i, members * rows, stride=width), :].astype(BF16)

    def send_edges():
        near_rows = [
            whole_number(ctl_halo[side, pl.ds(0, kl)]) * unit(ctl_halo[side, pl.ds(kl, PACK)]) for side in (0, 1)
        ]
        sides = 0.25 * dot3((small[0, 0], small[0, 1]), jnp.concatenate(near_rows, axis=1))
        for j in (0, 1):
            a = smooth_y(sides[:, j * ny:(j + 1) * ny]).reshape(members, 1, levels, ny)
            p = ens_stage[1 - j, 0].astype(F32).reshape(members, V, levels, ny) * a
            total = jnp.sum(p, axis=0).reshape(rows, ny)
            for i in range(n_mem):
                edge_src[i, j] = total[i * share:(i + 1) * share]
        for d in peers:
            who = m ^ d
            to_mem(d, edge_src.at[who], edge_main.at[d - 1], sent.at[2], edge_recv.at[2]).start()

        def start(side):
            for d in (*peers, 0):
                to_side(
                    side, d, edge_src.at[m ^ d, 1 - side], edge_halo.at[side, d], sent.at[side], edge_recv.at[side]
                ).start()

        both_sides(start)

    def wait_edges():
        wait_all(edge_main, edge_recv.at[2])
        for side in (0, 1):
            @pl.when(has[side])
            def _():
                wait_all(edge_halo.at[side], edge_recv.at[side])

    def add_edges(p):
        rows_of = pl.ds(p * sp, sp)
        for j, x, out in ((0, 0, -1), (1, width - 1, width)):
            v = edge_src[m, j, rows_of]
            for d in range(n_mem - 1):
                v = v + edge_main[d, j, rows_of]
            at = pl.ds((reach + x) * sp, sp)
            inc[0, p, at] = inc[0, p, at] + v
            v = edge_halo[j, 0, rows_of]
            for d in range(1, n_mem):
                v = v + edge_halo[j, d, rows_of]
            at = pl.ds((reach + out) * sp, sp)
            inc[0, p, at] = inc[0, p, at] + v

    def halo_cells(side):
        return jnp.concatenate([surf_halo[side, pl.ds(2 * HALO + c, 1)] for c in range(cuts)], axis=1).astype(I32)

    def coefficients():
        code = jnp.concatenate(
            [surf_halo[0, pl.ds(HALO, HALO)], codes[...].astype(F32), surf_halo[1, pl.ds(HALO, HALO)]], axis=0
        )
        speed = jnp.concatenate([surf_halo[0, pl.ds(0, HALO)], wind[...], surf_halo[1, pl.ds(0, HALO)]], axis=0)
        opened = (code != 1.0).astype(F32)
        absorb = jnp.where(code == 2.0, absorbing, 1.0).astype(F32)
        yy = iota(code.shape, 1)
        west = lambda v: pltpu.roll(v, 1, 0)
        east = lambda v: pltpu.roll(v, n - 1, 0)
        south = lambda v: pltpu.roll(v, 1, 1)
        north = lambda v: pltpu.roll(v, ny - 1, 1)
        oe = opened * east(opened)
        ow = opened * west(opened)
        on = jnp.where(yy < ny - 1, opened * north(opened), 0.0)
        os = jnp.where(yy > 0, opened * south(opened), 0.0)
        k = diffusion_rate
        center = 1.0 - k * (oe + ow + on + os) - speed * oe
        every = (
            absorb * center, absorb * (k + west(speed)) * ow, absorb * k * oe, absorb * k * os, absorb * k * on,
            center * absorb, k * ow * west(absorb), (k + speed) * oe * east(absorb),
            k * os * south(absorb), k * on * north(absorb),
        )
        for i, v in enumerate(every):
            thin[i] = v
            for r in range(sp):
                coef[i, pl.ds(r, across, stride=sp), :] = thin[i, pl.ds(HALO - reach, across), :]

    def stencil(q, which):
        size = across * sp
        return (
            coef[which] * q
            + coef[which + 1] * pltpu.roll(q, sp, 0)
            + coef[which + 2] * pltpu.roll(q, size - sp, 0)
            + coef[which + 3] * pltpu.roll(q, 1, 1)
            + coef[which + 4] * pltpu.roll(q, ny - 1, 1)
        )

    def copy_seen(i, values):
        for p in range(parts):
            for c in range(copies):
                at = pl.ds(c * sp, sp)
                seen[i, p, 0, at] = values[0, pl.ds(p * sp, sp), :]
                seen[i, p, 1, at] = 1.0 / values[1, pl.ds(p * sp, sp), :]

    def observe(state, p):
        tiles = (
            (halo_cells(0), 0, reach, width - reach),
            (cell[...], reach, width, 0),
            (halo_cells(1), reach + width, reach, 0),
        )
        pieces = []
        for i, (where, at, count, offset) in enumerate(tiles):
            hot_y = hot[i]
            lines = count * sp
            shape = (lines // deep, deep, nobs)
            place = jnp.broadcast_to(where >> ys, (deep, nobs)) - offset
            hit = place[None] == ((iota(shape, 0) * deep + iota(shape, 1)) >> log2(sp))
            hi, low = split(state[at * sp:at * sp + lines])
            got = mm(jnp.concatenate([hi, low], axis=0), hot_y)
            some = jnp.sum(jnp.where(hit, (got[:lines] + got[lines:]).reshape(shape), 0.0), axis=0)
            sampled = some
            for c in range(1, copies):
                sampled = sampled + pltpu.roll(some, c * sp, 0)
            weight = jnp.clip((sampled - seen[i, p, 0]) * seen[i, p, 1], -huber_delta, huber_delta) * seen[i, p, 1]
            put = [
                jnp.where(hit, w.astype(F32)[None], 0.0).reshape(lines, nobs).astype(BF16) for w in split(weight)
            ]
            both = lax.dot_general(jnp.concatenate(put, axis=0), hot_y, NT, preferred_element_type=F32)
            pieces.append(both[:lines] + both[lines:])
        return jnp.concatenate(pieces, axis=0)

    def short(x):
        return x.astype(I32).astype(I16)

    def members_sum(e, p):
        for d in (*peers, 0):
            who = m ^ d
            r0 = who * share + p * sp
            l0 = lax.rem(r0, levels)
            total = jnp.zeros((sp, width, ny), F32)
            for k in range(members):
                a = work[pl.ds(pl.multiple_of(k * block + l0 * width, width), sp * width), :]
                total += ens[k, pl.ds(r0, sp)].astype(F32) * a.reshape(sp, width, ny)
            tot[p, d] = total.reshape(inner_rows, ny)
            ex = exponent([total], ny)
            scale = jnp.exp2(-ex) * SPAN
            for x in range(width):
                stage[p, d, pl.ds(x * sp, sp), :] = tot[p, d, pl.ds(x, sp, stride=width), :]
            filler = jnp.broadcast_to(ex, (hb - data, ny))
            for first, at in ((0, 0), (inner_rows - data, hb + mb)):
                v = jnp.round(stage[p, d, pl.ds(first, data), :] * scale)
                rs_src[e, p, d, pl.ds(at, hb)] = short(jnp.concatenate([v, filler], axis=0))
            if mb:
                rs_src[e, p, d, pl.ds(hb, mb)] = short(jnp.round(stage[p, d, pl.ds(data, mb), :] * scale))
    def send_sum(e, p):
        for d in peers:
            to_mem(d, rs_src.at[e, p, d], rs_main.at[e, p, d - 1], sent.at[2], rs_recv.at[e, p, 2]).start()

        def start(side):
            at = pl.multiple_of((1 - side) * (hb + mb), PACK)
            for d in (*peers, 0):
                to_side(
                    side, d, rs_src.at[e, p, d, pl.ds(at, hb)], rs_halo.at[e, p, side, d],
                    sent.at[side], rs_recv.at[e, p, side],
                ).start()

        both_sides(start)

    def gather_sum(e, p):
        wait_all(rs_main.at[e, p], rs_recv.at[e, p, 2])
        for side in (0, 1):
            @pl.when(has[side])
            def _():
                wait_all(rs_halo.at[e, p, side], rs_recv.at[e, p, side])
        bounds = ((0, data, 0, hb), (data, mb, hb, mb), (inner_rows - data, data, hb + mb, hb))
        pieces = [stage[p, 0, pl.ds(at, count), :] if count else None for at, count, _, _ in bounds]
        for d in range(n_mem - 1):
            u = None
            for i, (_, count, at, size) in enumerate(bounds):
                if count:
                    v = whole_number(rs_main[e, p, d, pl.ds(at, size)])
                    u = jnp.exp2(v[data:data + 1]) * (1.0 / SPAN) if u is None else u
                    pieces[i] = pieces[i] + (v * u)[:count]
        outer = []
        for side in (0, 1):
            total = None
            for d in range(n_mem):
                v = whole_number(rs_halo[e, p, side, d])
                v = v * (jnp.exp2(v[data:data + 1]) * (1.0 / SPAN))
                total = v if total is None else total + v
            outer.append(total[:data])
        at = 0
        for v in (outer[0], *pieces, outer[1]):
            if v is not None:
                inc[e, p, pl.ds(at, v.shape[0])] = v
                at += v.shape[0]

    def observation_term(e, some, fields):
        ag = (ag0, ag1)[e]
        margin = margin_of(e, sp)
        for i in range(STEPS):
            fields = [stencil(q, 0) for q in fields]
        with mark("observe"):
            fields = [observe(q, p) for p, q in zip(some, fields)]
        for i in range(STEPS):
            fields = [stencil(q, 5) for q in fields]
        lines = (-1, width) + ((-2, width + 1) if e == 0 else ())
        used = len(lines) * sp
        for p, q in zip(some, fields):
            turned[p] = q
            ex = exponent([turned[p, pl.ds((reach - 2) * sp, (width + 4) * sp), :]], ny)
            scale = jnp.exp2(-ex) * SPAN
            for i, x in enumerate(lines):
                fringe[p, pl.ds(i * sp, sp), :] = jnp.round(turned[p, pl.ds((reach + x) * sp, sp), :] * scale)
            fringe[p, pl.ds(used, margin - used), :] = jnp.broadcast_to(ex, (margin - used, ny))
            for r in range(sp):
                v = turned[p, pl.ds(reach * sp + r, width, stride=sp), :]
                ag[p, m, pl.ds(r * width, width)] = short(jnp.round(v * scale))
            ag[p, m, pl.ds(inner_rows, margin)] = short(fringe[p, pl.ds(0, margin), :])
        for p in some:
            for d in peers:
                to_mem(d, ag.at[p, m], ag.at[p, m], sent.at[2], ag_recv.at[e, p]).start()

    def adjoint_rows(e, p):
        ag = (ag0, ag1)[e]
        margin = margin_of(e, sp)
        wait_all(ag.at[p, pl.ds(0, n_mem - 1)], ag_recv.at[e, p])
        for i in range(n_mem):
            v = whole_number(ag[p, i, pl.ds(inner_rows, margin)])
            u = jnp.exp2(v[margin - 1:margin]) * (1.0 / SPAN)
            at = i * share + p * sp
            adj_out[pl.ds(at * width, inner_rows), :] = whole_number(ag[p, i, pl.ds(0, inner_rows)]) * u
            fringes[p, i, pl.ds(0, margin)] = v * u
            for j in range(4 - 2 * e):
                marks_all[j, pl.ds(at, sp), :] = fringes[p, i, pl.ds(j * sp, sp), :]

    def edge_terms(e):
        terms = []
        for j in range(4 - 2 * e):
            v = ens_halo[j % 2, j // 2].astype(F32).reshape(members, rows, ny) * marks_all[j][None]
            terms.append((v[:, :levels] + v[:, levels:]).reshape(kl, ny))
        return terms

    def pair_term(k, p):
        return member_pair(ensf, adj_out, levels, width, share, k, p)

    with mark("part0"):
        members_sum(0, 0)
        send_sum(0, 0)
        for p in range(1, parts):
            members_sum(0, p)
    with mark("member_edges"):
        member_edges()
    with mark("w_ctlhalo"):
        recv_sides((CTL,))
    with mark("edges"):
        send_edges()
        for p in range(1, parts):
            send_sum(0, p)
    with mark("hidden"):
        pick = (lev((block, levels), 0, xs) == iota((block, levels), 1)).astype(F32)
        both = nt(lo, lo)
        xi = iota((block, levels), 0) & (width - 1)
        at_x = lambda v, *marks: v * sum(jnp.where(xi == x, c, 0.0).astype(F32) for x, c in marks)
        last = width - 1
        high = jnp.dot(pick, both, precision=HIGHEST, preferred_element_type=F32)
        columns = block // parts
        ci = iota((columns, levels), 0)
        level = ((ci >> log2(inner_rows)) << log2(share)) + ((ci & (inner_rows - 1)) >> xs)
        far_x = gap((block, columns), width - 1)
        far_x = jnp.where(far_x == 0, 0.375, jnp.where(far_x == 1, 0.25, jnp.where(far_x == 2, 0.0625, 0.0)))
        xr, xc = iota((block, columns), 0) & (width - 1), iota((block, columns), 1) & (width - 1)
        for side, x in ((0, 0), (1, last)):
            lost = jnp.where(has[side], 0.0, 0.0625).astype(F32)
            far_x = far_x - jnp.where((xr == x) & (xc == x), lost, 0.0)
        outer = jnp.concatenate([
            at_x(high, (0, 0.25), (1, 0.0625)), at_x(high, (last, 0.25), (last - 1, 0.0625)),
            at_x(high, (0, 0.0625)), at_x(high, (last, 0.0625)),
        ], axis=1)
        for p in range(parts):
            own_pick = (level + p * sp == iota((columns, levels), 1)).astype(F32)
            tables[p][...] = tripled(nt(high, own_pick) * far_x, outer if p == parts - 1 else None)
        high = nt(pick, lo)
        near_x = gap((block, columns), width - 1)
        near_x = jnp.where(near_x == 0, 0.5, jnp.where(near_x == 1, 0.25, 0.0)).astype(F32)
        outer = jnp.concatenate([at_x(high, (0, 0.25)), at_x(high, (last, 0.25))], axis=1)
        for p in range(parts):
            own_pick = (level + p * sp == iota((columns, levels), 1)).astype(F32)
            finals[p][...] = tripled(nt(high, own_pick) * near_x, outer if p == parts - 1 else None)
        yr, yc = iota((2 * ny, 2 * ny), 0), iota((2 * ny, 2 * ny), 1)
        far_y = jnp.abs(yr - yc)
        corner = (yr & (ny - 1) == 0) | (yr & (ny - 1) == ny - 1)
        far_y = jnp.where(
            far_y == 0, jnp.where(corner, 0.3125, 0.375),
            jnp.where(far_y == 1, 0.25, jnp.where(far_y == 2, 0.0625, 0.0)),
        )
        blur2[...] = jnp.where((yr >> ys) == (yc >> ys), far_y, 0.0).astype(BF16)
        recv_sides((SURF,))
        copy_seen(1, obs)
        for i, where in enumerate((halo_cells(0), cell[...], halo_cells(1))):
            hot[i] = (iota((ny, nobs), 0) == (where & (ny - 1))).astype(BF16)
        coefficients()
        start_sides((ENS,))
    for p in range(parts):
        with mark(f"w_rs0_{p}"):
            gather_sum(0, p)
        if p == 0:
            with mark("w_obs"):
                recv_sides((OBS,))
                for side in (0, 1):
                    copy_seen(2 * side, obs_halo.at[side])
            with mark("w_edge"):
                wait_edges()
        with mark(f"obs0_{p}"):
            add_edges(p)
            observation_term(0, [p], [inc[0, p]])
    with mark("w_ens"):
        recv_sides((ENS,))
    for p in range(parts - 1):
        with mark(f"w_ag0_{p}"):
            adjoint_rows(0, p)
        with mark(f"mix1_{p}"):
            for k in range(0, members, 2):
                v = mixed(tables[p][...], pair_term(k, p), None)
                wide[k // 2] = v if p == 0 else wide[k // 2] + v
    with mark("w_ag0"):
        adjoint_rows(0, parts - 1)
        terms = edge_terms(0)
    with mark("mix1"):
        def blur(v):
            hi, low = split(v)
            return mm(jnp.concatenate([hi, low], axis=1), jnp.concatenate([blur2[...], blur2[...]], axis=0))

        for k in range(0, members, 2):
            v = mixed(tables[parts - 1][...], pair_term(k, parts - 1), side_by_side(terms, k, levels))
            wide[k // 2] = v if parts == 1 else wide[k // 2] + v
        for k in range(0, members, 2):
            done = blur(wide[k // 2])
            work[k * block:(k + 1) * block, :] = done[:, :ny]
            work[(k + 1) * block:(k + 2) * block, :] = done[:, ny:]
    with mark("part1"):
        for p in range(parts):
            members_sum(1, p)
            send_sum(1, p)
    for p in range(parts):
        with mark(f"w_rs1_{p}"):
            gather_sum(1, p)
        with mark(f"obs1_{p}"):
            observation_term(1, [p], [step_length * (inc[0, p] - inc[1, p])])
    for p in range(parts - 1):
        with mark(f"w_ag1_{p}"):
            adjoint_rows(1, p)
        with mark(f"mix2_{p}"):
            for k in range(0, members, 2):
                v = mixed(finals[p][...], pair_term(k, p), None)
                wide[k // 2] = v if p == 0 else wide[k // 2] + v
    with mark("term1"):
        adjoint_rows(1, parts - 1)
        terms = edge_terms(1)
        for side in (0, 1):
            edges_out[:, side * ny:(side + 1) * ny] = terms[side]
    with mark("drain"):
        size = lambda ref: math.prod(ref.shape) * ref.dtype.itemsize
        line = ny * 4
        total = size(rs_main) + size(edge_main) + (n_mem - 1) * (size(ag0) + size(ag1)) // n_mem
        wait_all(ensf.at[pl.ds(0, total // line)], sent.at[2])
        total = sum(size(ref) for ref in (rs_halo, edge_halo, ctl_halo, surf_halo, obs_halo, ens_halo)) // 2
        for side in (0, 1):
            @pl.when(has[1 - side])
            def _():
                wait_all(ensf.at[pl.ds(0, total // line)], sent.at[side])


def member_pair(ensf, adj, levels, width, share, k, p):
    block = levels * width
    _, sp = parts_of(share)

    def term(k):
        pieces = []
        for i in range(levels // share):
            at = (i * share + p * sp) * width
            low, high = pl.ds(at, sp * width), pl.ds(block + at, sp * width)
            base = 2 * k * block + at
            pieces.append(
                ensf[pl.ds(base, sp * width), :] * adj[low, :] + ensf[pl.ds(base + block, sp * width), :] * adj[high, :]
            )
        return jnp.concatenate(pieces, axis=0)

    return jnp.concatenate([term(k), term(k + 1)], axis=1)


def finish(members, levels, width, share, ny, ensf, adj, edges, wide, table, out, work, sem):
    block = levels * width
    parts, _ = parts_of(share)
    smooth_y = smoother(ny)
    terms = [edges[:, j * ny:(j + 1) * ny] for j in (0, 1)]
    for k in range(0, members, 2):
        done = mixed(
            table[...], member_pair(ensf, adj, levels, width, share, k, parts - 1), side_by_side(terms, k, levels)
        )
        if parts > 1:
            done = done + wide[k // 2]
        for i in (0, 1):
            at = pl.ds((k + i) * block, block)
            work[at, :] = smooth_y(done[:, i * ny:(i + 1) * ny])
            pltpu.make_async_copy(work.at[at], out.at[at], sem.at[0]).start()
    pltpu.make_async_copy(work, out, sem.at[0]).wait()


def body(n_mem, n_tile, ensemble, control, level_loc, wind_speed, cell_codes, obs_cell, innovation, obs_sigma):
    members, rows, width, ny = ensemble.shape
    levels = control.shape[1]
    assert width >= 2 * HALO and members % 2 == 0 and rows == 2 * levels
    nobs = obs_cell.shape[0]
    share = rows // n_mem
    kl = members * levels
    block = levels * width
    n = width + 2 * HALO
    vmem = pltpu.VMEM
    dma = pltpu.SemaphoreType.DMA
    parts, sp = parts_of(share)
    reach, data, hb, mb = blocks_of(sp, width)
    size = 2 * hb + mb
    tall = max(8, sp)
    margins = [margin_of(e, sp) for e in (0, 1)]
    surf = up(2 * HALO + nobs // ny, 8)
    scratch = [
        vmem((members, rows, width, ny), BF16),
        vmem((members * block, ny), F32),
        vmem((levels, levels), F32),
        vmem((width, ny), F32),
        vmem((width, ny), I32),
        vmem((1, nobs), I32),
        vmem((2, share, nobs), F32),
        dma((7 + members // 2,)),
        vmem((3, ny, nobs), BF16),
        vmem((members * block, ny), F32),
        vmem((1, 2, block, block), BF16),
        vmem((1, 2, kl, kl), BF16),
        vmem((block, up(3 * block // parts, 128)), BF16),
        vmem((block, up(3 * block // parts + 12 * levels, 128)), BF16),
        vmem((2 * ny, 2 * ny), BF16),
        vmem((10, (width + 2 * reach) * sp, ny), F32),
        vmem((10, n, ny), F32),
        vmem((2, kl + PACK, ny), I16),
        vmem((2, kl + PACK, ny), I16),
        vmem((2, surf, ny), F32),
        vmem((2, surf, ny), F32),
        vmem((2, 2, share, nobs), F32),
        vmem((3, parts, 2, tall, nobs), F32),
        vmem((2, 2, members * rows, ny), BF16),
        vmem((2, 2, members * rows, ny), BF16),
        vmem((parts, n_mem, sp * width, ny), F32),
        vmem((parts, n_mem, sp * width, ny), F32),
        vmem((2, parts, n_mem, size, ny), I16),
        vmem((2, parts, n_mem - 1, size, ny), I16),
        vmem((2, parts, 2, n_mem, hb, ny), I16),
        vmem((2, parts, (width + 2 * reach) * sp, ny), F32),
        vmem((parts, (width + 2 * reach) * sp, ny), F32),
        vmem((parts, margins[0], ny), F32),
        vmem((parts, n_mem, margins[0], ny), F32),
        vmem((4, rows, ny), F32),
        *(vmem((parts, n_mem, sp * width + margins[e], ny), I16) for e in (0, 1)),
        vmem((n_mem, 2, share, ny), F32),
        vmem((n_mem - 1, 2, share, ny), F32),
        vmem((2, n_mem, share, ny), F32),
        vmem((block, up(3 * block // parts, 128)), BF16),
        dma((3,)), dma((2, 4)), dma((2, parts, 3)), dma((2, parts)), dma((3,)),
    ]
    whole = pl.BlockSpec(memory_space=pltpu.VMEM)
    hbm = pl.BlockSpec(memory_space=pltpu.HBM)
    handed = pl.pallas_call(
        functools.partial(kernel, n_mem, n_tile, members, levels, width, ny, nobs),
        out_shape=(
            vmem((members * rows * width, ny), F32), vmem((rows * width, ny), F32), vmem((kl, 2 * ny), F32),
            vmem((members // 2, block, 2 * ny), F32), vmem((block, up(3 * block // parts + 6 * levels, 128)), BF16),
        ),
        in_specs=[hbm] * 8,
        out_specs=(whole,) * 5,
        scratch_shapes=scratch,
        compiler_params=pltpu.CompilerParams(
            collective_id=0, has_side_effects=True, vmem_limit_bytes=40 << 20
        ),
    )(*(pltpu.with_memory_space_constraint(x, pltpu.HBM) for x in (
        ensemble,
        control.reshape(members * block, ny),
        level_loc,
        wind_speed,
        cell_codes,
        obs_cell.reshape(1, nobs),
        innovation.reshape(n_mem, share, nobs),
        obs_sigma.reshape(n_mem, share, nobs),
    )))
    result = pl.pallas_call(
        functools.partial(finish, members, levels, width, share, ny),
        out_shape=jax.ShapeDtypeStruct((members * block, ny), F32),
        in_specs=[whole] * 5,
        out_specs=hbm,
        scratch_shapes=[vmem((members * block, ny), F32), dma((1,))],
        compiler_params=pltpu.CompilerParams(vmem_limit_bytes=40 << 20),
    )(*(pltpu.with_memory_space_constraint(x, pltpu.VMEM) for x in handed))
    return result.reshape(members, levels, width, ny)


def solution(mesh):
    placed = (
        P("mem", None, "tile", None),
        P("mem", None, "tile", None),
        P(),
        P("tile", None),
        P("tile", None),
        P("tile"),
        P(None, "tile"),
        P(None, "tile"),
    )
    return jax.shard_map(
        functools.partial(body, mesh.shape["mem"], mesh.shape["tile"]),
        mesh=mesh, in_specs=placed, out_specs=P("mem", None, "tile", None), check_vma=False,
    )
```

```python
import contextlib
import functools
import math

import jax
import jax.numpy as jnp
from jax import lax
from jax.experimental import pallas as pl
from jax.experimental.pallas import tpu as pltpu
from jax.sharding import PartitionSpec as P

V = 2
STEPS = 2
HALO = 8
PACK = 16
SPAN = 32760.0

diffusion_rate = 0.12
absorbing = 0.7
step_length = 0.5
huber_delta = 1.0

MESH = pl.DeviceIdType.MESH
F32 = jnp.float32
BF16 = jnp.bfloat16
I16 = jnp.int16
I32 = jnp.int32
HIGHEST = lax.Precision.HIGHEST
NT = (((1,), (1,)), ((), ()))
mark = contextlib.nullcontext


def log2(n):
    assert n & (n - 1) == 0
    return n.bit_length() - 1


def iota(shape, dim):
    return lax.broadcasted_iota(I32, shape, dim)


def split(x):
    hi = x.astype(BF16)
    return hi, (x - hi.astype(F32)).astype(BF16)


def mm(a, b):
    return jnp.dot(a, b, preferred_element_type=F32)


def nt(a, b):
    return lax.dot_general(a, b, NT, precision=HIGHEST, preferred_element_type=F32)


def dot3(a, b):
    ah, al = a
    bh, bl = split(b)
    return mm(jnp.concatenate([ah, ah, al], axis=1), jnp.concatenate([bh, bl, bh], axis=0))


def tripled(a, outer):
    pieces = []
    for v in (a, outer):
        if v is not None:
            hi, low = split(v)
            pieces += [hi, hi, low]
    used = sum(v.shape[1] for v in pieces)
    spare = up(used, 128) - used
    if spare:
        pieces.append(jnp.zeros((a.shape[0], spare), BF16))
    return jnp.concatenate(pieces, axis=1)


def mixed(table, b, outer):
    pieces = []
    for v in (b, outer):
        if v is not None:
            hi, low = split(v)
            pieces += [hi, low, hi]
    used = sum(v.shape[0] for v in pieces)
    spare = up(used, 128) - used
    if spare:
        pieces.append(jnp.zeros((spare, b.shape[1]), BF16))
    return mm(table, jnp.concatenate(pieces, axis=0))


def side_by_side(terms, k, levels):
    return jnp.concatenate(
        [jnp.concatenate([v[(k + i) * levels:(k + i + 1) * levels] for v in terms], axis=0) for i in (0, 1)], axis=1
    )


def up(n, to):
    return -(-n // to) * to


def parts_of(share):
    parts = 2 if share % 8 == 0 else 1
    return parts, share // parts


def blocks_of(part, width):
    least = 2 * STEPS + 2
    reach = least if least * part % 8 == 0 else HALO
    data = reach * part
    return reach, data, up(data + 1, PACK), up(width * part - 2 * data, PACK)


def margin_of(e, part):
    return up((4 - 2 * e) * part + 1, PACK)


def wait_all(ref, sem):
    pltpu.make_async_copy(ref, ref, sem).wait()


def smoother(ny):
    yi = iota((1, ny), 1)
    from_south = jnp.where(yi > 0, 0.25, 0.0).astype(F32)
    from_north = jnp.where(yi < ny - 1, 0.25, 0.0).astype(F32)

    def smooth_y(v):
        return 0.5 * v + (from_south * pltpu.roll(v, 1, 1) + from_north * pltpu.roll(v, ny - 1, 1))

    return smooth_y


def exponent(parts, ny):
    most = None
    for p in parts:
        v = jnp.max(jnp.abs(p.reshape(-1, ny)), axis=0, keepdims=True)
        most = v if most is None else jnp.maximum(most, v)
    return jnp.floor(jnp.log2(jnp.maximum(most, 1e-30))) + 1.0


def encode(x, e):
    return jnp.round(x * (jnp.exp2(-e) * SPAN)).astype(I32).astype(I16)


def whole_number(q):
    return q.astype(I32).astype(F32)


def unit(code):
    return jnp.exp2(whole_number(code)[0:1]) * (1.0 / SPAN)


def kernel(
    n_mem, n_tile, members, levels, width, ny, nobs,
    ens_hbm, ctl_hbm, loc_hbm, wind_hbm, codes_hbm, cell_hbm, innov_hbm, sigma_hbm,
    ensf, adj_out, edges_out, wide, final_b,
    ens, ctl, loc, wind, codes, cell, obs, in_sem, hot,
    work, mats, small, table_a, table_b, blur2, coef, thin,
    ctl_stage, ctl_halo, surf_stage, surf_halo, obs_halo, seen, ens_stage, ens_halo,
    tot, stage, rs_src, rs_main, rs_halo, inc,
    turned, fringe, fringes, marks_all, ag0, ag1, edge_src, edge_main, edge_halo, final_a,
    sent, r0_recv, rs_recv, ag_recv, edge_recv,
):
    m = lax.axis_index("mem")
    t = lax.axis_index("tile")
    has = (t > 0, t < n_tile - 1)
    rows = V * levels
    share = rows // n_mem
    block = levels * width
    kl = members * levels
    xs, ys = log2(width), log2(ny)
    n = HALO + width + HALO
    parts, sp = parts_of(share)
    reach, data, hb, mb = blocks_of(sp, width)
    across = width + 2 * reach
    copies = max(8 // sp, 1)
    deep = sp * copies
    tables, finals = (table_a, table_b)[2 - parts:], (final_a, final_b)[2 - parts:]
    cuts = nobs // ny
    assert 1 << log2(n_mem) == n_mem
    peers = range(n_mem - 1, 0, -1)
    outward = 1 - (t & 1)
    inner_rows = sp * width

    def tell(dev):
        pl.semaphore_signal(pltpu.get_barrier_semaphore(), inc=1, device_id=dev, device_id_type=MESH)

    for d in peers:
        tell((m ^ d, t))

    @pl.when(has[0])
    def _():
        for d in range(n_mem):
            tell((m ^ d, t - 1))

    @pl.when(has[1])
    def _():
        for d in range(n_mem):
            tell((m ^ d, t + 1))

    loads = [
        pltpu.make_async_copy(src, dst, in_sem.at[i])
        for i, (src, dst) in enumerate((
            (loc_hbm, loc),
            *((ctl_hbm.at[at], ctl.at[at]) for at in (pl.ds(0, 2 * block), pl.ds(2 * block, (members - 2) * block))),
            (ens_hbm, ens), (wind_hbm, wind), (codes_hbm, codes),
            (cell_hbm, cell), (innov_hbm.at[m], obs.at[0]), (sigma_hbm.at[m], obs.at[1]),
        ))
    ]
    for load in loads:
        load.start()

    def to_side(side, d, src, dst, ssem, rsem):
        dev = (m ^ d, t + 1 - 2 * side)
        return pltpu.make_async_remote_copy(
            src_ref=src, dst_ref=dst, send_sem=ssem, recv_sem=rsem, device_id=dev, device_id_type=MESH
        )

    def to_mem(d, src, dst, ssem, rsem):
        return pltpu.make_async_remote_copy(
            src_ref=src, dst_ref=dst, send_sem=ssem, recv_sem=rsem,
            device_id=(m ^ d, t), device_id_type=MESH,
        )

    ctl_loads, late_loads = loads[1:3], loads[3:]
    def both_sides(start):
        for s in (outward, 1 - outward):
            dev = t + 1 - 2 * s

            @pl.when((dev >= 0) & (dev < n_tile))
            def _():
                start(s)

    CTL, SURF, OBS, ENS = range(4)
    def first_msg(side, i):
        s, d = (
            (ctl_stage.at[side], ctl_halo.at[side]),
            (surf_stage.at[side], surf_halo.at[side]),
            (obs, obs_halo.at[side]),
            (ens_stage.at[side], ens_halo.at[side]),
        )[i]
        return to_side(side, 0, s, d, sent.at[side], r0_recv.at[side, i])

    def start_sides(which):
        def start(side):
            for i in which:
                first_msg(side, i).start()

        both_sides(start)

    def recv_sides(which):
        for side in (0, 1):
            @pl.when(has[side])
            def _():
                for i in which:
                    first_msg(side, i).wait_recv()

    for side in (0, 1):
        @pl.when(jnp.logical_not(has[side]))
        def _():
            ctl_halo[side] = jnp.zeros_like(ctl_halo[side])
            surf_halo[side, pl.ds(0, HALO)] = jnp.zeros((HALO, ny), F32)
            surf_halo[side, pl.ds(HALO, HALO)] = jnp.ones((HALO, ny), F32)
            surf_halo[side, pl.ds(2 * HALO, cuts)] = jnp.full((cuts, ny), -1.0, F32)
            obs_halo[side, 0] = jnp.zeros((share, nobs), F32)
            obs_halo[side, 1] = jnp.ones((share, nobs), F32)
            ens_halo[side] = jnp.zeros_like(ens_halo[side])
            edge_halo[side] = jnp.zeros_like(edge_halo[side])
            for e in (0, 1):
                for p in range(parts):
                    rs_halo[e, p, side] = jnp.zeros_like(rs_halo[e, p, side])

    smooth_y = smoother(ny)
    gap = lambda shape, mask: jnp.abs((iota(shape, 0) & mask) - (iota(shape, 1) & mask))
    lev = lambda shape, dim, shift: iota(shape, dim) >> shift

    with mark("w_loc"):
        loads[0].wait()
    with mark("mats0"):
        lo = loc[...]
        spread = (lev((levels, block), 1, xs) == iota((levels, block), 0)).astype(BF16)
        repeat = ((iota((levels, kl), 1) & (levels - 1)) == iota((levels, kl), 0)).astype(BF16)
        near_x = gap((block, block), width - 1)
        near_x = jnp.where(near_x == 0, 0.5, jnp.where(near_x == 1, 0.25, 0.0)).astype(F32)
        same_k = (lev((kl, kl), 0, log2(levels)) == lev((kl, kl), 1, log2(levels))).astype(F32)
        for j, piece in enumerate(split(lo)):
            p = piece.astype(F32)
            tall = jnp.broadcast_to(p[:, None, :], (levels, width, levels)).reshape(block, levels)
            mats[0, j] = (mm(tall.astype(BF16), spread) * near_x).astype(BF16)
            tall = jnp.concatenate([p] * members, axis=0)
            small[0, j] = (mm(tall.astype(BF16), repeat) * same_k).astype(BF16)

    def mix_pair(k):
        both = jnp.concatenate(
            [ctl[k * block:(k + 1) * block, :], ctl[(k + 1) * block:(k + 2) * block, :]], axis=1
        )
        wide[k // 2] = dot3((mats[0, 0], mats[0, 1]), both)

    with mark("mix_first"):
        ctl_loads[0].wait()
        mix_pair(0)
    with mark("w_ctl"):
        for load in ctl_loads[1:]:
            load.wait()
    for side, x in ((0, width - 1), (1, 0)):
        v = ctl[pl.ds(x, kl, stride=width), :]
        ex = exponent([v], ny)
        ctl_stage[side, pl.ds(0, kl)] = encode(v, ex)
        ctl_stage[side, pl.ds(kl, PACK)] = jnp.broadcast_to(ex, (PACK, ny)).astype(I32).astype(I16)

    with mark("w_barrier"):
        count = n_mem - 1 + n_mem * (jnp.where(t > 0, 1, 0) + jnp.where(t < n_tile - 1, 1, 0))
        pl.semaphore_wait(pltpu.get_barrier_semaphore(), count)

    start_sides((CTL,))

    with mark("mix_a0"):
        for k in range(2, members, 2):
            mix_pair(k)
        for k in range(members):
            work[pl.ds(k * block, block), :] = smooth_y(wide[k // 2, :, (k % 2) * ny:(k % 2 + 1) * ny])

    with mark("stage"):
        for load in late_loads:
            load.wait()
        for side, at in ((0, pl.ds(width - HALO, HALO)), (1, pl.ds(0, HALO))):
            surf_stage[side, pl.ds(0, HALO)] = wind[at, :]
            surf_stage[side, pl.ds(HALO, HALO)] = codes[at, :].astype(F32)
            for c in range(cuts):
                surf_stage[side, pl.ds(2 * HALO + c, 1)] = cell[:, c * ny:(c + 1) * ny].astype(F32)
        start_sides((SURF, OBS))

    def member_edges():
        for k in range(members):
            ensf[pl.ds(k * rows * width, rows * width), :] = ens[k].astype(F32).reshape(rows * width, ny)
        for i in (0, 1):
            ens_stage[0, i] = ensf[pl.ds(width - 1 - i, members * rows, stride=width), :].astype(BF16)
            ens_stage[1, i] = ensf[pl.ds(i, members * rows, stride=width), :].astype(BF16)

    def send_edges():
        near_rows = [
            whole_number(ctl_halo[side, pl.ds(0, kl)]) * unit(ctl_halo[side, pl.ds(kl, PACK)]) for side in (0, 1)
        ]
        sides = 0.25 * dot3((small[0, 0], small[0, 1]), jnp.concatenate(near_rows, axis=1))
        for j in (0, 1):
            a = smooth_y(sides[:, j * ny:(j + 1) * ny]).reshape(members, 1, levels, ny)
            p = ens_stage[1 - j, 0].astype(F32).reshape(members, V, levels, ny) * a
            total = jnp.sum(p, axis=0).reshape(rows, ny)
            for i in range(n_mem):
                edge_src[i, j] = total[i * share:(i + 1) * share]
        for d in peers:
            who = m ^ d
            to_mem(d, edge_src.at[who], edge_main.at[d - 1], sent.at[2], edge_recv.at[2]).start()

        def start(side):
            for d in (*peers, 0):
                to_side(
                    side, d, edge_src.at[m ^ d, 1 - side], edge_halo.at[side, d], sent.at[side], edge_recv.at[side]
                ).start()

        both_sides(start)

    def wait_edges():
        wait_all(edge_main, edge_recv.at[2])
        for side in (0, 1):
            @pl.when(has[side])
            def _():
                wait_all(edge_halo.at[side], edge_recv.at[side])

    def add_edges(p):
        rows_of = pl.ds(p * sp, sp)
        for j, x, out in ((0, 0, -1), (1, width - 1, width)):
            v = edge_src[m, j, rows_of]
            for d in range(n_mem - 1):
                v = v + edge_main[d, j, rows_of]
            at = pl.ds((reach + x) * sp, sp)
            inc[0, p, at] = inc[0, p, at] + v
            v = edge_halo[j, 0, rows_of]
            for d in range(1, n_mem):
                v = v + edge_halo[j, d, rows_of]
            at = pl.ds((reach + out) * sp, sp)
            inc[0, p, at] = inc[0, p, at] + v

    def halo_cells(side):
        return jnp.concatenate([surf_halo[side, pl.ds(2 * HALO + c, 1)] for c in range(cuts)], axis=1).astype(I32)

    def coefficients():
        code = jnp.concatenate(
            [surf_halo[0, pl.ds(HALO, HALO)], codes[...].astype(F32), surf_halo[1, pl.ds(HALO, HALO)]], axis=0
        )
        speed = jnp.concatenate([surf_halo[0, pl.ds(0, HALO)], wind[...], surf_halo[1, pl.ds(0, HALO)]], axis=0)
        opened = (code != 1.0).astype(F32)
        absorb = jnp.where(code == 2.0, absorbing, 1.0).astype(F32)
        yy = iota(code.shape, 1)
        west = lambda v: pltpu.roll(v, 1, 0)
        east = lambda v: pltpu.roll(v, n - 1, 0)
        south = lambda v: pltpu.roll(v, 1, 1)
        north = lambda v: pltpu.roll(v, ny - 1, 1)
        oe = opened * east(opened)
        ow = opened * west(opened)
        on = jnp.where(yy < ny - 1, opened * north(opened), 0.0)
        os = jnp.where(yy > 0, opened * south(opened), 0.0)
        k = diffusion_rate
        center = 1.0 - k * (oe + ow + on + os) - speed * oe
        every = (
            absorb * center, absorb * (k + west(speed)) * ow, absorb * k * oe, absorb * k * os, absorb * k * on,
            center * absorb, k * ow * west(absorb), (k + speed) * oe * east(absorb),
            k * os * south(absorb), k * on * north(absorb),
        )
        for i, v in enumerate(every):
            thin[i] = v
            for r in range(sp):
                coef[i, pl.ds(r, across, stride=sp), :] = thin[i, pl.ds(HALO - reach, across), :]

    def stencil(q, which):
        size = across * sp
        return (
            coef[which] * q
            + coef[which + 1] * pltpu.roll(q, sp, 0)
            + coef[which + 2] * pltpu.roll(q, size - sp, 0)
            + coef[which + 3] * pltpu.roll(q, 1, 1)
            + coef[which + 4] * pltpu.roll(q, ny - 1, 1)
        )

    def copy_seen(i, values):
        for p in range(parts):
            for c in range(copies):
                at = pl.ds(c * sp, sp)
                seen[i, p, 0, at] = values[0, pl.ds(p * sp, sp), :]
                seen[i, p, 1, at] = 1.0 / values[1, pl.ds(p * sp, sp), :]

    def observe(state, p):
        tiles = (
            (halo_cells(0), 0, reach, width - reach),
            (cell[...], reach, width, 0),
            (halo_cells(1), reach + width, reach, 0),
        )
        pieces = []
        for i, (where, at, count, offset) in enumerate(tiles):
            hot_y = hot[i]
            lines = count * sp
            shape = (lines // deep, deep, nobs)
            place = jnp.broadcast_to(where >> ys, (deep, nobs)) - offset
            hit = place[None] == ((iota(shape, 0) * deep + iota(shape, 1)) >> log2(sp))
            hi, low = split(state[at * sp:at * sp + lines])
            got = mm(jnp.concatenate([hi, low], axis=0), hot_y)
            some = jnp.sum(jnp.where(hit, (got[:lines] + got[lines:]).reshape(shape), 0.0), axis=0)
            sampled = some
            for c in range(1, copies):
                sampled = sampled + pltpu.roll(some, c * sp, 0)
            weight = jnp.clip((sampled - seen[i, p, 0]) * seen[i, p, 1], -huber_delta, huber_delta) * seen[i, p, 1]
            put = [
                jnp.where(hit, w.astype(F32)[None], 0.0).reshape(lines, nobs).astype(BF16) for w in split(weight)
            ]
            both = lax.dot_general(jnp.concatenate(put, axis=0), hot_y, NT, preferred_element_type=F32)
            pieces.append(both[:lines] + both[lines:])
        return jnp.concatenate(pieces, axis=0)

    def short(x):
        return x.astype(I32).astype(I16)

    def members_sum(e, p):
        for d in (*peers, 0):
            who = m ^ d
            r0 = who * share + p * sp
            l0 = lax.rem(r0, levels)
            total = jnp.zeros((sp, width, ny), F32)
            for k in range(members):
                a = work[pl.ds(pl.multiple_of(k * block + l0 * width, width), sp * width), :]
                total += ens[k, pl.ds(r0, sp)].astype(F32) * a.reshape(sp, width, ny)
            tot[p, d] = total.reshape(inner_rows, ny)
            ex = exponent([total], ny)
            scale = jnp.exp2(-ex) * SPAN
            for x in range(width):
                stage[p, d, pl.ds(x * sp, sp), :] = tot[p, d, pl.ds(x, sp, stride=width), :]
            filler = jnp.broadcast_to(ex, (hb - data, ny))
            for first, at in ((0, 0), (inner_rows - data, hb + mb)):
                v = jnp.round(stage[p, d, pl.ds(first, data), :] * scale)
                rs_src[e, p, d, pl.ds(at, hb)] = short(jnp.concatenate([v, filler], axis=0))
            if mb:
                rs_src[e, p, d, pl.ds(hb, mb)] = short(jnp.round(stage[p, d, pl.ds(data, mb), :] * scale))
    def send_sum(e, p):
        for d in peers:
            to_mem(d, rs_src.at[e, p, d], rs_main.at[e, p, d - 1], sent.at[2], rs_recv.at[e, p, 2]).start()

        def start(side):
            at = pl.multiple_of((1 - side) * (hb + mb), PACK)
            for d in (*peers, 0):
                to_side(
                    side, d, rs_src.at[e, p, d, pl.ds(at, hb)], rs_halo.at[e, p, side, d],
                    sent.at[side], rs_recv.at[e, p, side],
                ).start()

        both_sides(start)

    def gather_sum(e, p):
        wait_all(rs_main.at[e, p], rs_recv.at[e, p, 2])
        for side in (0, 1):
            @pl.when(has[side])
            def _():
                wait_all(rs_halo.at[e, p, side], rs_recv.at[e, p, side])
        bounds = ((0, data, 0, hb), (data, mb, hb, mb), (inner_rows - data, data, hb + mb, hb))
        pieces = [stage[p, 0, pl.ds(at, count), :] if count else None for at, count, _, _ in bounds]
        for d in range(n_mem - 1):
            u = None
            for i, (_, count, at, size) in enumerate(bounds):
                if count:
                    v = whole_number(rs_main[e, p, d, pl.ds(at, size)])
                    u = jnp.exp2(v[data:data + 1]) * (1.0 / SPAN) if u is None else u
                    pieces[i] = pieces[i] + (v * u)[:count]
        outer = []
        for side in (0, 1):
            total = None
            for d in range(n_mem):
                v = whole_number(rs_halo[e, p, side, d])
                v = v * (jnp.exp2(v[data:data + 1]) * (1.0 / SPAN))
                total = v if total is None else total + v
            outer.append(total[:data])
        at = 0
        for v in (outer[0], *pieces, outer[1]):
            if v is not None:
                inc[e, p, pl.ds(at, v.shape[0])] = v
                at += v.shape[0]

    def observation_term(e, some, fields):
        ag = (ag0, ag1)[e]
        margin = margin_of(e, sp)
        for i in range(STEPS):
            fields = [stencil(q, 0) for q in fields]
        with mark("observe"):
            fields = [observe(q, p) for p, q in zip(some, fields)]
        for i in range(STEPS):
            fields = [stencil(q, 5) for q in fields]
        lines = (-1, width) + ((-2, width + 1) if e == 0 else ())
        used = len(lines) * sp
        for p, q in zip(some, fields):
            turned[p] = q
            ex = exponent([turned[p, pl.ds((reach - 2) * sp, (width + 4) * sp), :]], ny)
            scale = jnp.exp2(-ex) * SPAN
            for i, x in enumerate(lines):
                fringe[p, pl.ds(i * sp, sp), :] = jnp.round(turned[p, pl.ds((reach + x) * sp, sp), :] * scale)
            fringe[p, pl.ds(used, margin - used), :] = jnp.broadcast_to(ex, (margin - used, ny))
            for r in range(sp):
                v = turned[p, pl.ds(reach * sp + r, width, stride=sp), :]
                ag[p, m, pl.ds(r * width, width)] = short(jnp.round(v * scale))
            ag[p, m, pl.ds(inner_rows, margin)] = short(fringe[p, pl.ds(0, margin), :])
        for p in some:
            for d in peers:
                to_mem(d, ag.at[p, m], ag.at[p, m], sent.at[2], ag_recv.at[e, p]).start()

    def adjoint_rows(e, p):
        ag = (ag0, ag1)[e]
        margin = margin_of(e, sp)
        wait_all(ag.at[p, pl.ds(0, n_mem - 1)], ag_recv.at[e, p])
        for i in range(n_mem):
            v = whole_number(ag[p, i, pl.ds(inner_rows, margin)])
            u = jnp.exp2(v[margin - 1:margin]) * (1.0 / SPAN)
            at = i * share + p * sp
            adj_out[pl.ds(at * width, inner_rows), :] = whole_number(ag[p, i, pl.ds(0, inner_rows)]) * u
            fringes[p, i, pl.ds(0, margin)] = v * u
            for j in range(4 - 2 * e):
                marks_all[j, pl.ds(at, sp), :] = fringes[p, i, pl.ds(j * sp, sp), :]

    def edge_terms(e):
        terms = []
        for j in range(4 - 2 * e):
            v = ens_halo[j % 2, j // 2].astype(F32).reshape(members, rows, ny) * marks_all[j][None]
            terms.append((v[:, :levels] + v[:, levels:]).reshape(kl, ny))
        return terms

    def pair_term(k, p):
        return member_pair(ensf, adj_out, levels, width, share, k, p)

    with mark("part0"):
        members_sum(0, 0)
        send_sum(0, 0)
        for p in range(1, parts):
            members_sum(0, p)
    with mark("member_edges"):
        member_edges()
    with mark("w_ctlhalo"):
        recv_sides((CTL,))
    with mark("edges"):
        send_edges()
        for p in range(1, parts):
            send_sum(0, p)
    with mark("hidden"):
        pick = (lev((block, levels), 0, xs) == iota((block, levels), 1)).astype(F32)
        both = nt(lo, lo)
        xi = iota((block, levels), 0) & (width - 1)
        at_x = lambda v, *marks: v * sum(jnp.where(xi == x, c, 0.0).astype(F32) for x, c in marks)
        last = width - 1
        high = jnp.dot(pick, both, precision=HIGHEST, preferred_element_type=F32)
        columns = block // parts
        ci = iota((columns, levels), 0)
        level = ((ci >> log2(inner_rows)) << log2(share)) + ((ci & (inner_rows - 1)) >> xs)
        far_x = gap((block, columns), width - 1)
        far_x = jnp.where(far_x == 0, 0.375, jnp.where(far_x == 1, 0.25, jnp.where(far_x == 2, 0.0625, 0.0)))
        xr, xc = iota((block, columns), 0) & (width - 1), iota((block, columns), 1) & (width - 1)
        for side, x in ((0, 0), (1, last)):
            lost = jnp.where(has[side], 0.0, 0.0625).astype(F32)
            far_x = far_x - jnp.where((xr == x) & (xc == x), lost, 0.0)
        outer = jnp.concatenate([
            at_x(high, (0, 0.25), (1, 0.0625)), at_x(high, (last, 0.25), (last - 1, 0.0625)),
            at_x(high, (0, 0.0625)), at_x(high, (last, 0.0625)),
        ], axis=1)
        for p in range(parts):
            own_pick = (level + p * sp == iota((columns, levels), 1)).astype(F32)
            tables[p][...] = tripled(nt(high, own_pick) * far_x, outer if p == parts - 1 else None)
        high = nt(pick, lo)
        near_x = gap((block, columns), width - 1)
        near_x = jnp.where(near_x == 0, 0.5, jnp.where(near_x == 1, 0.25, 0.0)).astype(F32)
        outer = jnp.concatenate([at_x(high, (0, 0.25)), at_x(high, (last, 0.25))], axis=1)
        for p in range(parts):
            own_pick = (level + p * sp == iota((columns, levels), 1)).astype(F32)
            finals[p][...] = tripled(nt(high, own_pick) * near_x, outer if p == parts - 1 else None)
        yr, yc = iota((2 * ny, 2 * ny), 0), iota((2 * ny, 2 * ny), 1)
        far_y = jnp.abs(yr - yc)
        corner = (yr & (ny - 1) == 0) | (yr & (ny - 1) == ny - 1)
        far_y = jnp.where(
            far_y == 0, jnp.where(corner, 0.3125, 0.375),
            jnp.where(far_y == 1, 0.25, jnp.where(far_y == 2, 0.0625, 0.0)),
        )
        blur2[...] = jnp.where((yr >> ys) == (yc >> ys), far_y, 0.0).astype(BF16)
        recv_sides((SURF,))
        copy_seen(1, obs)
        for i, where in enumerate((halo_cells(0), cell[...], halo_cells(1))):
            hot[i] = (iota((ny, nobs), 0) == (where & (ny - 1))).astype(BF16)
        coefficients()
        start_sides((ENS,))
    for p in range(parts):
        with mark(f"w_rs0_{p}"):
            gather_sum(0, p)
        if p == 0:
            with mark("w_obs"):
                recv_sides((OBS,))
                for side in (0, 1):
                    copy_seen(2 * side, obs_halo.at[side])
            with mark("w_edge"):
                wait_edges()
        with mark(f"obs0_{p}"):
            add_edges(p)
            observation_term(0, [p], [inc[0, p]])
    with mark("w_ens"):
        recv_sides((ENS,))
    for p in range(parts - 1):
        with mark(f"w_ag0_{p}"):
            adjoint_rows(0, p)
        with mark(f"mix1_{p}"):
            for k in range(0, members, 2):
                v = mixed(tables[p][...], pair_term(k, p), None)
                wide[k // 2] = v if p == 0 else wide[k // 2] + v
    with mark("w_ag0"):
        adjoint_rows(0, parts - 1)
        terms = edge_terms(0)
    with mark("mix1"):
        def blur(v):
            hi, low = split(v)
            return mm(jnp.concatenate([hi, low], axis=1), jnp.concatenate([blur2[...], blur2[...]], axis=0))

        for k in range(0, members, 2):
            v = mixed(tables[parts - 1][...], pair_term(k, parts - 1), side_by_side(terms, k, levels))
            wide[k // 2] = v if parts == 1 else wide[k // 2] + v
        for k in range(0, members, 2):
            done = blur(wide[k // 2])
            work[k * block:(k + 1) * block, :] = done[:, :ny]
            work[(k + 1) * block:(k + 2) * block, :] = done[:, ny:]
    with mark("part1"):
        for p in range(parts):
            members_sum(1, p)
            send_sum(1, p)
    for p in range(parts):
        with mark(f"w_rs1_{p}"):
            gather_sum(1, p)
        with mark(f"obs1_{p}"):
            observation_term(1, [p], [step_length * (inc[0, p] - inc[1, p])])
    for p in range(parts - 1):
        with mark(f"w_ag1_{p}"):
            adjoint_rows(1, p)
        with mark(f"mix2_{p}"):
            for k in range(0, members, 2):
                v = mixed(finals[p][...], pair_term(k, p), None)
                wide[k // 2] = v if p == 0 else wide[k // 2] + v
    with mark("term1"):
        adjoint_rows(1, parts - 1)
        terms = edge_terms(1)
        for side in (0, 1):
            edges_out[:, side * ny:(side + 1) * ny] = terms[side]
    with mark("drain"):
        size = lambda ref: math.prod(ref.shape) * ref.dtype.itemsize
        line = ny * 4
        total = size(rs_main) + size(edge_main) + (n_mem - 1) * (size(ag0) + size(ag1)) // n_mem
        wait_all(ensf.at[pl.ds(0, total // line)], sent.at[2])
        total = sum(size(ref) for ref in (rs_halo, edge_halo, ctl_halo, surf_halo, obs_halo, ens_halo)) // 2
        for side in (0, 1):
            @pl.when(has[1 - side])
            def _():
                wait_all(ensf.at[pl.ds(0, total // line)], sent.at[side])


def member_pair(ensf, adj, levels, width, share, k, p):
    block = levels * width
    _, sp = parts_of(share)

    def term(k):
        pieces = []
        for i in range(levels // share):
            at = (i * share + p * sp) * width
            low, high = pl.ds(at, sp * width), pl.ds(block + at, sp * width)
            base = 2 * k * block + at
            pieces.append(
                ensf[pl.ds(base, sp * width), :] * adj[low, :] + ensf[pl.ds(base + block, sp * width), :] * adj[high, :]
            )
        return jnp.concatenate(pieces, axis=0)

    return jnp.concatenate([term(k), term(k + 1)], axis=1)


def finish(members, levels, width, share, ny, ensf, adj, edges, wide, table, out, work, sem):
    block = levels * width
    parts, _ = parts_of(share)
    smooth_y = smoother(ny)
    terms = [edges[:, j * ny:(j + 1) * ny] for j in (0, 1)]
    for k in range(0, members, 2):
        done = mixed(
            table[...], member_pair(ensf, adj, levels, width, share, k, parts - 1), side_by_side(terms, k, levels)
        )
        if parts > 1:
            done = done + wide[k // 2]
        for i in (0, 1):
            at = pl.ds((k + i) * block, block)
            work[at, :] = smooth_y(done[:, i * ny:(i + 1) * ny])
            pltpu.make_async_copy(work.at[at], out.at[at], sem.at[0]).start()
    pltpu.make_async_copy(work, out, sem.at[0]).wait()


def body(n_mem, n_tile, ensemble, control, level_loc, wind_speed, cell_codes, obs_cell, innovation, obs_sigma):
    members, rows, width, ny = ensemble.shape
    levels = control.shape[1]
    assert width >= 2 * HALO and members % 2 == 0 and rows == 2 * levels
    nobs = obs_cell.shape[0]
    share = rows // n_mem
    kl = members * levels
    block = levels * width
    n = width + 2 * HALO
    vmem = pltpu.VMEM
    dma = pltpu.SemaphoreType.DMA
    parts, sp = parts_of(share)
    reach, data, hb, mb = blocks_of(sp, width)
    size = 2 * hb + mb
    tall = max(8, sp)
    margins = [margin_of(e, sp) for e in (0, 1)]
    surf = up(2 * HALO + nobs // ny, 8)
    scratch = [
        vmem((members, rows, width, ny), BF16),
        vmem((members * block, ny), F32),
        vmem((levels, levels), F32),
        vmem((width, ny), F32),
        vmem((width, ny), I32),
        vmem((1, nobs), I32),
        vmem((2, share, nobs), F32),
        dma((9,)),
        vmem((3, ny, nobs), BF16),
        vmem((members * block, ny), F32),
        vmem((1, 2, block, block), BF16),
        vmem((1, 2, kl, kl), BF16),
        vmem((block, up(3 * block // parts, 128)), BF16),
        vmem((block, up(3 * block // parts + 12 * levels, 128)), BF16),
        vmem((2 * ny, 2 * ny), BF16),
        vmem((10, (width + 2 * reach) * sp, ny), F32),
        vmem((10, n, ny), F32),
        vmem((2, kl + PACK, ny), I16),
        vmem((2, kl + PACK, ny), I16),
        vmem((2, surf, ny), F32),
        vmem((2, surf, ny), F32),
        vmem((2, 2, share, nobs), F32),
        vmem((3, parts, 2, tall, nobs), F32),
        vmem((2, 2, members * rows, ny), BF16),
        vmem((2, 2, members * rows, ny), BF16),
        vmem((parts, n_mem, sp * width, ny), F32),
        vmem((parts, n_mem, sp * width, ny), F32),
        vmem((2, parts, n_mem, size, ny), I16),
        vmem((2, parts, n_mem - 1, size, ny), I16),
        vmem((2, parts, 2, n_mem, hb, ny), I16),
        vmem((2, parts, (width + 2 * reach) * sp, ny), F32),
        vmem((parts, (width + 2 * reach) * sp, ny), F32),
        vmem((parts, margins[0], ny), F32),
        vmem((parts, n_mem, margins[0], ny), F32),
        vmem((4, rows, ny), F32),
        *(vmem((parts, n_mem, sp * width + margins[e], ny), I16) for e in (0, 1)),
        vmem((n_mem, 2, share, ny), F32),
        vmem((n_mem - 1, 2, share, ny), F32),
        vmem((2, n_mem, share, ny), F32),
        vmem((block, up(3 * block // parts, 128)), BF16),
        dma((3,)), dma((2, 4)), dma((2, parts, 3)), dma((2, parts)), dma((3,)),
    ]
    whole = pl.BlockSpec(memory_space=pltpu.VMEM)
    hbm = pl.BlockSpec(memory_space=pltpu.HBM)
    handed = pl.pallas_call(
        functools.partial(kernel, n_mem, n_tile, members, levels, width, ny, nobs),
        out_shape=(
            vmem((members * rows * width, ny), F32), vmem((rows * width, ny), F32), vmem((kl, 2 * ny), F32),
            vmem((members // 2, block, 2 * ny), F32), vmem((block, up(3 * block // parts + 6 * levels, 128)), BF16),
        ),
        in_specs=[hbm] * 8,
        out_specs=(whole,) * 5,
        scratch_shapes=scratch,
        compiler_params=pltpu.CompilerParams(
            collective_id=0, has_side_effects=True, vmem_limit_bytes=40 << 20
        ),
    )(*(pltpu.with_memory_space_constraint(x, pltpu.HBM) for x in (
        ensemble,
        control.reshape(members * block, ny),
        level_loc,
        wind_speed,
        cell_codes,
        obs_cell.reshape(1, nobs),
        innovation.reshape(n_mem, share, nobs),
        obs_sigma.reshape(n_mem, share, nobs),
    )))
    result = pl.pallas_call(
        functools.partial(finish, members, levels, width, share, ny),
        out_shape=jax.ShapeDtypeStruct((members * block, ny), F32),
        in_specs=[whole] * 5,
        out_specs=hbm,
        scratch_shapes=[vmem((members * block, ny), F32), dma((1,))],
        compiler_params=pltpu.CompilerParams(vmem_limit_bytes=40 << 20),
    )(*(pltpu.with_memory_space_constraint(x, pltpu.VMEM) for x in handed))
    return result.reshape(members, levels, width, ny)


def solution(mesh):
    placed = (
        P("mem", None, "tile", None),
        P("mem", None, "tile", None),
        P(),
        P("tile", None),
        P("tile", None),
        P("tile"),
        P(None, "tile"),
        P(None, "tile"),
    )
    return jax.shard_map(
        functools.partial(body, mesh.shape["mem"], mesh.shape["tile"]),
        mesh=mesh, in_specs=placed, out_specs=P("mem", None, "tile", None), check_vma=False,
    )
```
